32 devices in a mesh: grp: 4 (over x, core), dev: 8 (over z, y).
Axes of the slice: x: 2, y: 2, z: 4, core: 2. Of those that a mesh axis runs over, the one named last changes fastest.
Arguments:
- charges: bfloat16 [32, 131072], P(None, ('grp', 'dev')), may hold values from -6 to 6
- points: bfloat16 [3, 131072], P(None, ('grp', 'dev')), may hold values from -1.1953125 to 1.1953125
- basis: bfloat16 [64, 131072], P(None, ('grp', 'dev')), may hold values from -0.75 to 0.75
- up_leaf: bfloat16 [64, 64, 2048], P(None, None, ('grp', 'dev')), may hold values from -0.25 to 0.25
- up_branch: bfloat16 [64, 64, 256], P(None, None, ('grp', 'dev')), may hold values from -0.25 to 0.25
- up_device: bfloat16 [64, 64, 32], P(None, None, ('grp', 'dev')), may hold values from -0.25 to 0.25
- down_leaf: bfloat16 [64, 64, 2048], P(None, None, ('grp', 'dev')), may hold values from -0.75 to 0.75
- down_branch: bfloat16 [64, 64, 256], P(None, None, ('grp', 'dev')), may hold values from -0.75 to 0.75
- down_device: bfloat16 [64, 64, 32], P(None, None, ('grp', 'dev')), may hold values from -0.75 to 0.75
- proxy_leaf: bfloat16 [3, 64, 2048], P(None, None, ('grp', 'dev')), may hold values from -12 to 12
- proxy_branch: bfloat16 [3, 64, 256], P(None, None, ('grp', 'dev')), may hold values from -12 to 12
- proxy_device: bfloat16 [3, 64, 32], P(None, None, ('grp', 'dev')), may hold values from -12 to 12
- proxy_group: bfloat16 [3, 64, 4], P(None, None, 'grp'), may hold values from -12 to 12
- far_leaf: int32 [16, 2048], P(None, ('grp', 'dev')), may hold values from 0 to 191
- send_leaf: int32 [4, 1024], P(None, ('grp', 'dev')), may hold values from 0 to 63
- far_branch: int32 [16, 256], P(None, ('grp', 'dev')), may hold values from 0 to 63
- near_leaf: int32 [16, 2048], P(None, ('grp', 'dev')), may hold values from -4 to 4
Outputs:
- potential: float32 [32, 131072], P(None, ('grp', 'dev'))
The draws below stay inside these ranges and needn't reach their ends.
All inputs are finite; a program needn't handle non-finite values.
Results may differ from the reference program's by a relative error of at most 0.0034.
Values may be sent and summed in bfloat16 or wider, within the bound.
No kernel may reach another device: no remote copies, remote signals or barrier semaphores. Data moves between devices by JAX's collectives and lax.ppermute only.
A program may use at most 192 MiB of HBM per device.

```python
import math
import jax
import jax.numpy as jnp
from jax import lax

LEAF = 64
RANK = 64
RHS = 32
LEAF_DEV = 64
FAR_LEAF = 16
FAR_BRANCH = 16
NEAR = 16
REACH = 4
SLOTS = 4
BRANCH_DEV = 8
LEAVES = 2048
BRANCHES = 256
POINTS = 131072
N_GRP = 4
N_DEV = 8
DEVICES = 32


def with_ends(entries, rng, low, top_value):
    place = [jax.random.randint(jax.random.fold_in(rng, axis), (), 0, length) for axis, length in enumerate(entries.shape)]
    longest = entries.shape.index(max(entries.shape))
    beside = place[:longest] + [(place[longest] + 1) % entries.shape[longest]] + place[longest + 1:]
    return entries.at[tuple(place)].set(low).at[tuple(beside)].set(top_value)


def shard_levels(key, dims, pieces, least, high):
    def one(dim, parts):
        steps = jax.random.uniform(jax.random.fold_in(jax.random.fold_in(key, 6), dim), (parts,), jnp.float32, least / len(pieces), high / len(pieces))
        return jnp.repeat(jnp.exp(steps), dims[dim] // parts).reshape((-1,) + (1,) * (len(dims) - dim - 1))

    factor_of = one(*pieces[0])
    for cut in pieces[1:]:
        factor_of = factor_of * one(*cut)
    return factor_of


def bell_draw(rng, shape, spread, limit, cuts=(), kind=jnp.bfloat16):
    entries = jax.random.normal(rng, shape, jnp.float32) * spread
    if len(cuts) > 0:
        entries = shard_levels(rng, shape, cuts, -0.22, 0.18) * entries
    return jnp.clip(entries, min=-limit, max=limit).astype(kind)


def setup_inputs(seed: int = 0) -> dict:
    arg_keys = jax.random.split(jax.random.key(seed), 18)
    return {
        "charges": bell_draw(arg_keys[0], (RHS, POINTS), 1.0, 6.0, ((1, 32),)),
        "points": bell_draw(arg_keys[1], (3, POINTS), 0.2, 1.1953125, ((1, 32),)),
        "basis": bell_draw(arg_keys[2], (RANK, POINTS), LEAF ** -0.5, 0.75, ((1, 32),)),
        "up_leaf": bell_draw(arg_keys[3], (RANK, RANK, LEAVES), (8 * RANK) ** -0.5, 0.25, ((2, 32),)),
        "up_branch": bell_draw(arg_keys[4], (RANK, RANK, BRANCHES), (BRANCH_DEV * RANK) ** -0.5, 0.25, ((2, 32),)),
        "up_device": bell_draw(arg_keys[5], (RANK, RANK, DEVICES), (N_DEV * RANK) ** -0.5, 0.25, ((2, 32),)),
        "down_leaf": bell_draw(arg_keys[6], (RANK, RANK, LEAVES), RANK ** -0.5, 0.75, ((2, 32),)),
        "down_branch": bell_draw(arg_keys[7], (RANK, RANK, BRANCHES), RANK ** -0.5, 0.75, ((2, 32),)),
        "down_device": bell_draw(arg_keys[8], (RANK, RANK, DEVICES), RANK ** -0.5, 0.75, ((2, 32),)),
        "proxy_leaf": bell_draw(arg_keys[9], (3, RANK, LEAVES), 2.0, 12.0, ((2, 32),)),
        "proxy_branch": bell_draw(arg_keys[10], (3, RANK, BRANCHES), 2.0, 12.0, ((2, 32),)),
        "proxy_device": bell_draw(arg_keys[11], (3, RANK, DEVICES), 2.0, 12.0, ((2, 32),)),
        "proxy_group": bell_draw(arg_keys[12], (3, RANK, N_GRP), 2.0, 12.0, ((2, 4),)),
        "far_leaf": with_ends(jax.random.randint(arg_keys[13], (FAR_LEAF, LEAVES), 0, LEAF_DEV + DEVICES * SLOTS), jax.random.fold_in(arg_keys[13], 1), 0, (LEAF_DEV + DEVICES * SLOTS) - 1).astype(jnp.int32),
        "send_leaf": with_ends(jax.random.randint(arg_keys[14], (SLOTS, DEVICES * DEVICES), 0, LEAF_DEV), jax.random.fold_in(arg_keys[14], 1), 0, LEAF_DEV - 1).astype(jnp.int32),
        "far_branch": with_ends(jax.random.randint(arg_keys[15], (FAR_BRANCH, BRANCHES), 0, N_DEV * BRANCH_DEV), jax.random.fold_in(arg_keys[15], 1), 0, (N_DEV * BRANCH_DEV) - 1).astype(jnp.int32),
        "near_leaf": with_ends(jax.random.randint(arg_keys[16], (NEAR, LEAVES), 0 - REACH, REACH + 1), jax.random.fold_in(arg_keys[16], 1), 0 - REACH, REACH).astype(jnp.int32),
    }


INV_FOUR_PI = 1.0 / (4.0 * math.pi)
SOFTEN = 0.25

def kernel_block(target, source):
    delta = target.astype(jnp.float32)[:, :, None] - source.astype(jnp.float32)[:, None, :]
    square = lax.optimization_barrier(jnp.sum(delta * delta, axis=0))
    return (INV_FOUR_PI * lax.rsqrt(square + SOFTEN)).astype(jnp.bfloat16)

def widen(array):
    return array.astype(jnp.float32)

def split_last(array, count_blocks, width):
    shaped = array.reshape(array.shape[:-1] + (count_blocks, width))
    return jnp.moveaxis(shaped, -2, 0)

def reference(charges, points, basis, up_leaf, up_branch, up_device, down_leaf, down_branch, down_device, proxy_leaf, proxy_branch, proxy_device, proxy_group, far_leaf, send_leaf, far_branch, near_leaf):
    m_leaf = jnp.einsum('kbp,rbp->rkb', widen(basis.reshape(RANK, LEAVES, LEAF)), widen(charges.reshape(RHS, LEAVES, LEAF))).astype(jnp.bfloat16)
    m_branch = jnp.einsum('kjci,rjci->rkc', widen(up_leaf.reshape(RANK, RANK, BRANCHES, 8)), widen(m_leaf.reshape(RHS, RANK, BRANCHES, 8))).astype(jnp.bfloat16)
    m_device = jnp.einsum('kjdc,rjdc->rkd', widen(up_branch.reshape(RANK, RANK, DEVICES, BRANCH_DEV)), widen(m_branch.reshape(RHS, RANK, DEVICES, BRANCH_DEV))).astype(jnp.bfloat16)
    m_group = jnp.einsum('kjgv,rjgv->rkg', widen(up_device.reshape(RANK, RANK, N_GRP, N_DEV)), widen(m_device.reshape(RHS, RANK, N_GRP, N_DEV))).astype(jnp.bfloat16)
    group_ids = jnp.arange(N_GRP, dtype=jnp.int32)
    mask_top = (jnp.abs(group_ids[:, None] - group_ids[None, :]) >= 2).astype(jnp.float32)
    kern_top = widen(kernel_block(proxy_group[:, :, :, None], proxy_group[:, :, None, :])) * mask_top
    l_group = jnp.einsum('kjgh,rjh->rkg', kern_top, widen(m_group)).astype(jnp.bfloat16)
    member_ids = jnp.arange(N_DEV, dtype=jnp.int32)
    mask_dev = (jnp.abs(member_ids[:, None] - member_ids[None, :]) >= 2).astype(jnp.float32)
    proxy_dev4 = proxy_device.reshape(3, RANK, N_GRP, N_DEV)
    kern_dev = widen(kernel_block(proxy_dev4[:, :, :, :, None], proxy_dev4[:, :, :, None, :])) * mask_dev
    l_device = jnp.einsum('kjgvw,rjgw->rkgv', kern_dev, widen(m_device.reshape(RHS, RANK, N_GRP, N_DEV)))
    l_device = l_device + jnp.einsum('kjgv,rjg->rkgv', widen(down_device.reshape(RANK, RANK, N_GRP, N_DEV)), widen(l_group))
    l_device = l_device.astype(jnp.bfloat16).reshape(RHS, RANK, DEVICES)
    group_span = N_DEV * BRANCH_DEV
    branch_ids = jnp.arange(BRANCHES, dtype=jnp.int32)
    branch_global = far_branch + (branch_ids // group_span * group_span)[None, :]

    def branch_step(inputs):
        ids, target_p, down_blk, parent_blk = inputs
        src_m = jnp.take(m_branch, ids, axis=2)
        src_p = jnp.take(proxy_branch, ids, axis=2)
        kern = widen(kernel_block(target_p[:, :, None, :], src_p))
        total = jnp.einsum('kjeb,rjeb->rkb', kern, widen(src_m))
        total = total + jnp.einsum('kjb,rj->rkb', widen(down_blk), widen(parent_blk))
        return total.astype(jnp.bfloat16)
    branch_blocks = lax.map(branch_step, (split_last(branch_global, DEVICES, BRANCH_DEV), split_last(proxy_branch, DEVICES, BRANCH_DEV), split_last(down_branch, DEVICES, BRANCH_DEV), jnp.moveaxis(l_device, 2, 0)))
    l_branch = jnp.moveaxis(branch_blocks, 0, 2).reshape(RHS, RANK, BRANCHES)
    leaf_ids = jnp.arange(LEAVES, dtype=jnp.int32)
    owner = (leaf_ids // LEAF_DEV)[None, :]
    beyond = jnp.maximum(far_leaf - LEAF_DEV, 0)
    peer = beyond // SLOTS
    slot = beyond % SLOTS
    remote = peer * LEAF_DEV + send_leaf[slot, peer * DEVICES + owner]
    far_global = jnp.where(far_leaf < LEAF_DEV, owner * LEAF_DEV + far_leaf, remote).astype(jnp.int32)
    near_rows = (near_leaf + leaf_ids[None, :] + REACH).astype(jnp.int32)
    stacked = jnp.concatenate([charges, points], axis=0)
    wide = jnp.pad(stacked, ((0, 0), (REACH * LEAF, REACH * LEAF))).reshape(RHS + 3, LEAVES + 2 * REACH, LEAF)
    parents = jnp.repeat(l_branch, 8, axis=2)
    width = math.gcd(LEAVES, 64)
    count_blocks = LEAVES // width

    def leaf_step(inputs):
        far_ids, rows, target_p, down_blk, parent_blk, basis_blk, point_blk = inputs
        src_m = jnp.take(m_leaf, far_ids, axis=2)
        src_p = jnp.take(proxy_leaf, far_ids, axis=2)
        kern = widen(kernel_block(target_p[:, :, None, :], src_p))
        local = jnp.einsum('kjeb,rjeb->rkb', kern, widen(src_m))
        local = local + jnp.einsum('kjb,rjb->rkb', widen(down_blk), widen(parent_blk))
        l_leaf = local.astype(jnp.bfloat16)
        result = jnp.einsum('kbp,rkb->rbp', widen(basis_blk), widen(l_leaf))
        source = jnp.take(wide, rows, axis=1)
        src_x = source[:RHS]
        src_pt = jnp.moveaxis(source[RHS:], 3, 1)
        target_pt = jnp.moveaxis(point_blk, 2, 1)[:, :, None, :]
        kern_near = widen(kernel_block(target_pt, src_pt))
        return result + jnp.einsum('ijeb,rebj->rbi', kern_near, widen(src_x))
    basis_blocks = jnp.moveaxis(basis.reshape(RANK, count_blocks, width, LEAF), 1, 0)
    point_blocks = jnp.moveaxis(points.reshape(3, count_blocks, width, LEAF), 1, 0)
    blocks = lax.map(leaf_step, (split_last(far_global, count_blocks, width), split_last(near_rows, count_blocks, width), split_last(proxy_leaf, count_blocks, width), split_last(down_leaf, count_blocks, width), split_last(parents, count_blocks, width), basis_blocks, point_blocks))
    return jnp.moveaxis(blocks, 0, 1).reshape(RHS, POINTS)
```

```python
import functools
import math

import jax
import jax.numpy as jnp
from jax import lax
from jax.experimental import pallas as pl
from jax.experimental.pallas import tpu as pltpu
from jax.sharding import PartitionSpec as P

REACH = 4
FAN = 8

INV_FOUR_PI = 1.0 / (4.0 * math.pi)
SOFTEN = 0.25
FEATURES = 16

BF16 = jnp.bfloat16
F32 = jnp.float32


def dot(a, b):
    return jnp.dot(a, b, preferred_element_type=F32)


def dot_t(a, b):
    return lax.dot_general(a, b, (((1,), (1,)), ((), ())), preferred_element_type=F32)


def dot_0(a, b):
    return lax.dot_general(a, b, (((0,), (0,)), ((), ())), preferred_element_type=F32)


def low_half(shape):
    width = shape[-1]
    return lax.broadcasted_iota(jnp.int32, shape, len(shape) - 1) < width // 2


def pair(low, first, second):
    return jnp.where(low, first, second)


def swap(tile):
    half = tile.shape[-1] // 2
    return jnp.concatenate([tile[..., half:], tile[..., :half]], axis=-1)


def twice(tile):
    return jnp.concatenate([tile, tile], axis=-1)


def three(value):
    first = value.astype(BF16).astype(F32)
    rest = value - first
    second = rest.astype(BF16).astype(F32)
    return first, second, rest - second


def source_rows(x, y, z):
    one = jnp.ones_like(x)
    return (-2.0 * x, -2.0 * y, -2.0 * z, one, one, one) + three(x * x + y * y + z * z)


def target_rows(x, y, z):
    one = jnp.ones_like(x)
    return (x, y, z) + three(x * x + y * y + z * z + SOFTEN) + (one, one, one)


def put_rows(ref, rows, start, count, step):
    for f in range(FEATURES):
        value = rows[f] if f < len(rows) else jnp.zeros_like(rows[0])
        ref[pl.ds(start * FEATURES + f, count, stride=step * FEATURES), :] = value


def kern_of(square):
    return (INV_FOUR_PI * lax.rsqrt(square)).astype(BF16)


def interact(target, slots, source_ref, moment_ref):
    rank2 = source_ref.shape[-1]
    low_s = low_half((FEATURES, rank2))
    low_m = low_half(moment_ref.shape[1:])
    sources, moments = [], []
    for first, second in zip(slots[0::2], slots[1::2]):
        sources.append(pair(low_s, source_ref[first], source_ref[second]))
        moments.append(pair(low_m, moment_ref[first], moment_ref[second]))
    square = dot_0(target, jnp.concatenate(sources, axis=1))
    return dot_t(jnp.concatenate(moments, axis=1), kern_of(square))


def listed_kernel(send_ref, charges_ref, basis_ref, proxy_ref, moment_ref, own_ref, out_ref, tile_ref):
    slots, devices = send_ref.shape
    leaves, rhs, rank2 = moment_ref.shape
    rank = rank2 // 2
    low = low_half((rhs, rank2))
    tile_ref[...] = jnp.zeros_like(tile_ref)
    for c in range(3):
        spread = twice(jnp.transpose(proxy_ref[c].astype(F32)))
        own_ref[c] = spread
        tile_ref[pl.ds(c, leaves, stride=8), :] = spread
        tile_ref[pl.ds(c + 4, leaves, stride=8), :] = spread

    def leaf_pair(i, carry):
        columns = pl.ds(pl.multiple_of(i * rank2, rank2), rank2)
        q = charges_ref[:, columns]
        u = basis_ref[:, columns]
        zero = jnp.zeros_like(q)
        stacked = jnp.concatenate([jnp.where(low, q, zero), jnp.where(low, zero, q)], axis=0)
        product = dot_t(stacked, jnp.concatenate([u, u], axis=0)).astype(BF16)
        moment_ref[2 * i] = product[:rhs]
        moment_ref[2 * i + 1] = product[rhs:]
        return carry

    lax.fori_loop(0, leaves // 2, leaf_pair, 0, unroll=8)

    low8 = low_half((8, rank2))
    top8 = lax.broadcasted_iota(jnp.int32, (8, rank2), 0) < 4

    def pack(p, carry):
        s = [send_ref[t, p] for t in range(slots)]
        tiles = []
        for q in range(slots // 2):
            out_ref[p, q * rhs : (q + 1) * rhs, :] = pair(low, moment_ref[s[2 * q]], moment_ref[s[2 * q + 1]])
            a = tile_ref[pl.ds(pl.multiple_of(s[2 * q] * 8, 8), 8), :]
            b = tile_ref[pl.ds(pl.multiple_of(s[2 * q + 1] * 8, 8), 8), :]
            tiles.append(pair(low8, a, b))
        out_ref[p, slots // 2 * rhs :, :] = jnp.where(top8, tiles[0], tiles[1]).astype(BF16)
        return carry

    lax.fori_loop(0, devices, pack, 0, unroll=4)


def relayout(x_ref, scratch_ref):
    rank, _, leaves = x_ref.shape
    half = rank // 2
    eye = (
        lax.broadcasted_iota(jnp.int32, (leaves, leaves), 0)
        == lax.broadcasted_iota(jnp.int32, (leaves, leaves), 1)
    ).astype(BF16)
    for k in range(0, half, 2):
        block = jnp.concatenate(
            [x_ref[k], x_ref[k + half], x_ref[k + 1], x_ref[k + 1 + half]], axis=0
        )
        turned = dot_t(eye, block)
        for n in range(2):
            scratch_ref[pl.ds(k + n, leaves, stride=half), :] = turned[:, n * 2 * rank : (n + 1) * 2 * rank]


def spread_rows(block, low):
    zero = jnp.zeros_like(block)
    return jnp.concatenate([jnp.where(low, block, zero), jnp.where(low, zero, block)], axis=0)


def upward_kernel(
    moment_ref, up_leaf_ref, up_branch_ref, up_device_ref, pbranch_ref, pdevice_ref, out_ref, scratch_ref, branch_ref
):
    leaves, rhs, rank2 = moment_ref.shape
    rank = rank2 // 2
    half = rank // 2
    branches = leaves // FAN
    relayout(up_leaf_ref, scratch_ref)
    low = low_half((half, rank2))
    low_m = low_half((rhs, rank2))
    wide = up_branch_ref[...].astype(F32).reshape(rank * branches, rank)
    branch_ref[...] = twice(wide)
    m_device = jnp.zeros((rhs, rank), F32)
    previous = None
    for c in range(branches):
        blocks, moments = [], []
        for b in range(c * FAN, (c + 1) * FAN):
            block = scratch_ref[b * half : (b + 1) * half, :].astype(BF16)
            blocks.append(spread_rows(block, low))
            moments.append(moment_ref[b])
        m_branch = dot_t(jnp.concatenate(moments, axis=1), jnp.concatenate(blocks, axis=1)).astype(BF16)
        matrix = branch_ref[pl.ds(c, rank, stride=branches), :][:, :rank].astype(BF16)
        m_device = m_device + dot_t(m_branch, matrix)
        spread = twice(m_branch)
        if c % 2 == 1:
            out_ref[(c // 2) * rhs : (c // 2 + 1) * rhs, :] = pair(low_m, previous, spread)
        previous = spread
    m_device = m_device.astype(BF16)
    base = branches // 2 * rhs
    proxies = jnp.concatenate(
        [
            pdevice_ref[...].astype(F32),
            jnp.zeros((5, rank), F32),
            pbranch_ref[...].astype(F32).reshape(3 * branches, rank),
        ],
        axis=0,
    )
    out_ref[base : base + rhs, :] = jnp.concatenate([m_device.astype(F32), proxies], axis=1).astype(BF16)
    share = dot_t(m_device, up_device_ref[...])
    high = share.astype(BF16).astype(F32)
    out_ref[base + rhs : base + 2 * rhs, :] = jnp.concatenate([high, share - high], axis=1).astype(BF16)


def near_kernel(
    near_ref, charges_ref, points_ref, left_ref, right_ref, down_leaf_ref, out_ref, down_ref,
    wide_ref, source_ref, target_ref, scratch_ref, count_ref, weight_ref,
):
    rhs, total = charges_ref.shape
    entries, leaves = near_ref.shape
    size = total // leaves
    halo = REACH * size
    span = 2 * REACH + 1
    reach = (span + 1) * size
    relayout(down_leaf_ref, scratch_ref)
    down_ref[...] = scratch_ref[...].astype(BF16)

    wide_ref[:, :halo] = left_ref[:rhs, :]
    wide_ref[:, halo : halo + total] = charges_ref[...]
    wide_ref[:, halo + total :] = right_ref[:rhs, :]
    coords = [
        jnp.concatenate(
            [left_ref[rhs + c : rhs + c + 1, :], points_ref[c : c + 1, :], right_ref[rhs + c : rhs + c + 1, :]], axis=1
        ).astype(F32)
        for c in range(3)
    ]
    rows = source_rows(*coords)
    rows = rows + (jnp.zeros((FEATURES - len(rows), coords[0].shape[1]), F32),)
    source_ref[...] = jnp.concatenate(rows, axis=0).astype(BF16)
    rows = target_rows(*[c[:, halo : halo + total] for c in coords])
    rows = rows + (jnp.zeros((FEATURES - len(rows), total), F32),)
    target_ref[...] = jnp.concatenate(rows, axis=0).astype(BF16)

    near = near_ref[...]
    counts = [jnp.sum((near == o - REACH).astype(F32), axis=0, keepdims=True) for o in range(span)]
    counts = jnp.concatenate(counts + [jnp.zeros((FEATURES - span, leaves), F32)], axis=0).astype(BF16)
    offset = lax.broadcasted_iota(jnp.int32, (FEATURES, reach), 0)
    block = lax.broadcasted_iota(jnp.int32, (FEATURES, reach), 1) // size
    for h in range(2):
        weight_ref[h] = dot_0(counts, (block == offset + h).astype(BF16))

    low = low_half((rhs, 2 * size))

    def leaf_pair(i, carry):
        start = pl.multiple_of(i * 2 * size, 2 * size)
        square = dot_0(target_ref[:, pl.ds(start, 2 * size)], source_ref[:, pl.ds(start, reach)])
        kern = kern_of(square)
        x = wide_ref[:, pl.ds(start, reach)].astype(F32)
        parts = []
        for h in range(2):
            scaled = x * weight_ref[h, pl.ds(2 * i + h, 1), :]
            high = scaled.astype(BF16)
            parts += [high, (scaled - high.astype(F32)).astype(BF16)]
        product = dot_t(jnp.concatenate(parts, axis=0), kern)
        first = product[:rhs] + product[rhs : 2 * rhs]
        second = product[2 * rhs : 3 * rhs] + product[3 * rhs :]
        out_ref[:, pl.ds(start, 2 * size)] = pair(low, first, second)
        return carry

    lax.fori_loop(0, leaves // 2, leaf_pair, 0, unroll=2)


def group_kernel(*refs, members):
    far_ref, pgroup_ref = refs[:2]
    parts = refs[2 : 2 + members]
    fb_ref, ld_ref, out_ref = refs[2 + members : 5 + members]
    moment_ref, coord_ref, rows_ref, source_ref, dev_m_ref, dev_coord_ref, dev_rows_ref, dev_source_ref = refs[5 + members :]
    entries, branches = far_ref.shape
    rhs, rank2 = moment_ref.shape[1:]
    rank = rank2 // 2
    base = branches // 2 * rhs
    me = lax.axis_index("dev")
    low = low_half((rhs, rank2))
    m_group = jnp.zeros((rhs, rank), F32)
    for s, part in enumerate(parts):
        owner = lax.rem(me - s + members, members)
        for q in range(branches // 2):
            tile = part[q * rhs : (q + 1) * rhs, :]
            other = swap(tile)
            moment_ref[owner * branches + 2 * q] = pair(low, tile, other)
            moment_ref[owner * branches + 2 * q + 1] = pair(low, other, tile)
        mixed = part[base : base + rhs, :].astype(F32)
        turned = pltpu.roll(mixed, rank, 1)
        keep = (jnp.abs(owner - me) >= 2).astype(F32)
        dev_m_ref[owner] = (pair(low, mixed, turned) * keep).astype(BF16)
        spread = pair(low, turned, mixed)
        for c in range(3):
            rows = pl.ds(pl.multiple_of(owner * branches, branches), branches)
            coord_ref[c, rows, :] = spread[8 + c * branches : 8 + (c + 1) * branches, :]
            dev_coord_ref[c, pl.ds(owner, 1), :] = spread[c : c + 1, :]
        share = part[base + rhs : base + 2 * rhs, :].astype(F32)
        m_group = m_group + (share + pltpu.roll(share, rank, 1))[:, :rank]
    group_proxies = jnp.concatenate([pgroup_ref[...].astype(F32), jnp.zeros((rhs - 3, rank), F32)], axis=0)
    out_ref[...] = jnp.concatenate([m_group.astype(BF16).astype(F32), group_proxies], axis=1).astype(BF16)

    count = members * branches
    put_rows(rows_ref, source_rows(*[coord_ref[c] for c in range(3)]), 0, count, 1)
    source_ref[...] = rows_ref[...].astype(BF16).reshape(source_ref.shape)
    put_rows(dev_rows_ref, source_rows(*[dev_coord_ref[c] for c in range(3)]), 0, members, 1)
    dev_source_ref[...] = dev_rows_ref[...].astype(BF16).reshape(dev_source_ref.shape)

    def targets(x, y, z):
        rows = target_rows(x, y, z)
        rows = rows + (jnp.zeros((FEATURES - len(rows), rank), F32),)
        return jnp.concatenate(rows, axis=0).astype(BF16)

    mixed = parts[0][base : base + rhs, :].astype(F32)[:, rank:]
    for c in range(branches):
        target = targets(*[mixed[8 + a * branches + c : 9 + a * branches + c, :] for a in range(3)])
        fb_ref[c] = interact(target, [far_ref[e, c] for e in range(entries)], source_ref, moment_ref)
    target = targets(*[mixed[a : a + 1, :] for a in range(3)])
    ld_ref[...] = interact(target, list(range(members)), dev_source_ref, dev_m_ref)


def downward_kernel(*refs, groups):
    far_ref = refs[0]
    tiles = refs[1 : 1 + groups]
    (
        fb_ref, ld_ref, down_device_ref, down_branch_ref, down_ref, own_ref, own_m_ref, recv_ref, basis_ref, near_ref,
        out_ref, moment_ref, rows_ref, source_ref, trows_ref, target_ref, coord_ref, grp_m_ref, grp_coord_ref,
        grp_rows_ref, grp_source_ref, branch_ref, parent_ref,
    ) = refs[1 + groups :]
    entries, leaves = far_ref.shape
    rhs, rank2 = moment_ref.shape[1:]
    rank = rank2 // 2
    half = rank // 2
    branches = leaves // FAN
    devices = recv_ref.shape[0]
    slots = (moment_ref.shape[0] - leaves) // devices
    me = lax.axis_index("grp")
    low = low_half((rhs, rank2))

    for s, tile_ref in enumerate(tiles):
        owner = lax.rem(me - s + groups, groups)
        mixed = tile_ref[...].astype(F32)
        turned = pltpu.roll(mixed, rank, 1)
        keep = (jnp.abs(owner - me) >= 2).astype(F32)
        grp_m_ref[owner] = (pair(low, mixed, turned) * keep).astype(BF16)
        spread = pair(low, turned, mixed)
        for c in range(3):
            grp_coord_ref[c, pl.ds(owner, 1), :] = spread[c : c + 1, :]
    put_rows(grp_rows_ref, source_rows(*[grp_coord_ref[c] for c in range(3)]), 0, groups, 1)
    grp_source_ref[...] = grp_rows_ref[...].astype(BF16).reshape(grp_source_ref.shape)
    mixed = tiles[0][...].astype(F32)[:, rank:]
    rows = target_rows(*[mixed[a : a + 1, :] for a in range(3)])
    rows = rows + (jnp.zeros((FEATURES - len(rows), rank), F32),)
    target = jnp.concatenate(rows, axis=0).astype(BF16)
    l_group = interact(target, list(range(groups)), grp_source_ref, grp_m_ref).astype(BF16)
    l_device = (ld_ref[...] + dot_t(l_group, down_device_ref[...])).astype(BF16)
    branch_ref[...] = twice(down_branch_ref[...].astype(F32).reshape(rank * branches, rank))
    for c in range(branches):
        matrix = branch_ref[pl.ds(c, rank, stride=branches), :][:, :rank].astype(BF16)
        parent_ref[c] = twice((fb_ref[c] + dot_t(l_device, matrix)).astype(BF16))

    moment_ref[:leaves] = own_m_ref[...]

    def unpack(p, carry):
        for q in range(slots // 2):
            tile = recv_ref[p, q * rhs : (q + 1) * rhs, :]
            other = swap(tile)
            moment_ref[leaves + p * slots + 2 * q] = pair(low, tile, other)
            moment_ref[leaves + p * slots + 2 * q + 1] = pair(low, other, tile)
        coord_ref[pl.ds(pl.multiple_of(p * 8, 8), 8), :] = recv_ref[p, slots // 2 * rhs :, :].astype(F32)
        return carry

    lax.fori_loop(0, devices, unpack, 0, unroll=4)
    own = [own_ref[c] for c in range(3)]
    put_rows(rows_ref, source_rows(*own), 0, leaves, 1)
    put_rows(trows_ref, target_rows(*own), 0, leaves, 1)
    target_ref[...] = trows_ref[...].astype(BF16).reshape(target_ref.shape)
    low_p = low_half((devices, rank2))
    for q in range(slots // 2):
        found = [coord_ref[pl.ds(q * 4 + c, devices, stride=8), :] for c in range(3)]
        other = [pltpu.roll(v, rank, 1) for v in found]
        put_rows(rows_ref, source_rows(*[pair(low_p, v, o) for v, o in zip(found, other)]), leaves + 2 * q, devices, slots)
        put_rows(rows_ref, source_rows(*[pair(low_p, o, v) for v, o in zip(found, other)]), leaves + 2 * q + 1, devices, slots)
    source_ref[...] = rows_ref[...].astype(BF16).reshape(source_ref.shape)

    low_d = low_half((half, rank2))

    def leaf_pair(i, carry):
        sums = []
        for h in range(2):
            b = 2 * i + h
            far = interact(target_ref[b][:, :rank], [far_ref[e, b] for e in range(entries)], source_ref, moment_ref)
            rows = down_ref[pl.ds(pl.multiple_of(b * half, half), half), :]
            parent = parent_ref[b // FAN]
            sums.append((far + dot_t(parent, spread_rows(rows, low_d))).astype(BF16))
        columns = pl.ds(pl.multiple_of(i * rank2, rank2), rank2)
        product = dot(jnp.concatenate(sums, axis=0), basis_ref[:, columns])
        out_ref[:, columns] = near_ref[:, columns] + pair(low, product[:rhs], product[rhs:])
        return carry

    lax.fori_loop(0, leaves // 2, leaf_pair, 0)


VMEM = functools.partial(pl.BlockSpec, memory_space=pltpu.VMEM)
SMEM = functools.partial(pl.BlockSpec, memory_space=pltpu.SMEM)


def struct(shape, dtype):
    return jax.ShapeDtypeStruct(shape, dtype)


def on_device(
    charges, points, basis, up_leaf, up_branch, up_device, down_leaf, down_branch, down_device,
    proxy_leaf, proxy_branch, proxy_device, proxy_group, far_leaf, send_leaf, far_branch, near_leaf,
):
    rhs, total = charges.shape
    rank = basis.shape[0]
    leaves = up_leaf.shape[2]
    size = total // leaves
    branches = leaves // FAN
    slots = send_leaf.shape[0]
    groups = lax.axis_size("grp")
    members = lax.axis_size("dev")
    devices = groups * members
    rank2 = 2 * rank
    half = rank // 2
    halo = REACH * size
    assert rank == size and slots == 4 and rhs == 3 * branches + 8

    moments, own, listed = pl.pallas_call(
        listed_kernel,
        out_shape=(
            struct((leaves, rhs, rank2), BF16),
            struct((3, leaves, rank2), F32),
            struct((devices, slots // 2 * rhs + 8, rank2), BF16),
        ),
        in_specs=[SMEM(), VMEM(), VMEM(), VMEM()],
        out_specs=(VMEM(), VMEM(), VMEM()),
        scratch_shapes=[pltpu.VMEM((leaves * 8, rank2), F32)],
        name="listed",
    )(send_leaf, charges, basis, proxy_leaf)
    received = lax.all_to_all(listed, ("grp", "dev"), split_axis=0, concat_axis=0, tiled=True)

    stacked = jnp.concatenate([charges, points], axis=0)
    last = devices - 1
    left = lax.ppermute(stacked[:, total - halo :], ("grp", "dev"), [(i, i + 1) for i in range(last)])
    right = lax.ppermute(stacked[:, :halo], ("grp", "dev"), [(i + 1, i) for i in range(last)])

    shared = pl.pallas_call(
        upward_kernel,
        out_shape=struct((branches // 2 * rhs + 2 * rhs, rank2), BF16),
        in_specs=[VMEM()] * 6,
        out_specs=VMEM(),
        scratch_shapes=[pltpu.VMEM((leaves * half, rank2), F32), pltpu.VMEM((rank * branches, rank2), F32)],
        name="upward",
    )(
        moments,
        up_leaf,
        jnp.transpose(up_branch, (0, 2, 1)),
        up_device[:, :, 0],
        jnp.transpose(proxy_branch, (0, 2, 1)),
        proxy_device[:, :, 0],
    )
    parts = [shared] + [
        lax.ppermute(shared, "dev", [(i, (i + s) % members) for i in range(members)]) for s in range(1, members)
    ]

    reach = (2 * REACH + 2) * size
    near, down = pl.pallas_call(
        near_kernel,
        out_shape=(struct((rhs, total), F32), struct((leaves * half, rank2), BF16)),
        in_specs=[VMEM()] * 6,
        out_specs=(VMEM(), VMEM()),
        scratch_shapes=[
            pltpu.VMEM((rhs, total + 2 * halo), BF16),
            pltpu.VMEM((FEATURES, total + 2 * halo), BF16),
            pltpu.VMEM((FEATURES, total), BF16),
            pltpu.VMEM((leaves * half, rank2), F32),
            pltpu.VMEM((8, 128), F32),
            pltpu.VMEM((2, leaves, reach), F32),
        ],
        name="near",
    )(near_leaf, charges, points, left, right, down_leaf)

    far_b, part_d, tile = pl.pallas_call(
        functools.partial(group_kernel, members=members),
        out_shape=(struct((branches, rhs, rank), F32), struct((rhs, rank), F32), struct((rhs, rank2), BF16)),
        in_specs=[SMEM(), VMEM()] + [VMEM()] * members,
        out_specs=(VMEM(), VMEM(), VMEM()),
        scratch_shapes=[
            pltpu.VMEM((members * branches, rhs, rank2), BF16),
            pltpu.VMEM((3, members * branches, rank2), F32),
            pltpu.VMEM((members * branches * FEATURES, rank2), F32),
            pltpu.VMEM((members * branches, FEATURES, rank2), BF16),
            pltpu.VMEM((members, rhs, rank2), BF16),
            pltpu.VMEM((3, members, rank2), F32),
            pltpu.VMEM((members * FEATURES, rank2), F32),
            pltpu.VMEM((members, FEATURES, rank2), BF16),
        ],
        name="group",
    )(far_branch, proxy_group[:, :, 0], *parts)
    tiles = [tile] + [
        lax.ppermute(tile, "grp", [(i, (i + s) % groups) for i in range(groups)]) for s in range(1, groups)
    ]

    table = leaves + devices * slots
    return pl.pallas_call(
        functools.partial(downward_kernel, groups=groups),
        out_shape=struct((rhs, total), F32),
        in_specs=[SMEM()] + [VMEM()] * (groups + 10),
        out_specs=VMEM(),
        scratch_shapes=[
            pltpu.VMEM((table, rhs, rank2), BF16),
            pltpu.VMEM((table * FEATURES, rank2), F32),
            pltpu.VMEM((table, FEATURES, rank2), BF16),
            pltpu.VMEM((leaves * FEATURES, rank2), F32),
            pltpu.VMEM((leaves, FEATURES, rank2), BF16),
            pltpu.VMEM((devices * 8, rank2), F32),
            pltpu.VMEM((groups, rhs, rank2), BF16),
            pltpu.VMEM((3, groups, rank2), F32),
            pltpu.VMEM((groups * FEATURES, rank2), F32),
            pltpu.VMEM((groups, FEATURES, rank2), BF16),
            pltpu.VMEM((rank * branches, rank2), F32),
            pltpu.VMEM((branches, rhs, rank2), BF16),
        ],
        name="downward",
    )(
        far_leaf, *tiles, far_b, part_d, down_device[:, :, 0], jnp.transpose(down_branch, (0, 2, 1)), down, own,
        moments, received, basis, near,
    )


def solution(mesh):
    points = P(None, ("grp", "dev"))
    blocks = P(None, None, ("grp", "dev"))
    placed = (points,) * 3 + (blocks,) * 9 + (P(None, None, "grp"),) + (points,) * 4
    return jax.shard_map(on_device, mesh=mesh, in_specs=placed, out_specs=points, check_vma=False)
```

```python
import functools
import math

import jax
import jax.numpy as jnp
from jax import lax
from jax.experimental import pallas as pl
from jax.experimental.pallas import tpu as pltpu
from jax.sharding import PartitionSpec as P

REACH = 4
FAN = 8

INV_FOUR_PI = 1.0 / (4.0 * math.pi)
SOFTEN = 0.25
ROWS = 8

BF16 = jnp.bfloat16
F32 = jnp.float32


def dot(a, b):
    return jnp.dot(a, b, preferred_element_type=F32)


def dot_t(a, b):
    return lax.dot_general(a, b, (((1,), (1,)), ((), ())), preferred_element_type=F32)


def dot_0(a, b):
    return lax.dot_general(a, b, (((0,), (0,)), ((), ())), preferred_element_type=F32)


def low_half(shape):
    width = shape[-1]
    return lax.broadcasted_iota(jnp.int32, shape, len(shape) - 1) < width // 2


def pair(low, first, second):
    return jnp.where(low, first, second)


def swap(tile):
    half = tile.shape[-1] // 2
    return jnp.concatenate([tile[..., half:], tile[..., :half]], axis=-1)


def twice(tile):
    return jnp.concatenate([tile, tile], axis=-1)


def three(value):
    first = value.astype(BF16).astype(F32)
    rest = value - first
    second = rest.astype(BF16).astype(F32)
    return first, second, rest - second


def source_rows(x, y, z):
    return (-2.0 * x, -2.0 * y, -2.0 * z) + three(x * x + y * y + z * z)


def row_mask(shape, rows):
    row = lax.broadcasted_iota(jnp.int32, shape, 0)
    found = row == rows[0]
    for r in rows[1:]:
        found = found | (row == r)
    return found.astype(F32)


def source_tail(width):
    return row_mask((ROWS, width), (3, 4, 5, 6)).astype(BF16)


def target_of(rows):
    rows = rows.astype(F32)
    shape = rows.shape
    squares = row_mask(shape, (3, 4, 5))
    upper = rows * (-0.5 * row_mask(shape, (0, 1, 2))) + squares
    lower = rows * squares + SOFTEN * row_mask(shape, (6,))
    return jnp.concatenate([upper, lower], axis=0).astype(BF16)


def put_rows(ref, rows, count):
    for f in range(ROWS):
        value = rows[f] if f < len(rows) else jnp.zeros_like(rows[0])
        ref[pl.ds(f, count, stride=ROWS), :] = value


def stack_rows(rows):
    n = rows[0].shape[1]
    return jnp.concatenate(tuple(rows) + (jnp.zeros((ROWS - len(rows), n), F32),), axis=0)


def couplings(target, slots, source_ref, tail):
    low = low_half(source_ref.shape[1:])
    tiles = [
        jnp.concatenate([pair(low, source_ref[first], source_ref[second]), tail], axis=0)
        for first, second in zip(slots[0::2], slots[1::2])
    ]
    square = dot_0(target, jnp.concatenate(tiles, axis=1))
    return lax.rsqrt(square.astype(BF16))


def gathered(slots, moment_ref):
    low = low_half(moment_ref.shape[1:])
    tiles = [pair(low, moment_ref[first], moment_ref[second]) for first, second in zip(slots[0::2], slots[1::2])]
    return jnp.concatenate(tiles, axis=1)


def interact(target, slots, source_ref, tail, moment_ref):
    kern = couplings(target, slots, source_ref, tail)
    return INV_FOUR_PI * dot_t(gathered(slots, moment_ref), kern)


def listed_kernel(send_ref, charges_ref, basis_ref, proxy_ref, moment_ref, own_ref, out_ref, tile_ref):
    slots, devices = send_ref.shape
    leaves, rhs, rank2 = moment_ref.shape
    low = low_half((rhs, rank2))
    put_rows(tile_ref, source_rows(*[twice(jnp.transpose(proxy_ref[c].astype(F32))) for c in range(3)]), leaves)
    own_ref[...] = tile_ref[...].astype(BF16).reshape(own_ref.shape)

    def leaf_pair(i, carry):
        columns = pl.ds(pl.multiple_of(i * rank2, rank2), rank2)
        q = charges_ref[:, columns]
        u = basis_ref[:, columns]
        zero = jnp.zeros_like(q)
        stacked = jnp.concatenate([jnp.where(low, q, zero), jnp.where(low, zero, q)], axis=0)
        product = dot_t(stacked, jnp.concatenate([u, u], axis=0)).astype(BF16)
        moment_ref[2 * i] = product[:rhs]
        moment_ref[2 * i + 1] = product[rhs:]
        return carry

    lax.fori_loop(0, leaves // 2, leaf_pair, 0, unroll=8)
    low8 = low_half((ROWS, rank2))
    base = slots // 2 * rhs

    def pack(p, carry):
        s = [send_ref[t, p] for t in range(slots)]
        for q in range(slots // 2):
            first, second = s[2 * q], s[2 * q + 1]
            out_ref[p, q * rhs : (q + 1) * rhs, :] = pair(low, moment_ref[first], moment_ref[second])
            out_ref[p, base + q * ROWS : base + (q + 1) * ROWS, :] = pair(low8, own_ref[first], own_ref[second])
        return carry

    lax.fori_loop(0, devices, pack, 0, unroll=4)


def relayout(x_ref, scratch_ref):
    rank, _, leaves = x_ref.shape
    half = rank // 2
    eye = (
        lax.broadcasted_iota(jnp.int32, (leaves, leaves), 0)
        == lax.broadcasted_iota(jnp.int32, (leaves, leaves), 1)
    ).astype(BF16)
    for k in range(0, half, 2):
        block = jnp.concatenate(
            [x_ref[k], x_ref[k + half], x_ref[k + 1], x_ref[k + 1 + half]], axis=0
        )
        turned = dot_t(eye, block)
        for n in range(2):
            scratch_ref[pl.ds(k + n, leaves, stride=half), :] = turned[:, n * 2 * rank : (n + 1) * 2 * rank]


def spread_rows(block, low):
    zero = jnp.zeros_like(block)
    return jnp.concatenate([jnp.where(low, block, zero), jnp.where(low, zero, block)], axis=0)


def upward_kernel(
    moment_ref, up_leaf_ref, up_branch_ref, up_device_ref, pbranch_ref, pdevice_ref, out_ref, scratch_ref, branch_ref
):
    leaves, rhs, rank2 = moment_ref.shape
    rank = rank2 // 2
    half = rank // 2
    branches = leaves // FAN
    relayout(up_leaf_ref, scratch_ref)
    low = low_half((half, rank2))
    low_m = low_half((rhs, rank2))
    low_r = low_half((ROWS, rank2))
    wide = up_branch_ref[...].astype(F32).reshape(rank * branches, rank)
    branch_ref[...] = twice(wide)
    rows = source_rows(*[twice(pbranch_ref[c].astype(F32)) for c in range(3)])
    m_device = jnp.zeros((rhs, rank), F32)
    previous = None
    base = branches // 2 * rhs
    for c in range(branches):
        blocks, moments = [], []
        for b in range(c * FAN, (c + 1) * FAN):
            block = scratch_ref[b * half : (b + 1) * half, :].astype(BF16)
            blocks.append(spread_rows(block, low))
            moments.append(moment_ref[b])
        m_branch = dot_t(jnp.concatenate(moments, axis=1), jnp.concatenate(blocks, axis=1)).astype(BF16)
        matrix = branch_ref[pl.ds(c, rank, stride=branches), :][:, :rank].astype(BF16)
        m_device = m_device + dot_t(m_branch, matrix)
        spread = twice(m_branch)
        source = stack_rows([r[c : c + 1, :] for r in rows]).astype(BF16)
        if c % 2 == 1:
            q = c // 2
            out_ref[q * rhs : (q + 1) * rhs, :] = pair(low_m, previous[0], spread)
            out_ref[base + q * ROWS : base + (q + 1) * ROWS, :] = pair(low_r, previous[1], source)
        previous = spread, source
    base = base + branches // 2 * ROWS
    m_device = m_device.astype(BF16)
    share = dot_t(m_device, up_device_ref[...]).astype(BF16)
    out_ref[base : base + rhs, :] = jnp.concatenate([m_device, share], axis=1)
    rows = source_rows(*[twice(pdevice_ref[c : c + 1, :].astype(F32)) for c in range(3)])
    out_ref[base + rhs :, :] = stack_rows(rows).astype(BF16)


def near_kernel(
    near_ref, charges_ref, points_ref, left_ref, right_ref, down_leaf_ref, out_ref, down_ref,
    wide_ref, source_ref, target_ref, scratch_ref, weight_ref, kern_a_ref, kern_b_ref,
):
    rhs, total = charges_ref.shape
    entries, leaves = near_ref.shape
    size = total // leaves
    halo = REACH * size
    span = 2 * REACH + 1
    reach = (span + 1) * size
    pairs = leaves // 2
    relayout(down_leaf_ref, scratch_ref)
    down_ref[...] = scratch_ref[...].astype(BF16)

    wide_ref[:, :halo] = left_ref[:rhs, :]
    wide_ref[:, halo : halo + total] = charges_ref[...]
    wide_ref[:, halo + total :] = right_ref[:rhs, :]
    coords = [
        jnp.concatenate(
            [left_ref[rhs + c : rhs + c + 1, :], points_ref[c : c + 1, :], right_ref[rhs + c : rhs + c + 1, :]], axis=1
        ).astype(F32)
        for c in range(3)
    ]
    rows = stack_rows(source_rows(*coords))
    source_ref[...] = jnp.concatenate([rows.astype(BF16), source_tail(total + 2 * halo)], axis=0)
    target_ref[...] = target_of(rows[:, halo : halo + total])

    near = near_ref[...]
    counts = [jnp.sum((near == o - REACH).astype(F32), axis=0, keepdims=True) for o in range(span)]
    counts = jnp.concatenate(counts + [jnp.zeros((2 * ROWS - span, leaves), F32)], axis=0).astype(BF16)
    offset = lax.broadcasted_iota(jnp.int32, (2 * ROWS, reach), 0)
    block = lax.broadcasted_iota(jnp.int32, (2 * ROWS, reach), 1) // size
    for h in range(2):
        weight_ref[h] = dot_0(counts, (block == offset + h).astype(BF16))

    def evaluate(i, kern_ref):
        start = pl.multiple_of(i * 2 * size, 2 * size)
        square = dot_0(target_ref[:, pl.ds(start, 2 * size)], source_ref[:, pl.ds(start, reach)])
        kern = lax.rsqrt(square.astype(BF16))
        for h in range(2):
            weight = jnp.broadcast_to(weight_ref[h, pl.ds(2 * i + h, 1), :], (2 * ROWS, reach)).astype(BF16)
            for s in range(h * size, (h + 1) * size, 2 * ROWS):
                kern_ref[s : s + 2 * ROWS, :] = kern[s : s + 2 * ROWS, :] * weight

    def apply(i, kern_ref):
        start = pl.multiple_of(i * 2 * size, 2 * size)
        out_ref[:, pl.ds(start, 2 * size)] = INV_FOUR_PI * dot_t(wide_ref[:, pl.ds(start, reach)], kern_ref[...])

    evaluate(0, kern_a_ref)

    def step(t, carry):
        apply(2 * t, kern_a_ref)
        evaluate(2 * t + 1, kern_b_ref)
        evaluate(jnp.minimum(2 * t + 2, pairs - 1), kern_a_ref)
        apply(2 * t + 1, kern_b_ref)
        return carry

    lax.fori_loop(0, pairs // 2, step, 0)


def put_pair(moment_ref, slot, tile):
    low = low_half(tile.shape)
    other = swap(tile)
    moment_ref[slot] = pair(low, tile, other)
    moment_ref[slot + 1] = pair(low, other, tile)


def group_kernel(*refs, members):
    far_ref, pgroup_ref = refs[:2]
    parts = refs[2 : 2 + members]
    fb_ref, ld_ref, out_ref = refs[2 + members : 5 + members]
    moment_ref, source_ref, dev_m_ref, dev_source_ref = refs[5 + members :]
    entries, branches = far_ref.shape
    rhs, rank2 = moment_ref.shape[1:]
    rank = rank2 // 2
    me = lax.axis_index("dev")
    low = low_half((rhs, rank2))
    tail = source_tail(rank2)
    first = branches // 2 * rhs
    base = first + branches // 2 * ROWS
    m_group = jnp.zeros((rhs, rank2), F32)
    for s, part in enumerate(parts):
        owner = lax.rem(me - s + members, members)
        for q in range(branches // 2):
            put_pair(moment_ref, owner * branches + 2 * q, part[q * rhs : (q + 1) * rhs, :])
            put_pair(source_ref, owner * branches + 2 * q, part[first + q * ROWS : first + (q + 1) * ROWS, :])
        mixed = part[base : base + rhs, :].astype(F32)
        m_group = m_group + mixed
        keep = (jnp.abs(owner - me) >= 2).astype(F32)
        dev_m_ref[owner] = (pair(low, mixed, pltpu.roll(mixed, rank, 1)) * keep).astype(BF16)
        dev_source_ref[owner] = part[base + rhs :, :]
    out_ref[:rhs, :] = twice(m_group[:, rank:]).astype(BF16)
    rows = source_rows(*[twice(pgroup_ref[c : c + 1, :].astype(F32)) for c in range(3)])
    out_ref[rhs:, :] = stack_rows(rows).astype(BF16)

    for c in range(branches):
        target = target_of(source_ref[me * branches + c][:, :rank])
        fb_ref[c] = interact(target, [far_ref[e, c] for e in range(entries)], source_ref, tail, moment_ref)
    target = target_of(dev_source_ref[me][:, :rank])
    ld_ref[...] = interact(target, list(range(members)), dev_source_ref, tail, dev_m_ref)


def downward_kernel(*refs, groups):
    far_ref = refs[0]
    tiles = refs[1 : 1 + groups]
    (
        fb_ref, ld_ref, down_device_ref, down_branch_ref, down_ref, own_ref, own_m_ref, recv_ref, basis_ref, near_ref,
        out_ref, moment_ref, source_ref, grp_m_ref, grp_source_ref, branch_ref, parent_ref, kern_a_ref, kern_b_ref,
    ) = refs[1 + groups :]
    entries, leaves = far_ref.shape
    rhs, rank2 = moment_ref.shape[1:]
    rank = rank2 // 2
    half = rank // 2
    branches = leaves // FAN
    devices = recv_ref.shape[0]
    slots = (moment_ref.shape[0] - leaves) // devices
    pairs = leaves // 2
    me = lax.axis_index("grp")
    low = low_half((rhs, rank2))
    tail = source_tail(rank2)

    for s, tile_ref in enumerate(tiles):
        owner = lax.rem(me - s + groups, groups)
        keep = (jnp.abs(owner - me) >= 2).astype(F32)
        grp_m_ref[owner] = (tile_ref[:rhs, :].astype(F32) * keep).astype(BF16)
        grp_source_ref[owner] = tile_ref[rhs:, :]
    target = target_of(tiles[0][rhs:, :rank])
    l_group = interact(target, list(range(groups)), grp_source_ref, tail, grp_m_ref).astype(BF16)
    l_device = (ld_ref[...] + dot_t(l_group, down_device_ref[...])).astype(BF16)
    branch_ref[...] = twice(down_branch_ref[...].astype(F32).reshape(rank * branches, rank))
    for c in range(branches):
        matrix = branch_ref[pl.ds(c, rank, stride=branches), :][:, :rank].astype(BF16)
        parent_ref[c] = twice((fb_ref[c] + dot_t(l_device, matrix)).astype(BF16))

    moment_ref[:leaves] = own_m_ref[...]
    source_ref[:leaves] = own_ref[...]
    base = slots // 2 * rhs

    def unpack(p, carry):
        for q in range(slots // 2):
            slot = leaves + p * slots + 2 * q
            put_pair(moment_ref, slot, recv_ref[p, q * rhs : (q + 1) * rhs, :])
            put_pair(source_ref, slot, recv_ref[p, base + q * ROWS : base + (q + 1) * ROWS, :])
        return carry

    lax.fori_loop(0, devices, unpack, 0, unroll=4)
    low_d = low_half((half, rank2))

    def named(b):
        return [far_ref[e, b] for e in range(entries)]

    def evaluate(i, kern_ref):
        for h in range(2):
            b = 2 * i + h
            kern_ref[h] = couplings(target_of(source_ref[b][:, :rank]), named(b), source_ref, tail)

    def apply(i, kern_ref):
        sums = []
        for h in range(2):
            b = 2 * i + h
            far = INV_FOUR_PI * dot_t(gathered(named(b), moment_ref), kern_ref[h])
            rows = down_ref[pl.ds(pl.multiple_of(b * half, half), half), :]
            sums.append((far + dot_t(parent_ref[b // FAN], spread_rows(rows, low_d))).astype(BF16))
        return jnp.concatenate(sums, axis=0)

    def finish(i, sums):
        columns = pl.ds(pl.multiple_of(i * rank2, rank2), rank2)
        product = dot(sums, basis_ref[:, columns])
        out_ref[:, columns] = near_ref[:, columns] + pair(low, product[:rhs], product[rhs:])

    evaluate(0, kern_a_ref)

    def step(t, sums):
        finish(jnp.maximum(2 * t - 1, 0), sums)
        sums = apply(2 * t, kern_a_ref)
        evaluate(2 * t + 1, kern_b_ref)
        finish(2 * t, sums)
        evaluate(jnp.minimum(2 * t + 2, pairs - 1), kern_a_ref)
        return apply(2 * t + 1, kern_b_ref)

    finish(pairs - 1, lax.fori_loop(0, pairs // 2, step, jnp.zeros((2 * rhs, rank), BF16)))


VMEM = functools.partial(pl.BlockSpec, memory_space=pltpu.VMEM)
SMEM = functools.partial(pl.BlockSpec, memory_space=pltpu.SMEM)


def struct(shape, dtype):
    return jax.ShapeDtypeStruct(shape, dtype)


def on_device(
    charges, points, basis, up_leaf, up_branch, up_device, down_leaf, down_branch, down_device,
    proxy_leaf, proxy_branch, proxy_device, proxy_group, far_leaf, send_leaf, far_branch, near_leaf,
):
    rhs, total = charges.shape
    rank = basis.shape[0]
    leaves = up_leaf.shape[2]
    size = total // leaves
    branches = leaves // FAN
    slots = send_leaf.shape[0]
    groups = lax.axis_size("grp")
    members = lax.axis_size("dev")
    devices = groups * members
    rank2 = 2 * rank
    half = rank // 2
    halo = REACH * size
    assert rank == size and slots % 2 == 0 and branches % 2 == 0

    moments, own, listed = pl.pallas_call(
        listed_kernel,
        out_shape=(
            struct((leaves, rhs, rank2), BF16),
            struct((leaves, ROWS, rank2), BF16),
            struct((devices, slots // 2 * (rhs + ROWS), rank2), BF16),
        ),
        in_specs=[SMEM(), VMEM(), VMEM(), VMEM()],
        out_specs=(VMEM(), VMEM(), VMEM()),
        scratch_shapes=[pltpu.VMEM((leaves * ROWS, rank2), F32)],
        name="listed",
    )(send_leaf, charges, basis, proxy_leaf)
    received = lax.all_to_all(listed, ("grp", "dev"), split_axis=0, concat_axis=0, tiled=True)

    stacked = jnp.concatenate([charges, points], axis=0)
    last = devices - 1
    left = lax.ppermute(stacked[:, total - halo :], ("grp", "dev"), [(i, i + 1) for i in range(last)])
    right = lax.ppermute(stacked[:, :halo], ("grp", "dev"), [(i + 1, i) for i in range(last)])

    shared = pl.pallas_call(
        upward_kernel,
        out_shape=struct(((branches // 2 + 1) * (rhs + ROWS), rank2), BF16),
        in_specs=[VMEM()] * 6,
        out_specs=VMEM(),
        scratch_shapes=[pltpu.VMEM((leaves * half, rank2), F32), pltpu.VMEM((rank * branches, rank2), F32)],
        name="upward",
    )(
        moments,
        up_leaf,
        jnp.transpose(up_branch, (0, 2, 1)),
        up_device[:, :, 0],
        jnp.transpose(proxy_branch, (0, 2, 1)),
        proxy_device[:, :, 0],
    )
    parts = [shared] + [
        lax.ppermute(shared, "dev", [(i, (i + s) % members) for i in range(members)]) for s in range(1, members)
    ]

    reach = (2 * REACH + 2) * size
    near, down = pl.pallas_call(
        near_kernel,
        out_shape=(struct((rhs, total), F32), struct((leaves * half, rank2), BF16)),
        in_specs=[VMEM()] * 6,
        out_specs=(VMEM(), VMEM()),
        scratch_shapes=[
            pltpu.VMEM((rhs, total + 2 * halo), BF16),
            pltpu.VMEM((2 * ROWS, total + 2 * halo), BF16),
            pltpu.VMEM((2 * ROWS, total), BF16),
            pltpu.VMEM((leaves * half, rank2), F32),
            pltpu.VMEM((2, leaves, reach), F32),
            pltpu.VMEM((2 * size, reach), BF16),
            pltpu.VMEM((2 * size, reach), BF16),
        ],
        name="near",
    )(near_leaf, charges, points, left, right, down_leaf)

    far_b, part_d, tile = pl.pallas_call(
        functools.partial(group_kernel, members=members),
        out_shape=(struct((branches, rhs, rank), F32), struct((rhs, rank), F32), struct((rhs + ROWS, rank2), BF16)),
        in_specs=[SMEM(), VMEM()] + [VMEM()] * members,
        out_specs=(VMEM(), VMEM(), VMEM()),
        scratch_shapes=[
            pltpu.VMEM((members * branches, rhs, rank2), BF16),
            pltpu.VMEM((members * branches, ROWS, rank2), BF16),
            pltpu.VMEM((members, rhs, rank2), BF16),
            pltpu.VMEM((members, ROWS, rank2), BF16),
        ],
        name="group",
    )(far_branch, proxy_group[:, :, 0], *parts)
    tiles = [tile] + [
        lax.ppermute(tile, "grp", [(i, (i + s) % groups) for i in range(groups)]) for s in range(1, groups)
    ]

    table = leaves + devices * slots
    return pl.pallas_call(
        functools.partial(downward_kernel, groups=groups),
        out_shape=struct((rhs, total), F32),
        in_specs=[SMEM()] + [VMEM()] * (groups + 10),
        out_specs=VMEM(),
        scratch_shapes=[
            pltpu.VMEM((table, rhs, rank2), BF16),
            pltpu.VMEM((table, ROWS, rank2), BF16),
            pltpu.VMEM((groups, rhs, rank2), BF16),
            pltpu.VMEM((groups, ROWS, rank2), BF16),
            pltpu.VMEM((rank * branches, rank2), F32),
            pltpu.VMEM((branches, rhs, rank2), BF16),
            pltpu.VMEM((2, rank, far_leaf.shape[0] * rank), BF16),
            pltpu.VMEM((2, rank, far_leaf.shape[0] * rank), BF16),
        ],
        name="downward",
    )(
        far_leaf, *tiles, far_b, part_d, down_device[:, :, 0], jnp.transpose(down_branch, (0, 2, 1)), down, own,
        moments, received, basis, near,
    )


def solution(mesh):
    points = P(None, ("grp", "dev"))
    blocks = P(None, None, ("grp", "dev"))
    placed = (points,) * 3 + (blocks,) * 9 + (P(None, None, "grp"),) + (points,) * 4
    return jax.shard_map(on_device, mesh=mesh, in_specs=placed, out_specs=points, check_vma=False)
```

```python
import functools
import math

import jax
import jax.numpy as jnp
from jax import lax
from jax.experimental import pallas as pl
from jax.experimental.pallas import tpu as pltpu
from jax.sharding import PartitionSpec as P

REACH = 4
FAN = 8

INV_FOUR_PI = 1.0 / (4.0 * math.pi)
SOFTEN = 0.25
ROWS = 8

BF16 = jnp.bfloat16
F32 = jnp.float32


def dot(a, b):
    return jnp.dot(a, b, preferred_element_type=F32)


def dot_t(a, b):
    return lax.dot_general(a, b, (((1,), (1,)), ((), ())), preferred_element_type=F32)


def dot_0(a, b):
    return lax.dot_general(a, b, (((0,), (0,)), ((), ())), preferred_element_type=F32)


def low_half(shape):
    width = shape[-1]
    return lax.broadcasted_iota(jnp.int32, shape, len(shape) - 1) < width // 2


def pair(low, first, second):
    return jnp.where(low, first, second)


def swap(tile):
    half = tile.shape[-1] // 2
    return jnp.concatenate([tile[..., half:], tile[..., :half]], axis=-1)


def twice(tile):
    return jnp.concatenate([tile, tile], axis=-1)


def three(value):
    first = value.astype(BF16).astype(F32)
    rest = value - first
    second = rest.astype(BF16).astype(F32)
    return first, second, rest - second


def source_rows(x, y, z):
    return (-2.0 * x, -2.0 * y, -2.0 * z) + three(x * x + y * y + z * z)


def row_mask(shape, rows):
    row = lax.broadcasted_iota(jnp.int32, shape, 0)
    found = row == rows[0]
    for r in rows[1:]:
        found = found | (row == r)
    return found.astype(F32)


def source_tail(width):
    return row_mask((ROWS, width), (3, 4, 5, 6)).astype(BF16)


def target_of(rows):
    rows = rows.astype(F32)
    shape = rows.shape
    squares = row_mask(shape, (3, 4, 5))
    upper = rows * (-0.5 * row_mask(shape, (0, 1, 2))) + squares
    lower = rows * squares + SOFTEN * row_mask(shape, (6,))
    return jnp.concatenate([upper, lower], axis=0).astype(BF16)


def put_rows(ref, rows, count):
    for f in range(ROWS):
        value = rows[f] if f < len(rows) else jnp.zeros_like(rows[0])
        ref[pl.ds(f, count, stride=ROWS), :] = value


def stack_rows(rows):
    n = rows[0].shape[1]
    return jnp.concatenate(tuple(rows) + (jnp.zeros((ROWS - len(rows), n), F32),), axis=0)


def couplings(target, slots, source_ref, tail):
    low = low_half(source_ref.shape[1:])
    tiles = [
        jnp.concatenate([pair(low, source_ref[first], source_ref[second]), tail], axis=0)
        for first, second in zip(slots[0::2], slots[1::2])
    ]
    return kern_of(dot_0(target, jnp.concatenate(tiles, axis=1)))


def kern_of(square):
    return (INV_FOUR_PI * lax.rsqrt(square)).astype(BF16)


def gathered(slots, moment_ref):
    low = low_half(moment_ref.shape[1:])
    tiles = [pair(low, moment_ref[first], moment_ref[second]) for first, second in zip(slots[0::2], slots[1::2])]
    return jnp.concatenate(tiles, axis=1)


def interact(target, slots, source_ref, tail, moment_ref):
    return dot_t(gathered(slots, moment_ref), couplings(target, slots, source_ref, tail))


def listed_kernel(
    send_ref, charges_ref, points_ref, basis_ref, proxy_ref, moment_ref, own_ref, out_ref, head_ref, last_ref, tile_ref
):
    slots, devices = send_ref.shape
    leaves, rhs, rank2 = moment_ref.shape
    low = low_half((rhs, rank2))
    put_rows(tile_ref, source_rows(*[twice(jnp.transpose(proxy_ref[c].astype(F32))) for c in range(3)]), leaves)
    own_ref[...] = tile_ref[...].astype(BF16).reshape(own_ref.shape)

    def leaf_pair(i, carry):
        columns = pl.ds(pl.multiple_of(i * rank2, rank2), rank2)
        q = charges_ref[:, columns]
        u = basis_ref[:, columns]
        zero = jnp.zeros_like(q)
        stacked = jnp.concatenate([jnp.where(low, q, zero), jnp.where(low, zero, q)], axis=0)
        product = dot_t(stacked, jnp.concatenate([u, u], axis=0)).astype(BF16)
        moment_ref[2 * i] = product[:rhs]
        moment_ref[2 * i + 1] = product[rhs:]
        return carry

    lax.fori_loop(0, leaves // 2, leaf_pair, 0, unroll=8)
    low8 = low_half((ROWS, rank2))
    base = slots // 2 * rhs

    def pack(p, carry):
        s = [send_ref[t, p] for t in range(slots)]
        for q in range(slots // 2):
            first, second = s[2 * q], s[2 * q + 1]
            out_ref[p, q * rhs : (q + 1) * rhs, :] = pair(low, moment_ref[first], moment_ref[second])
            out_ref[p, base + q * ROWS : base + (q + 1) * ROWS, :] = pair(low8, own_ref[first], own_ref[second])
        return carry

    lax.fori_loop(0, devices, pack, 0, unroll=4)
    total = charges_ref.shape[1]
    halo = head_ref.shape[1]
    for ref, start in ((head_ref, 0), (last_ref, total - halo)):
        ref[:rhs, :] = charges_ref[:, start : start + halo]
        ref[rhs:, :] = jnp.zeros((ROWS, halo), BF16)
        ref[rhs : rhs + 3, :] = points_ref[:, start : start + halo]


def relayout(x_ref, scratch_ref):
    rank, _, leaves = x_ref.shape
    half = rank // 2
    eye = (
        lax.broadcasted_iota(jnp.int32, (leaves, leaves), 0)
        == lax.broadcasted_iota(jnp.int32, (leaves, leaves), 1)
    ).astype(BF16)
    for k in range(0, half, 2):
        block = jnp.concatenate(
            [x_ref[k], x_ref[k + half], x_ref[k + 1], x_ref[k + 1 + half]], axis=0
        )
        turned = dot_t(eye, block)
        for n in range(2):
            scratch_ref[pl.ds(k + n, leaves, stride=half), :] = turned[:, n * 2 * rank : (n + 1) * 2 * rank]


def spread_rows(block, low):
    zero = jnp.zeros_like(block)
    return jnp.concatenate([jnp.where(low, block, zero), jnp.where(low, zero, block)], axis=0)


def upward_kernel(
    moment_ref, up_leaf_ref, up_branch_ref, up_device_ref, pbranch_ref, pdevice_ref, out_ref, scratch_ref, branch_ref
):
    leaves, rhs, rank2 = moment_ref.shape
    rank = rank2 // 2
    half = rank // 2
    branches = leaves // FAN
    relayout(up_leaf_ref, scratch_ref)
    low = low_half((half, rank2))
    low_m = low_half((rhs, rank2))
    low_r = low_half((ROWS, rank2))
    wide = up_branch_ref[...].astype(F32).reshape(rank * branches, rank)
    branch_ref[...] = twice(wide)
    rows = source_rows(*[twice(pbranch_ref[c].astype(F32)) for c in range(3)])
    m_device = jnp.zeros((rhs, rank), F32)
    previous = None
    base = branches // 2 * rhs
    for c in range(branches):
        blocks, moments = [], []
        for b in range(c * FAN, (c + 1) * FAN):
            block = scratch_ref[b * half : (b + 1) * half, :].astype(BF16)
            blocks.append(spread_rows(block, low))
            moments.append(moment_ref[b])
        m_branch = dot_t(jnp.concatenate(moments, axis=1), jnp.concatenate(blocks, axis=1)).astype(BF16)
        matrix = branch_ref[pl.ds(c, rank, stride=branches), :][:, :rank].astype(BF16)
        m_device = m_device + dot_t(m_branch, matrix)
        spread = twice(m_branch)
        source = stack_rows([r[c : c + 1, :] for r in rows]).astype(BF16)
        if c % 2 == 1:
            q = c // 2
            out_ref[q * rhs : (q + 1) * rhs, :] = pair(low_m, previous[0], spread)
            out_ref[base + q * ROWS : base + (q + 1) * ROWS, :] = pair(low_r, previous[1], source)
        previous = spread, source
    base = base + branches // 2 * ROWS
    m_device = m_device.astype(BF16)
    share = dot_t(m_device, up_device_ref[...]).astype(BF16)
    out_ref[base : base + rhs, :] = jnp.concatenate([m_device, share], axis=1)
    rows = source_rows(*[twice(pdevice_ref[c : c + 1, :].astype(F32)) for c in range(3)])
    out_ref[base + rhs :, :] = stack_rows(rows).astype(BF16)


def turn_kernel(down_leaf_ref, _, down_ref, scratch_ref):
    relayout(down_leaf_ref, scratch_ref)
    down_ref[...] = scratch_ref[...].astype(BF16)


def near_kernel(
    near_ref, charges_ref, points_ref, left_ref, right_ref, _, out_ref,
    wide_ref, source_ref, target_ref, weight_ref, kern_a_ref, kern_b_ref,
):
    rhs, total = charges_ref.shape
    _, leaves = near_ref.shape
    size = total // leaves
    halo = REACH * size
    span = 2 * REACH + 1
    reach = (span + 1) * size
    pairs = leaves // 2
    wide_ref[:, :halo] = left_ref[:rhs, :]
    wide_ref[:, halo : halo + total] = charges_ref[...]
    wide_ref[:, halo + total :] = right_ref[:rhs, :]
    coords = [
        jnp.concatenate(
            [left_ref[rhs + c : rhs + c + 1, :], points_ref[c : c + 1, :], right_ref[rhs + c : rhs + c + 1, :]], axis=1
        ).astype(F32)
        for c in range(3)
    ]
    rows = stack_rows(source_rows(*coords))
    source_ref[...] = jnp.concatenate([rows.astype(BF16), source_tail(total + 2 * halo)], axis=0)
    target_ref[...] = target_of(rows[:, halo : halo + total])

    near = near_ref[...]
    counts = [jnp.sum((near == o - REACH).astype(F32), axis=0, keepdims=True) for o in range(span)]
    counts = jnp.concatenate(counts + [jnp.zeros((2 * ROWS - span, leaves), F32)], axis=0).astype(BF16)
    offset = lax.broadcasted_iota(jnp.int32, (2 * ROWS, reach), 0)
    block = lax.broadcasted_iota(jnp.int32, (2 * ROWS, reach), 1) // size
    for h in range(2):
        weight_ref[h] = dot_0(counts, (block == offset + h).astype(BF16))

    def evaluate(i, kern_ref):
        start = pl.multiple_of(i * 2 * size, 2 * size)
        square = dot_0(target_ref[:, pl.ds(start, 2 * size)], source_ref[:, pl.ds(start, reach)])
        kern = kern_of(square)
        for h in range(2):
            weight = jnp.broadcast_to(weight_ref[h, pl.ds(2 * i + h, 1), :], (2 * ROWS, reach)).astype(BF16)
            for s in range(h * size, (h + 1) * size, 2 * ROWS):
                kern_ref[s : s + 2 * ROWS, :] = kern[s : s + 2 * ROWS, :] * weight

    def apply(i, kern_ref):
        start = pl.multiple_of(i * 2 * size, 2 * size)
        out_ref[:, pl.ds(start, 2 * size)] = dot_t(wide_ref[:, pl.ds(start, reach)], kern_ref[...])

    evaluate(0, kern_a_ref)

    def step(t, carry):
        apply(2 * t, kern_a_ref)
        evaluate(2 * t + 1, kern_b_ref)
        evaluate(jnp.minimum(2 * t + 2, pairs - 1), kern_a_ref)
        apply(2 * t + 1, kern_b_ref)
        return carry

    lax.fori_loop(0, pairs // 2, step, 0)


def put_pair(moment_ref, slot, tile):
    low = low_half(tile.shape)
    other = swap(tile)
    moment_ref[slot] = pair(low, tile, other)
    moment_ref[slot + 1] = pair(low, other, tile)


def part_of(parts, s, members):
    length = parts[0].shape[0] // 2
    owner = lax.rem(lax.axis_index("dev") - s // 2 * 2 + members, members)
    owner = owner + s % 2 * (1 - 2 * lax.rem(owner, 2))
    return parts[s // 2].at[s % 2 * length : (s % 2 + 1) * length], owner


def top_kernel(*refs, members):
    _, pgroup_ref, *parts, out_ref = refs
    rhs = out_ref.shape[0] - ROWS
    rank2 = out_ref.shape[1]
    m_group = jnp.zeros((rhs, rank2), F32)
    for s in range(members):
        part, _ = part_of(parts, s, members)
        base = part.shape[0] - rhs - ROWS
        m_group = m_group + part[base : base + rhs, :].astype(F32)
    out_ref[:rhs, :] = twice(m_group[:, rank2 // 2 :]).astype(BF16)
    rows = source_rows(*[twice(pgroup_ref[c : c + 1, :].astype(F32)) for c in range(3)])
    out_ref[rhs:, :] = stack_rows(rows).astype(BF16)


def group_kernel(*refs, members):
    far_ref, _ = refs[:2]
    count = members // 2
    parts = refs[2 : 2 + count]
    fb_ref, ld_ref = refs[2 + count : 4 + count]
    moment_ref, source_ref, dev_m_ref, dev_source_ref = refs[4 + count :]
    branches, entries = far_ref.shape
    rhs, rank2 = moment_ref.shape[1:]
    rank = rank2 // 2
    me = lax.axis_index("dev")
    low = low_half((rhs, rank2))
    tail = source_tail(rank2)
    first = branches // 2 * rhs
    base = first + branches // 2 * ROWS
    for s in range(members):
        part, owner = part_of(parts, s, members)
        for q in range(branches // 2):
            put_pair(moment_ref, owner * branches + 2 * q, part[q * rhs : (q + 1) * rhs, :])
            put_pair(source_ref, owner * branches + 2 * q, part[first + q * ROWS : first + (q + 1) * ROWS, :])
        mixed = part[base : base + rhs, :].astype(F32)
        keep = (jnp.abs(owner - me) >= 2).astype(F32)
        dev_m_ref[owner] = (pair(low, mixed, pltpu.roll(mixed, rank, 1)) * keep).astype(BF16)
        dev_source_ref[owner] = part[base + rhs :, :]
    for c in range(branches):
        target = target_of(source_ref[me * branches + c][:, :rank])
        fb_ref[c] = interact(target, [far_ref[c, e] for e in range(entries)], source_ref, tail, moment_ref)
    target = target_of(dev_source_ref[me][:, :rank])
    ld_ref[...] = interact(target, list(range(members)), dev_source_ref, tail, dev_m_ref)


def downward_kernel(*refs, groups):
    far_ref = refs[0]
    tiles = refs[1 : 1 + groups]
    (
        fb_ref, ld_ref, down_device_ref, down_branch_ref, down_ref, own_ref, own_m_ref, recv_ref, basis_ref, near_ref,
        out_ref, moment_ref, source_ref, grp_m_ref, grp_source_ref, branch_ref, parent_ref, kern_a_ref, kern_b_ref,
    ) = refs[1 + groups :]
    entries, leaves = far_ref.shape
    rhs, rank2 = moment_ref.shape[1:]
    rank = rank2 // 2
    half = rank // 2
    branches = leaves // FAN
    devices = recv_ref.shape[0]
    slots = (moment_ref.shape[0] - leaves) // devices
    pairs = leaves // 2
    me = lax.axis_index("grp")
    low = low_half((rhs, rank2))
    tail = source_tail(rank2)

    for s, tile_ref in enumerate(tiles):
        owner = lax.rem(me - s + groups, groups)
        keep = (jnp.abs(owner - me) >= 2).astype(F32)
        grp_m_ref[owner] = (tile_ref[:rhs, :].astype(F32) * keep).astype(BF16)
        grp_source_ref[owner] = tile_ref[rhs:, :]
    target = target_of(tiles[0][rhs:, :rank])
    l_group = interact(target, list(range(groups)), grp_source_ref, tail, grp_m_ref).astype(BF16)
    l_device = (ld_ref[...] + dot_t(l_group, down_device_ref[...])).astype(BF16)
    branch_ref[...] = twice(down_branch_ref[...].astype(F32).reshape(rank * branches, rank))
    for c in range(branches):
        matrix = branch_ref[pl.ds(c, rank, stride=branches), :][:, :rank].astype(BF16)
        parent_ref[c] = twice((fb_ref[c] + dot_t(l_device, matrix)).astype(BF16))

    moment_ref[:leaves] = own_m_ref[...]
    source_ref[:leaves] = own_ref[...]
    base = slots // 2 * rhs

    def unpack(p, carry):
        for q in range(slots // 2):
            slot = leaves + p * slots + 2 * q
            put_pair(moment_ref, slot, recv_ref[p, q * rhs : (q + 1) * rhs, :])
            put_pair(source_ref, slot, recv_ref[p, base + q * ROWS : base + (q + 1) * ROWS, :])
        return carry

    lax.fori_loop(0, devices, unpack, 0, unroll=4)
    low_d = low_half((half, rank2))

    def named(b):
        return [far_ref[e, b] for e in range(entries)]

    def evaluate(i, kern_ref):
        for h in range(2):
            b = 2 * i + h
            kern_ref[h] = couplings(target_of(source_ref[b][:, :rank]), named(b), source_ref, tail)

    def apply(i, kern_ref):
        sums = []
        for h in range(2):
            b = 2 * i + h
            far = dot_t(gathered(named(b), moment_ref), kern_ref[h])
            rows = down_ref[pl.ds(pl.multiple_of(b * half, half), half), :]
            sums.append((far + dot_t(parent_ref[b // FAN], spread_rows(rows, low_d))).astype(BF16))
        return jnp.concatenate(sums, axis=0)

    def finish(i, sums):
        columns = pl.ds(pl.multiple_of(i * rank2, rank2), rank2)
        product = dot(sums, basis_ref[:, columns])
        out_ref[:, columns] = near_ref[:, columns] + pair(low, product[:rhs], product[rhs:])

    evaluate(0, kern_a_ref)

    def step(t, sums):
        finish(jnp.maximum(2 * t - 1, 0), sums)
        sums = apply(2 * t, kern_a_ref)
        evaluate(2 * t + 1, kern_b_ref)
        finish(2 * t, sums)
        evaluate(jnp.minimum(2 * t + 2, pairs - 1), kern_a_ref)
        return apply(2 * t + 1, kern_b_ref)

    finish(pairs - 1, lax.fori_loop(0, pairs // 2, step, jnp.zeros((2 * rhs, rank), BF16)))


VMEM = functools.partial(pl.BlockSpec, memory_space=pltpu.VMEM)
SMEM = functools.partial(pl.BlockSpec, memory_space=pltpu.SMEM)
ANY = functools.partial(pl.BlockSpec, memory_space=pl.ANY)
PARAMS = pltpu.CompilerParams()


def hbm(shape, dtype):
    return jax.ShapeDtypeStruct(shape, dtype)


def vmem(*arrays):
    return [pltpu.with_memory_space_constraint(a, pltpu.VMEM) if a.size <= 1 << 19 else a for a in arrays]


def on_device(
    charges, points, basis, up_leaf, up_branch, up_device, down_leaf, down_branch, down_device,
    proxy_leaf, proxy_branch, proxy_device, proxy_group, far_leaf, send_leaf, far_branch, near_leaf,
):
    rhs, total = charges.shape
    rank = basis.shape[0]
    leaves = up_leaf.shape[2]
    size = total // leaves
    branches = leaves // FAN
    slots = send_leaf.shape[0]
    groups = lax.axis_size("grp")
    members = lax.axis_size("dev")
    devices = groups * members
    rank2 = 2 * rank
    half = rank // 2
    halo = REACH * size
    assert rank == size and slots % 2 == 0 and branches % 2 == 0 and members % 2 == 0

    moments, own, listed, head, tail = pl.pallas_call(
        listed_kernel,
        out_shape=(
            pltpu.VMEM((leaves, rhs, rank2), BF16),
            hbm((leaves, ROWS, rank2), BF16),
            hbm((devices, slots // 2 * (rhs + ROWS), rank2), BF16),
            hbm((rhs + ROWS, halo), BF16),
            hbm((rhs + ROWS, halo), BF16),
        ),
        in_specs=[SMEM()] + [VMEM()] * 4,
        out_specs=(VMEM(),) * 5,
        scratch_shapes=[pltpu.VMEM((leaves * ROWS, rank2), F32)],
        compiler_params=PARAMS,
        name="listed",
    )(send_leaf, charges, points, basis, proxy_leaf)
    (moments,) = vmem(moments)
    received = lax.all_to_all(listed, ("grp", "dev"), split_axis=0, concat_axis=0, tiled=True)

    last = devices - 1
    left = lax.ppermute(tail, ("grp", "dev"), [(i, i + 1) for i in range(last)])
    right = lax.ppermute(head, ("grp", "dev"), [(i + 1, i) for i in range(last)])

    shared = pl.pallas_call(
        upward_kernel,
        out_shape=hbm(((branches // 2 + 1) * (rhs + ROWS), rank2), BF16),
        in_specs=[VMEM()] * 6,
        out_specs=VMEM(),
        scratch_shapes=[pltpu.VMEM((leaves * half, rank2), F32), pltpu.VMEM((rank * branches, rank2), F32)],
        compiler_params=PARAMS,
        name="upward",
    )(
        moments,
        up_leaf,
        jnp.transpose(up_branch, (0, 2, 1)),
        up_device[:, :, 0],
        jnp.transpose(proxy_branch, (0, 2, 1)),
        proxy_device[:, :, 0],
    )
    partner = lax.ppermute(shared, "dev", [(i, i ^ 1) for i in range(members)])
    down = pl.pallas_call(
        turn_kernel,
        out_shape=hbm((leaves * half, rank2), BF16),
        in_specs=[VMEM(), ANY()],
        out_specs=VMEM(),
        scratch_shapes=[pltpu.VMEM((leaves * half, rank2), F32)],
        compiler_params=PARAMS,
        name="turn",
    )(down_leaf, shared)
    partner, down = lax.optimization_barrier((partner, down))
    both = jnp.concatenate([shared, partner], axis=0)
    parts = [both] + [
        lax.ppermute(both, "dev", [(i, (i + s) % members) for i in range(members)]) for s in range(2, members, 2)
    ]

    reach = (2 * REACH + 2) * size
    near = pl.pallas_call(
        near_kernel,
        out_shape=pltpu.VMEM((rhs, total), F32),
        in_specs=[VMEM()] * 6,
        out_specs=VMEM(),
        scratch_shapes=[
            pltpu.VMEM((rhs, total + 2 * halo), BF16),
            pltpu.VMEM((2 * ROWS, total + 2 * halo), BF16),
            pltpu.VMEM((2 * ROWS, total), BF16),
            pltpu.VMEM((2, leaves, reach), F32),
            pltpu.VMEM((2 * size, reach), BF16),
            pltpu.VMEM((2 * size, reach), BF16),
        ],
        compiler_params=PARAMS,
        name="near",
    )(near_leaf, charges, points, *vmem(left, right, both))

    parts = vmem(*parts)
    tile = pl.pallas_call(
        functools.partial(top_kernel, members=members),
        out_shape=hbm((rhs + ROWS, rank2), BF16),
        in_specs=[VMEM()] * (2 + len(parts)),
        out_specs=VMEM(),
        compiler_params=PARAMS,
        name="top",
    )(*vmem(near), proxy_group[:, :, 0], *parts)
    tiles = [tile] + [
        lax.ppermute(tile, "grp", [(i, (i + s) % groups) for i in range(groups)]) for s in range(1, groups)
    ]
    far_b, part_d = pl.pallas_call(
        functools.partial(group_kernel, members=members),
        out_shape=(hbm((branches, rhs, rank), F32), hbm((rhs, rank), F32)),
        in_specs=[SMEM(), ANY()] + [VMEM()] * len(parts),
        out_specs=(VMEM(), VMEM()),
        scratch_shapes=[
            pltpu.VMEM((members * branches, rhs, rank2), BF16),
            pltpu.VMEM((members * branches, ROWS, rank2), BF16),
            pltpu.VMEM((members, rhs, rank2), BF16),
            pltpu.VMEM((members, ROWS, rank2), BF16),
        ],
        compiler_params=PARAMS,
        name="group",
    )(jnp.transpose(far_branch), tile, *parts)

    table = leaves + devices * slots
    return pl.pallas_call(
        functools.partial(downward_kernel, groups=groups),
        out_shape=hbm((rhs, total), F32),
        in_specs=[SMEM()] + [VMEM()] * (groups + 10),
        out_specs=VMEM(),
        scratch_shapes=[
            pltpu.VMEM((table, rhs, rank2), BF16),
            pltpu.VMEM((table, ROWS, rank2), BF16),
            pltpu.VMEM((groups, rhs, rank2), BF16),
            pltpu.VMEM((groups, ROWS, rank2), BF16),
            pltpu.VMEM((rank * branches, rank2), F32),
            pltpu.VMEM((branches, rhs, rank2), BF16),
            pltpu.VMEM((2, rank, far_leaf.shape[0] * rank), BF16),
            pltpu.VMEM((2, rank, far_leaf.shape[0] * rank), BF16),
        ],
        compiler_params=PARAMS,
        name="downward",
    )(
        far_leaf,
        tile,
        *vmem(*tiles[1:]),
        far_b,
        part_d,
        down_device[:, :, 0],
        jnp.transpose(down_branch, (0, 2, 1)),
        down,
        own,
        moments,
        *vmem(received),
        basis,
        *vmem(near),
    )


def solution(mesh):
    points = P(None, ("grp", "dev"))
    blocks = P(None, None, ("grp", "dev"))
    placed = (points,) * 3 + (blocks,) * 9 + (P(None, None, "grp"),) + (points,) * 4

    return jax.shard_map(on_device, mesh=mesh, in_specs=placed, out_specs=points, check_vma=False)
```

```python
import functools
import math

import jax
import jax.numpy as jnp
from jax import lax
from jax.experimental import pallas as pl
from jax.experimental.pallas import tpu as pltpu
from jax.sharding import PartitionSpec as P

REACH = 4
FAN = 8
ROUND = 8
PAIRS = 4

INV_FOUR_PI = 1.0 / (4.0 * math.pi)
SOFTEN = 0.25
ROWS = 8

BF16 = jnp.bfloat16
F32 = jnp.float32


def dot(a, b):
    return jnp.dot(a, b, preferred_element_type=F32)


def dot_t(a, b):
    return lax.dot_general(a, b, (((1,), (1,)), ((), ())), preferred_element_type=F32)


def dot_0(a, b):
    return lax.dot_general(a, b, (((0,), (0,)), ((), ())), preferred_element_type=F32)


def low_half(shape):
    width = shape[-1]
    return lax.broadcasted_iota(jnp.int32, shape, len(shape) - 1) < width // 2


def pair(low, first, second):
    return jnp.where(low, first, second)


def swap(tile):
    half = tile.shape[-1] // 2
    return jnp.concatenate([tile[..., half:], tile[..., :half]], axis=-1)


def twice(tile):
    return jnp.concatenate([tile, tile], axis=-1)


def three(value):
    first = value.astype(BF16).astype(F32)
    rest = value - first
    second = rest.astype(BF16).astype(F32)
    return first, second, rest - second


def source_rows(x, y, z):
    return (-2.0 * x, -2.0 * y, -2.0 * z) + three(x * x + y * y + z * z)


def row_mask(shape, rows):
    row = lax.broadcasted_iota(jnp.int32, shape, 0)
    found = row == rows[0]
    for r in rows[1:]:
        found = found | (row == r)
    return found.astype(F32)


def source_tail(width):
    return row_mask((ROWS, width), (3, 4, 5, 6)).astype(BF16)


def target_of(rows):
    rows = rows.astype(F32)
    shape = rows.shape
    squares = row_mask(shape, (3, 4, 5))
    upper = rows * (-0.5 * row_mask(shape, (0, 1, 2))) + squares
    lower = rows * squares + SOFTEN * row_mask(shape, (6,))
    return jnp.concatenate([upper, lower], axis=0).astype(BF16)


def put_rows(ref, rows, count):
    for f in range(ROWS):
        value = rows[f] if f < len(rows) else jnp.zeros_like(rows[0])
        ref[pl.ds(f, count, stride=ROWS), :] = value


def stack_rows(rows):
    n = rows[0].shape[1]
    return jnp.concatenate(tuple(rows) + (jnp.zeros((ROWS - len(rows), n), F32),), axis=0)


def couplings(target, slots, source_ref, tail):
    low = low_half(source_ref.shape[1:])
    tiles = [
        jnp.concatenate([pair(low, source_ref[first], source_ref[second]), tail], axis=0)
        for first, second in zip(slots[0::2], slots[1::2])
    ]
    return kern_of(dot_0(target, jnp.concatenate(tiles, axis=1)))


def kern_of(square):
    return (INV_FOUR_PI * lax.rsqrt(square)).astype(BF16)


def gathered(slots, moment_ref):
    low = low_half(moment_ref.shape[1:])
    tiles = [pair(low, moment_ref[first], moment_ref[second]) for first, second in zip(slots[0::2], slots[1::2])]
    return jnp.concatenate(tiles, axis=1)


def interact(target, slots, source_ref, tail, moment_ref):
    return dot_t(gathered(slots, moment_ref), couplings(target, slots, source_ref, tail))


def listed_kernel(
    send_ref, charges_ref, points_ref, basis_ref, proxy_ref, moment_ref, own_ref, out_ref, inner_ref, outer_ref, tile_ref
):
    slots, devices = send_ref.shape
    leaves, rhs, rank2 = moment_ref.shape
    low = low_half((rhs, rank2))
    put_rows(tile_ref, source_rows(*[twice(jnp.transpose(proxy_ref[c].astype(F32))) for c in range(3)]), leaves)
    own_ref[...] = tile_ref[...].astype(BF16).reshape(own_ref.shape)

    def leaf_pair(i, carry):
        columns = pl.ds(pl.multiple_of(i * rank2, rank2), rank2)
        q = charges_ref[:, columns]
        u = basis_ref[:, columns]
        zero = jnp.zeros_like(q)
        stacked = jnp.concatenate([jnp.where(low, q, zero), jnp.where(low, zero, q)], axis=0)
        product = dot_t(stacked, jnp.concatenate([u, u], axis=0)).astype(BF16)
        moment_ref[2 * i] = product[:rhs]
        moment_ref[2 * i + 1] = product[rhs:]
        return carry

    lax.fori_loop(0, leaves // 2, leaf_pair, 0, unroll=8)
    low8 = low_half((ROWS, rank2))
    base = slots // 2 * rhs

    def pack(p, carry):
        s = [send_ref[t, p] for t in range(slots)]
        for q in range(slots // 2):
            first, second = s[2 * q], s[2 * q + 1]
            out_ref[p, q * rhs : (q + 1) * rhs, :] = pair(low, moment_ref[first], moment_ref[second])
            out_ref[p, base + q * ROWS : base + (q + 1) * ROWS, :] = pair(low8, own_ref[first], own_ref[second])
        return carry

    lax.fori_loop(0, devices, pack, 0, unroll=4)
    total = charges_ref.shape[1]
    halo = inner_ref.shape[0] // (rhs + ROWS) * rank2
    odd = lax.rem(lax.axis_index("dev"), 2) == 1
    for ref, first in ((inner_ref, odd), (outer_ref, jnp.logical_not(odd))):
        start = jnp.where(first, 0, total - halo)
        for n in range(halo // rank2):
            columns = pl.ds(pl.multiple_of(start + n * rank2, rank2), rank2)
            base = n * (rhs + ROWS)
            ref[base : base + rhs, :] = charges_ref[:, columns]
            points = points_ref[:, columns].astype(F32)
            rows = jnp.concatenate([points, jnp.zeros((ROWS - 3, rank2), F32)], axis=0)
            ref[base + rhs : base + rhs + ROWS, :] = rows.astype(BF16)


def relayout(x_ref, scratch_ref):
    rank, _, leaves = x_ref.shape
    half = rank // 2
    eye = (
        lax.broadcasted_iota(jnp.int32, (leaves, leaves), 0)
        == lax.broadcasted_iota(jnp.int32, (leaves, leaves), 1)
    ).astype(BF16)
    for k in range(0, half, 2):
        block = jnp.concatenate(
            [x_ref[k], x_ref[k + half], x_ref[k + 1], x_ref[k + 1 + half]], axis=0
        )
        turned = dot_t(eye, block)
        for n in range(2):
            scratch_ref[pl.ds(k + n, leaves, stride=half), :] = turned[:, n * 2 * rank : (n + 1) * 2 * rank]


def spread_rows(block, low):
    zero = jnp.zeros_like(block)
    return jnp.concatenate([jnp.where(low, block, zero), jnp.where(low, zero, block)], axis=0)


def upward_kernel(
    moment_ref, up_leaf_ref, up_branch_ref, up_device_ref, pbranch_ref, pdevice_ref, out_ref, scratch_ref, branch_ref
):
    leaves, rhs, rank2 = moment_ref.shape
    rank = rank2 // 2
    half = rank // 2
    branches = leaves // FAN
    relayout(up_leaf_ref, scratch_ref)
    low = low_half((half, rank2))
    low_m = low_half((rhs, rank2))
    low_r = low_half((ROWS, rank2))
    wide = up_branch_ref[...].astype(F32).reshape(rank * branches, rank)
    branch_ref[...] = twice(wide)
    rows = source_rows(*[twice(pbranch_ref[c].astype(F32)) for c in range(3)])
    m_device = jnp.zeros((rhs, rank), F32)
    previous = None
    base = branches // 2 * rhs
    for c in range(branches):
        blocks, moments = [], []
        for b in range(c * FAN, (c + 1) * FAN):
            block = scratch_ref[b * half : (b + 1) * half, :].astype(BF16)
            blocks.append(spread_rows(block, low))
            moments.append(moment_ref[b])
        m_branch = dot_t(jnp.concatenate(moments, axis=1), jnp.concatenate(blocks, axis=1)).astype(BF16)
        matrix = branch_ref[pl.ds(c, rank, stride=branches), :][:, :rank].astype(BF16)
        m_device = m_device + dot_t(m_branch, matrix)
        spread = twice(m_branch)
        source = stack_rows([r[c : c + 1, :] for r in rows]).astype(BF16)
        if c % 2 == 1:
            q = c // 2
            out_ref[q * rhs : (q + 1) * rhs, :] = pair(low_m, previous[0], spread)
            out_ref[base + q * ROWS : base + (q + 1) * ROWS, :] = pair(low_r, previous[1], source)
        previous = spread, source
    base = base + branches // 2 * ROWS
    m_device = m_device.astype(BF16)
    share = dot_t(m_device, up_device_ref[...]).astype(BF16)
    out_ref[base : base + rhs, :] = jnp.concatenate([m_device, share], axis=1)
    rows = source_rows(*[twice(pdevice_ref[c : c + 1, :].astype(F32)) for c in range(3)])
    out_ref[base + rhs :, :] = stack_rows(rows).astype(BF16)


def turn_kernel(down_leaf_ref, far_ref, _, down_ref, turned_ref, scratch_ref):
    turned_ref[...] = jnp.transpose(far_ref[...].astype(F32)).astype(jnp.int32)
    relayout(down_leaf_ref, scratch_ref)
    down_ref[...] = scratch_ref[...].astype(BF16)


def near_kernel(
    near_ref, charges_ref, points_ref, inner_ref, outer_ref, _, out_ref,
    wide_ref, source_ref, target_ref, weight_ref, kern_a_ref, kern_b_ref,
):
    rhs, total = charges_ref.shape
    _, leaves = near_ref.shape
    size = total // leaves
    halo = REACH * size
    span = 2 * REACH + 1
    reach = (span + 1) * size
    odd = lax.rem(lax.axis_index("dev"), 2) == 1
    wide_ref[:, halo : halo + total] = charges_ref[...]
    lanes = 2 * size
    sides = [[], []]
    for n in range(halo // lanes):
        rows = slice(n * (rhs + ROWS), (n + 1) * (rhs + ROWS))
        inner, outer = inner_ref[rows, :], outer_ref[rows, :]
        for side, block in enumerate((jnp.where(odd, inner, outer), jnp.where(odd, outer, inner))):
            start = side * (halo + total) + n * lanes
            wide_ref[:, start : start + lanes] = block[:rhs, :]
            sides[side].append(block[rhs:, :].astype(F32))
    left, right = (jnp.concatenate(side, axis=1) for side in sides)
    coords = [
        jnp.concatenate([left[c : c + 1, :], points_ref[c : c + 1, :].astype(F32), right[c : c + 1, :]], axis=1)
        for c in range(3)
    ]
    rows = stack_rows(source_rows(*coords))
    source_ref[...] = jnp.concatenate([rows.astype(BF16), source_tail(total + 2 * halo)], axis=0)
    target_ref[...] = target_of(rows[:, halo : halo + total])

    near = near_ref[...]
    counts = [jnp.sum((near == o - REACH).astype(F32), axis=0, keepdims=True) for o in range(span)]
    counts = jnp.concatenate(counts + [jnp.zeros((2 * ROWS - span, leaves), F32)], axis=0).astype(BF16)
    offset = lax.broadcasted_iota(jnp.int32, (2 * ROWS, reach), 0)
    block = lax.broadcasted_iota(jnp.int32, (2 * ROWS, reach), 1) // size
    for h in range(2):
        weight_ref[h] = dot_0(counts, (block == offset + h).astype(BF16))

    def evaluate(i, kern_ref):
        for n in range(width):
            j = i * width + n
            start = pl.multiple_of(j * 2 * size, 2 * size)
            kern = kern_of(dot_0(target_ref[:, pl.ds(start, 2 * size)], source_ref[:, pl.ds(start, reach)]))
            for h in range(2):
                weight = jnp.broadcast_to(weight_ref[h, pl.ds(2 * j + h, 1), :], (2 * ROWS, reach)).astype(BF16)
                for s in range(h * size, (h + 1) * size, 2 * ROWS):
                    kern_ref[n, s : s + 2 * ROWS, :] = kern[s : s + 2 * ROWS, :] * weight

    def apply(i, kern_ref):
        for n in range(width):
            start = pl.multiple_of((i * width + n) * 2 * size, 2 * size)
            out_ref[:, pl.ds(start, 2 * size)] = dot_t(wide_ref[:, pl.ds(start, reach)], kern_ref[n])

    width = kern_a_ref.shape[0]
    rounds = leaves // 2 // width
    evaluate(0, kern_a_ref)

    def step(t, carry):
        evaluate(2 * t + 1, kern_b_ref)
        apply(2 * t, kern_a_ref)
        evaluate(jnp.minimum(2 * t + 2, rounds - 1), kern_a_ref)
        apply(2 * t + 1, kern_b_ref)
        return carry

    lax.fori_loop(0, rounds // 2, step, 0)


def put_pair(ref, slot, tile, row=0):
    low = low_half(tile.shape)
    other = swap(tile)
    ref[slot, row : row + tile.shape[0], :] = pair(low, tile, other)
    ref[slot + 1, row : row + tile.shape[0], :] = pair(low, other, tile)


def part_of(parts, s, members):
    length = parts[0].shape[0] // 2
    owner = lax.axis_index("dev") ^ (s // 2 + s % 2 * (members // 2))
    return parts[s // 2].at[s % 2 * length : (s % 2 + 1) * length], owner


def top_kernel(*refs, members):
    _, pgroup_ref, *parts, out_ref = refs
    rhs = out_ref.shape[0] - ROWS
    rank2 = out_ref.shape[1]
    m_group = jnp.zeros((rhs, rank2), F32)
    for s in range(members):
        part, _ = part_of(parts, s, members)
        base = part.shape[0] - rhs - ROWS
        m_group = m_group + part[base : base + rhs, :].astype(F32)
    out_ref[:rhs, :] = twice(m_group[:, rank2 // 2 :]).astype(BF16)
    rows = source_rows(*[twice(pgroup_ref[c : c + 1, :].astype(F32)) for c in range(3)])
    out_ref[rhs:, :] = stack_rows(rows).astype(BF16)


def group_kernel(*refs, members):
    far_ref, _ = refs[:2]
    count = members // 2
    parts = refs[2 : 2 + count]
    fb_ref, ld_ref = refs[2 + count : 4 + count]
    moment_ref, source_ref, dev_m_ref, dev_source_ref = refs[4 + count :]
    branches, entries = far_ref.shape
    rhs, rank2 = moment_ref.shape[1:]
    rank = rank2 // 2
    me = lax.axis_index("dev")
    low = low_half((rhs, rank2))
    tail = source_tail(rank2)
    first = branches // 2 * rhs
    base = first + branches // 2 * ROWS
    for s in range(members):
        part, owner = part_of(parts, s, members)
        for q in range(branches // 2):
            put_pair(moment_ref, owner * branches + 2 * q, part[q * rhs : (q + 1) * rhs, :])
            put_pair(source_ref, owner * branches + 2 * q, part[first + q * ROWS : first + (q + 1) * ROWS, :])
        mixed = part[base : base + rhs, :].astype(F32)
        keep = (jnp.abs(owner - me) >= 2).astype(F32)
        dev_m_ref[owner] = (pair(low, mixed, pltpu.roll(mixed, rank, 1)) * keep).astype(BF16)
        dev_source_ref[owner] = part[base + rhs :, :]
    for c in range(branches):
        target = target_of(source_ref[me * branches + c][:, :rank])
        fb_ref[c] = interact(target, [far_ref[c, e] for e in range(entries)], source_ref, tail, moment_ref)
    target = target_of(dev_source_ref[me][:, :rank])
    ld_ref[...] = interact(target, list(range(members)), dev_source_ref, tail, dev_m_ref)


def downward_kernel(*refs, groups):
    far_ref = refs[0]
    tiles = refs[1 : 1 + groups]
    (
        fb_ref, ld_ref, down_device_ref, down_branch_ref, down_ref, own_ref, own_m_ref, recv_ref, basis_ref, near_ref,
        out_ref, table_ref, grp_m_ref, grp_source_ref, branch_ref, parent_ref, *buffers,
    ) = refs[1 + groups :]
    leaves, entries = far_ref.shape
    rhs, rank2 = parent_ref.shape[1:]
    rank = rank2 // 2
    half = rank // 2
    branches = leaves // FAN
    devices = recv_ref.shape[0]
    slots = (table_ref.shape[0] - leaves) // devices
    me = lax.axis_index("grp")
    low = low_half((rhs, rank2))
    tail = source_tail(rank2)

    for s, tile_ref in enumerate(tiles):
        owner = me ^ s
        keep = (jnp.abs(owner - me) >= 2).astype(F32)
        grp_m_ref[owner] = (tile_ref[:rhs, :].astype(F32) * keep).astype(BF16)
        grp_source_ref[owner] = tile_ref[rhs:, :]
    target = target_of(tiles[0][rhs:, :rank])
    l_group = interact(target, list(range(groups)), grp_source_ref, tail, grp_m_ref).astype(BF16)
    l_device = (ld_ref[...] + dot_t(l_group, down_device_ref[...])).astype(BF16)
    branch_ref[...] = twice(down_branch_ref[...].astype(F32).reshape(rank * branches, rank))
    for c in range(branches):
        matrix = branch_ref[pl.ds(c, rank, stride=branches), :][:, :rank].astype(BF16)
        parent_ref[c] = twice((fb_ref[c] + dot_t(l_device, matrix)).astype(BF16))

    table_ref[:leaves, :rhs, :] = own_m_ref[...]
    table_ref[:leaves, rhs:, :] = own_ref[...]
    base = slots // 2 * rhs

    def unpack(p, carry):
        for q in range(slots // 2):
            slot = leaves + p * slots + 2 * q
            put_pair(table_ref, slot, recv_ref[p, q * rhs : (q + 1) * rhs, :], 0)
            put_pair(table_ref, slot, recv_ref[p, base + q * ROWS : base + (q + 1) * ROWS, :], rhs)
        return carry

    lax.fori_loop(0, devices, unpack, 0, unroll=4)
    low_d = low_half((half, rank2))

    width = buffers[0].shape[0]
    rounds = leaves // width
    low_s = low_half((ROWS, rank2))

    def gather(b, low, rows, ref):
        for e in range(0, entries, 2):
            first, second = far_ref[b, e], far_ref[b, e + 1]
            ref[:, e * rank : (e + 2) * rank] = pair(low, table_ref[first, rows, :], table_ref[second, rows, :])

    def collect_sources(i, targets_ref, sources_ref):
        for h in range(width):
            b = width * i + h
            targets_ref[h] = jnp.transpose(target_of(table_ref[b, rhs:, :rank]))
            gather(b, low_s, slice(rhs, None), sources_ref.at[h])

    def collect_moments(i, moments_ref):
        for h in range(width):
            gather(width * i + h, low, slice(None, rhs), moments_ref.at[h])

    def evaluate(targets_ref, sources_ref, kern_ref):
        for h in range(width):
            sources = jnp.concatenate([sources_ref[h], source_tail(sources_ref.shape[2])], axis=0)
            kern_ref[h] = kern_of(dot(targets_ref[h], sources))

    def apply(i, moments_ref, kern_ref):
        sums = []
        for h in range(width):
            b = width * i + h
            far = dot_t(moments_ref[h], kern_ref[h])
            rows = down_ref[pl.ds(pl.multiple_of(b * half, half), half), :]
            sums.append((far + dot_t(parent_ref[b // FAN], spread_rows(rows, low_d))).astype(BF16))
        return tuple(sums)

    def finish(i, sums):
        for h in range(0, width, 2):
            columns = pl.ds(pl.multiple_of((width * i + h) * rank, rank2), rank2)
            product = dot(jnp.concatenate(sums[h : h + 2], axis=0), basis_ref[:, columns])
            out_ref[:, columns] = near_ref[:, columns] + pair(low, product[:rhs], product[rhs:])

    def stage(i, sums, this, other):
        finish(jnp.maximum(i - 2, 0), sums)
        evaluate(this[0], this[1], this[3])
        sums = apply(jnp.maximum(i - 1, 0), other[2], other[3])
        collect_sources(jnp.minimum(i + 2, rounds - 1), this[0], this[1])
        collect_moments(jnp.minimum(i + 1, rounds - 1), other[2])
        return sums

    even, odd = buffers[:4], buffers[4:]
    collect_sources(0, *even[:2])
    collect_sources(1, *odd[:2])
    collect_moments(0, even[2])
    odd[2][...] = jnp.zeros_like(odd[2])
    odd[3][...] = jnp.zeros_like(odd[3])

    def step(t, sums):
        return stage(2 * t + 1, stage(2 * t, sums, even, odd), odd, even)

    sums = lax.fori_loop(0, rounds // 2, step, (jnp.zeros((rhs, rank), BF16),) * width)
    finish(rounds - 2, sums)
    finish(rounds - 1, apply(rounds - 1, odd[2], odd[3]))


VMEM = functools.partial(pl.BlockSpec, memory_space=pltpu.VMEM)
SMEM = functools.partial(pl.BlockSpec, memory_space=pltpu.SMEM)
ANY = functools.partial(pl.BlockSpec, memory_space=pl.ANY)
PARAMS = pltpu.CompilerParams()


def hbm(shape, dtype):
    return jax.ShapeDtypeStruct(shape, dtype)


def vmem(*arrays):
    return [pltpu.with_memory_space_constraint(a, pltpu.VMEM) if a.size <= 1 << 19 else a for a in arrays]


def on_device(
    charges, points, basis, up_leaf, up_branch, up_device, down_leaf, down_branch, down_device,
    proxy_leaf, proxy_branch, proxy_device, proxy_group, far_leaf, send_leaf, far_branch, near_leaf,
):
    rhs, total = charges.shape
    rank = basis.shape[0]
    leaves = up_leaf.shape[2]
    size = total // leaves
    branches = leaves // FAN
    slots = send_leaf.shape[0]
    groups = lax.axis_size("grp")
    members = lax.axis_size("dev")
    devices = groups * members
    rank2 = 2 * rank
    half = rank // 2
    halo = REACH * size
    assert rank == size and slots % 2 == 0 and branches % 2 == 0 and members % 2 == 0

    moments, own, listed, inner, outer = pl.pallas_call(
        listed_kernel,
        out_shape=(
            pltpu.VMEM((leaves, rhs, rank2), BF16),
            hbm((leaves, ROWS, rank2), BF16),
            hbm((devices, slots // 2 * (rhs + ROWS), rank2), BF16),
            pltpu.VMEM((halo // rank2 * (rhs + ROWS), rank2), BF16),
            pltpu.VMEM((halo // rank2 * (rhs + ROWS), rank2), BF16),
        ),
        in_specs=[SMEM()] + [VMEM()] * 4,
        out_specs=(VMEM(),) * 5,
        scratch_shapes=[pltpu.VMEM((leaves * ROWS, rank2), F32)],
        compiler_params=PARAMS,
        name="listed",
    )(send_leaf, charges, points, basis, proxy_leaf)
    (moments,) = vmem(moments)
    received = lax.all_to_all(listed, ("grp", "dev"), split_axis=0, concat_axis=0, tiled=True)

    swaps = [(i, i + 1 if i % 2 else i - 1) for i in range(1, devices - 1)]
    outer = lax.ppermute(outer, ("grp", "dev"), swaps)
    inner = lax.ppermute(inner, "dev", [(i, i ^ 1) for i in range(members)])

    shared = pl.pallas_call(
        upward_kernel,
        out_shape=hbm(((branches // 2 + 1) * (rhs + ROWS), rank2), BF16),
        in_specs=[VMEM()] * 6,
        out_specs=VMEM(),
        scratch_shapes=[pltpu.VMEM((leaves * half, rank2), F32), pltpu.VMEM((rank * branches, rank2), F32)],
        compiler_params=PARAMS,
        name="upward",
    )(
        moments,
        up_leaf,
        jnp.transpose(up_branch, (0, 2, 1)),
        up_device[:, :, 0],
        jnp.transpose(proxy_branch, (0, 2, 1)),
        proxy_device[:, :, 0],
    )
    partner = lax.ppermute(shared, "dev", [(i, i ^ members // 2) for i in range(members)])
    down, far_turned = pl.pallas_call(
        turn_kernel,
        out_shape=(pltpu.VMEM((leaves * half, rank2), BF16), hbm(far_leaf.shape[::-1], jnp.int32)),
        in_specs=[VMEM(), VMEM(), ANY()],
        out_specs=(VMEM(), VMEM()),
        scratch_shapes=[pltpu.VMEM((leaves * half, rank2), F32)],
        compiler_params=PARAMS,
        name="turn",
    )(down_leaf, far_leaf, shared)
    partner, down = lax.optimization_barrier((partner, down))
    both = jnp.concatenate([shared, partner], axis=0)
    parts = [both] + [
        lax.ppermute(both, "dev", [(i, i ^ s) for i in range(members)]) for s in range(1, members // 2)
    ]

    reach = (2 * REACH + 2) * size
    near = pl.pallas_call(
        near_kernel,
        out_shape=pltpu.VMEM((rhs, total), F32),
        in_specs=[VMEM()] * 6,
        out_specs=VMEM(),
        scratch_shapes=[
            pltpu.VMEM((rhs, total + 2 * halo), BF16),
            pltpu.VMEM((2 * ROWS, total + 2 * halo), BF16),
            pltpu.VMEM((2 * ROWS, total), BF16),
            pltpu.VMEM((2, leaves, reach), F32),
            pltpu.VMEM((PAIRS, 2 * size, reach), BF16),
            pltpu.VMEM((PAIRS, 2 * size, reach), BF16),
        ],
        compiler_params=PARAMS,
        name="near",
    )(near_leaf, charges, points, *vmem(inner, outer, both))

    parts = vmem(*parts)
    tile = pl.pallas_call(
        functools.partial(top_kernel, members=members),
        out_shape=hbm((rhs + ROWS, rank2), BF16),
        in_specs=[VMEM()] * (2 + len(parts)),
        out_specs=VMEM(),
        compiler_params=PARAMS,
        name="top",
    )(*vmem(near), proxy_group[:, :, 0], *parts)
    assert groups & (groups - 1) == 0 and members & (members - 1) == 0
    tiles = [tile] + [lax.ppermute(tile, "grp", [(i, i ^ s) for i in range(groups)]) for s in range(1, groups)]
    far_b, part_d = pl.pallas_call(
        functools.partial(group_kernel, members=members),
        out_shape=(hbm((branches, rhs, rank), F32), hbm((rhs, rank), F32)),
        in_specs=[SMEM(), ANY()] + [VMEM()] * len(parts),
        out_specs=(VMEM(), VMEM()),
        scratch_shapes=[
            pltpu.VMEM((members * branches, rhs, rank2), BF16),
            pltpu.VMEM((members * branches, ROWS, rank2), BF16),
            pltpu.VMEM((members, rhs, rank2), BF16),
            pltpu.VMEM((members, ROWS, rank2), BF16),
        ],
        compiler_params=PARAMS,
        name="group",
    )(jnp.transpose(far_branch), tile, *parts)

    table = leaves + devices * slots
    return pl.pallas_call(
        functools.partial(downward_kernel, groups=groups),
        out_shape=hbm((rhs, total), F32),
        in_specs=[SMEM()] + [VMEM()] * (groups + 10),
        out_specs=VMEM(),
        scratch_shapes=[
            pltpu.VMEM((table, rhs + ROWS, rank2), BF16),
            pltpu.VMEM((groups, rhs, rank2), BF16),
            pltpu.VMEM((groups, ROWS, rank2), BF16),
            pltpu.VMEM((rank * branches, rank2), F32),
            pltpu.VMEM((branches, rhs, rank2), BF16),
        ]
        + [
            pltpu.VMEM((ROUND, rank, 2 * ROWS), BF16),
            pltpu.VMEM((ROUND, ROWS, far_leaf.shape[0] * rank), BF16),
            pltpu.VMEM((ROUND, rhs, far_leaf.shape[0] * rank), BF16),
            pltpu.VMEM((ROUND, rank, far_leaf.shape[0] * rank), BF16),
        ]
        * 2,
        compiler_params=PARAMS,
        name="downward",
    )(
        far_turned,
        tile,
        *vmem(*tiles[1:]),
        far_b,
        part_d,
        down_device[:, :, 0],
        jnp.transpose(down_branch, (0, 2, 1)),
        *vmem(down),
        own,
        moments,
        *vmem(received),
        basis,
        *vmem(near),
    )


def solution(mesh):
    points = P(None, ("grp", "dev"))
    blocks = P(None, None, ("grp", "dev"))
    placed = (points,) * 3 + (blocks,) * 9 + (P(None, None, "grp"),) + (points,) * 4

    return jax.shard_map(on_device, mesh=mesh, in_specs=placed, out_specs=points, check_vma=False)
```

```python
import functools
import math

import jax
import jax.numpy as jnp
from jax import lax
from jax.experimental import pallas as pl
from jax.experimental.pallas import tpu as pltpu
from jax.sharding import PartitionSpec as P

REACH = 4
FAN = 8
ROUND = 8
PAIRS = 2

INV_FOUR_PI = 1.0 / (4.0 * math.pi)
SOFTEN = 0.25
ROWS = 8

BF16 = jnp.bfloat16
F32 = jnp.float32


def dot(a, b):
    return jnp.dot(a, b, preferred_element_type=F32)


def dot_t(a, b):
    return lax.dot_general(a, b, (((1,), (1,)), ((), ())), preferred_element_type=F32)


def dot_0(a, b):
    return lax.dot_general(a, b, (((0,), (0,)), ((), ())), preferred_element_type=F32)


def fetch(source, target, sem):
    copy = pltpu.make_async_copy(source, target, sem)
    copy.start()
    return copy


def low_half(shape):
    width = shape[-1]
    return lax.broadcasted_iota(jnp.int32, shape, len(shape) - 1) < width // 2


def pair(low, first, second):
    return jnp.where(low, first, second)


def swap(tile):
    half = tile.shape[-1] // 2
    return jnp.concatenate([tile[..., half:], tile[..., :half]], axis=-1)


def twice(tile):
    return jnp.concatenate([tile, tile], axis=-1)


def three(value):
    first = value.astype(BF16).astype(F32)
    rest = value - first
    second = rest.astype(BF16).astype(F32)
    return first, second, rest - second


def source_rows(x, y, z):
    return (-2.0 * x, -2.0 * y, -2.0 * z) + three(x * x + y * y + z * z)


def row_mask(shape, rows):
    row = lax.broadcasted_iota(jnp.int32, shape, 0)
    found = row == rows[0]
    for r in rows[1:]:
        found = found | (row == r)
    return found.astype(F32)


def source_tail(width):
    return row_mask((ROWS, width), (3, 4, 5, 6)).astype(BF16)


def target_of(rows):
    rows = rows.astype(F32)
    shape = rows.shape
    squares = row_mask(shape, (3, 4, 5))
    upper = rows * (-0.5 * row_mask(shape, (0, 1, 2))) + squares
    lower = rows * squares + SOFTEN * row_mask(shape, (6,))
    return jnp.concatenate([upper, lower], axis=0).astype(BF16)


def put_rows(ref, rows, count):
    for f in range(ROWS):
        value = rows[f] if f < len(rows) else jnp.zeros_like(rows[0])
        ref[pl.ds(f, count, stride=ROWS), :] = value


def stack_rows(rows):
    n = rows[0].shape[1]
    return jnp.concatenate(tuple(rows) + (jnp.zeros((ROWS - len(rows), n), F32),), axis=0)


def couplings(target, slots, source_ref, tail):
    low = low_half(source_ref.shape[1:])
    tiles = [
        jnp.concatenate([pair(low, source_ref[first], source_ref[second]), tail], axis=0)
        for first, second in zip(slots[0::2], slots[1::2])
    ]
    return kern_of(dot_0(target, jnp.concatenate(tiles, axis=1)))


def kern_of(square):
    return (INV_FOUR_PI * lax.rsqrt(square)).astype(BF16)


def gathered(slots, moment_ref):
    low = low_half(moment_ref.shape[1:])
    tiles = [pair(low, moment_ref[first], moment_ref[second]) for first, second in zip(slots[0::2], slots[1::2])]
    return jnp.concatenate(tiles, axis=1)


def interact(target, slots, source_ref, tail, moment_ref):
    return dot_t(gathered(slots, moment_ref), couplings(target, slots, source_ref, tail))


def upward_kernel(
    send_ref, charges_ref, points_ref, basis_ref, proxy_ref, up_leaf_hbm, up_branch_ref, up_device_ref, pbranch_ref,
    pdevice_ref, moment_ref, own_ref, out_ref, inner_ref, outer_ref, shared_ref, tile_ref, up_leaf_ref, scratch_ref,
    branch_ref, sem,
):
    slots, devices = send_ref.shape
    leaves, rhs, rank2 = moment_ref.shape
    transfers = fetch(up_leaf_hbm, up_leaf_ref, sem)
    low = low_half((rhs, rank2))
    put_rows(tile_ref, source_rows(*[twice(jnp.transpose(proxy_ref[c].astype(F32))) for c in range(3)]), leaves)
    own_ref[...] = tile_ref[...].astype(BF16).reshape(own_ref.shape)

    def leaf_pair(i, carry):
        columns = pl.ds(pl.multiple_of(i * rank2, rank2), rank2)
        q = charges_ref[:, columns]
        u = basis_ref[:, columns]
        zero = jnp.zeros_like(q)
        stacked = jnp.concatenate([jnp.where(low, q, zero), jnp.where(low, zero, q)], axis=0)
        product = dot_t(stacked, jnp.concatenate([u, u], axis=0)).astype(BF16)
        moment_ref[2 * i] = product[:rhs]
        moment_ref[2 * i + 1] = product[rhs:]
        return carry

    lax.fori_loop(0, leaves // 2, leaf_pair, 0, unroll=8)
    low8 = low_half((ROWS, rank2))
    base = slots // 2 * rhs

    def pack(p, carry):
        s = [send_ref[t, p] for t in range(slots)]
        for q in range(slots // 2):
            first, second = s[2 * q], s[2 * q + 1]
            out_ref[p, q * rhs : (q + 1) * rhs, :] = pair(low, moment_ref[first], moment_ref[second])
            out_ref[p, base + q * ROWS : base + (q + 1) * ROWS, :] = pair(low8, own_ref[first], own_ref[second])
        return carry

    lax.fori_loop(0, devices, pack, 0, unroll=4)
    total = charges_ref.shape[1]
    halo = inner_ref.shape[0] // (rhs + ROWS) * rank2
    odd = lax.rem(lax.axis_index("dev"), 2) == 1
    for ref, first in ((inner_ref, odd), (outer_ref, jnp.logical_not(odd))):
        start = jnp.where(first, 0, total - halo)
        for n in range(halo // rank2):
            columns = pl.ds(pl.multiple_of(start + n * rank2, rank2), rank2)
            base = n * (rhs + ROWS)
            ref[base : base + rhs, :] = charges_ref[:, columns]
            points = points_ref[:, columns].astype(F32)
            rows = jnp.concatenate([points, jnp.zeros((ROWS - 3, rank2), F32)], axis=0)
            ref[base + rhs : base + rhs + ROWS, :] = rows.astype(BF16)
    transfers.wait()
    raise_moments(
        moment_ref, up_leaf_ref, up_branch_ref, up_device_ref, pbranch_ref, pdevice_ref, shared_ref, scratch_ref, branch_ref
    )


def relayout(x_ref, scratch_ref):
    rank, _, leaves = x_ref.shape
    half = rank // 2
    eye = (
        lax.broadcasted_iota(jnp.int32, (leaves, leaves), 0)
        == lax.broadcasted_iota(jnp.int32, (leaves, leaves), 1)
    ).astype(BF16)
    for k in range(0, half, 2):
        block = jnp.concatenate(
            [x_ref[k], x_ref[k + half], x_ref[k + 1], x_ref[k + 1 + half]], axis=0
        )
        turned = dot_t(eye, block)
        for n in range(2):
            scratch_ref[pl.ds(k + n, leaves, stride=half), :] = turned[:, n * 2 * rank : (n + 1) * 2 * rank]


def spread_rows(block, low):
    zero = jnp.zeros_like(block)
    return jnp.concatenate([jnp.where(low, block, zero), jnp.where(low, zero, block)], axis=0)


def raise_moments(
    moment_ref, up_leaf_ref, up_branch_ref, up_device_ref, pbranch_ref, pdevice_ref, out_ref, scratch_ref, branch_ref
):
    leaves, rhs, rank2 = moment_ref.shape
    rank = rank2 // 2
    half = rank // 2
    branches = leaves // FAN
    relayout(up_leaf_ref, scratch_ref)
    low = low_half((half, rank2))
    low_m = low_half((rhs, rank2))
    low_r = low_half((ROWS, rank2))
    wide = up_branch_ref[...].astype(F32).reshape(rank * branches, rank)
    branch_ref[...] = twice(wide)
    rows = source_rows(*[twice(pbranch_ref[c].astype(F32)) for c in range(3)])
    m_device = jnp.zeros((rhs, rank), F32)
    previous = None
    base = branches // 2 * rhs
    for c in range(branches):
        blocks, moments = [], []
        for b in range(c * FAN, (c + 1) * FAN):
            block = scratch_ref[b * half : (b + 1) * half, :].astype(BF16)
            blocks.append(spread_rows(block, low))
            moments.append(moment_ref[b])
        m_branch = dot_t(jnp.concatenate(moments, axis=1), jnp.concatenate(blocks, axis=1)).astype(BF16)
        matrix = branch_ref[pl.ds(c, rank, stride=branches), :][:, :rank].astype(BF16)
        m_device = m_device + dot_t(m_branch, matrix)
        spread = twice(m_branch)
        source = stack_rows([r[c : c + 1, :] for r in rows]).astype(BF16)
        if c % 2 == 1:
            q = c // 2
            out_ref[q * rhs : (q + 1) * rhs, :] = pair(low_m, previous[0], spread)
            out_ref[base + q * ROWS : base + (q + 1) * ROWS, :] = pair(low_r, previous[1], source)
        previous = spread, source
    base = base + branches // 2 * ROWS
    m_device = m_device.astype(BF16)
    share = dot_t(m_device, up_device_ref[...]).astype(BF16)
    out_ref[base : base + rhs, :] = jnp.concatenate([m_device, share], axis=1)
    rows = source_rows(*[twice(pdevice_ref[c : c + 1, :].astype(F32)) for c in range(3)])
    out_ref[base + rhs :, :] = stack_rows(rows).astype(BF16)


def turn_kernel(down_leaf_ref, far_ref, _, down_ref, turned_ref, scratch_ref):
    turned_ref[...] = jnp.transpose(far_ref[...].astype(F32)).astype(jnp.int32)
    relayout(down_leaf_ref, scratch_ref)
    down_ref[...] = scratch_ref[...].astype(BF16)


def point_rows(points):
    return stack_rows(source_rows(*[points[c : c + 1, :] for c in range(3)]))


def near_weights(near_ref, size, weight_ref):
    near = near_ref[...]
    leaves = near.shape[1]
    reach = weight_ref.shape[2]
    span = 2 * REACH + 1
    counts = [jnp.sum((near == o - REACH).astype(F32), axis=0, keepdims=True) for o in range(span)]
    counts = jnp.concatenate(counts + [jnp.zeros((2 * ROWS - span, leaves), F32)], axis=0).astype(BF16)
    offset = lax.broadcasted_iota(jnp.int32, (2 * ROWS, reach), 0)
    block = lax.broadcasted_iota(jnp.int32, (2 * ROWS, reach), 1) // size
    for h in range(2):
        weight_ref[h] = dot_0(counts, (block == offset + h).astype(BF16))


def near_couplings(target, source, weights, kern_ref):
    kern = kern_of(dot_0(target, source))
    size, reach = kern.shape[0] // 2, kern.shape[1]
    for h in range(2):
        weight = jnp.broadcast_to(weights[h], (2 * ROWS, reach)).astype(BF16)
        for s in range(h * size, (h + 1) * size, 2 * ROWS):
            kern_ref[s : s + 2 * ROWS, :] = kern[s : s + 2 * ROWS, :] * weight


def near_kernel(
    near_ref, charges_ref, points_ref, _, out_ref, source_ref, target_ref, weight_ref, kern_a_ref, kern_b_ref
):
    rhs, total = charges_ref.shape
    size = total // near_ref.shape[1]
    halo = REACH * size
    lanes = 2 * size
    reach = weight_ref.shape[2]
    rows = point_rows(points_ref[...].astype(F32))
    source_ref[...] = jnp.concatenate([rows.astype(BF16), source_tail(total)], axis=0)
    target_ref[...] = target_of(rows)
    near_weights(near_ref, size, weight_ref)
    out_ref[:, :halo] = jnp.zeros((rhs, halo), F32)
    out_ref[:, total - halo :] = jnp.zeros((rhs, halo), F32)
    width = kern_a_ref.shape[0]
    first = halo // lanes
    rounds = (total - 2 * halo) // lanes // width

    def evaluate(i, kern_ref):
        for n in range(width):
            j = first + i * width + n
            start = pl.multiple_of(j * lanes, lanes)
            near_couplings(
                target_ref[:, pl.ds(start, lanes)],
                source_ref[:, pl.ds(pl.multiple_of(start - halo, lanes), reach)],
                [weight_ref[h, pl.ds(2 * j + h, 1), :] for h in range(2)],
                kern_ref.at[n],
            )

    def apply(i, kern_ref):
        for n in range(width):
            start = pl.multiple_of((first + i * width + n) * lanes, lanes)
            columns = pl.ds(pl.multiple_of(start - halo, lanes), reach)
            out_ref[:, pl.ds(start, lanes)] = dot_t(charges_ref[:, columns], kern_ref[n])

    evaluate(0, kern_a_ref)

    def step(t, carry):
        evaluate(2 * t + 1, kern_b_ref)
        apply(2 * t, kern_a_ref)
        evaluate(jnp.minimum(2 * t + 2, rounds - 1), kern_a_ref)
        apply(2 * t + 1, kern_b_ref)
        return carry

    lax.fori_loop(0, rounds // 2, step, 0)


def edge_pairs(near_ref, ends_ref, end_points_ref, inner_ref, outer_ref, out_ref, weight_ref, kern_ref):
    rhs = ends_ref.shape[1]
    leaves = near_ref.shape[1]
    halo = out_ref.shape[1] // 2
    lanes = inner_ref.shape[1]
    size = lanes // 2
    count = halo // lanes
    reach = weight_ref.shape[2]
    odd = lax.rem(lax.axis_index("dev"), 2) == 1
    near_weights(near_ref, size, weight_ref)
    inner, outer = inner_ref[...], outer_ref[...]
    height = inner.shape[0] // count
    for side, block in enumerate((jnp.where(odd, inner, outer), jnp.where(odd, outer, inner))):
        beyond = jnp.concatenate([block[n * height : (n + 1) * height, :] for n in range(count)], axis=1)
        parts = [(beyond[:rhs, :], beyond[rhs : rhs + 3, :].astype(F32)), (ends_ref[side], end_points_ref[side].astype(F32))]
        parts = parts if side == 0 else parts[::-1]
        wide = jnp.concatenate([p[0] for p in parts], axis=1)
        rows = point_rows(jnp.concatenate([p[1] for p in parts], axis=1))
        source = jnp.concatenate([rows.astype(BF16), source_tail(rows.shape[1])], axis=0)
        target = target_of(rows[:, halo : 2 * halo])
        for j in range(count):
            leaf = 2 * j + side * (leaves - 2 * count)
            place = side * count + j
            near_couplings(
                target[:, j * lanes : (j + 1) * lanes],
                source[:, j * lanes : j * lanes + reach],
                [weight_ref[h, leaf + h : leaf + h + 1, :] for h in range(2)],
                kern_ref.at[place],
            )
            columns = slice(place * lanes, (place + 1) * lanes)
            out_ref[:, columns] = dot_t(wide[:, j * lanes : j * lanes + reach], kern_ref[place])


def put_pair(ref, slot, tile, row=0):
    low = low_half(tile.shape)
    other = swap(tile)
    ref[slot, row : row + tile.shape[0], :] = pair(low, tile, other)
    ref[slot + 1, row : row + tile.shape[0], :] = pair(low, other, tile)


def part_of(parts, s, members):
    length = parts[0].shape[0] // 2
    owner = lax.axis_index("dev") ^ (s // 2 + s % 2 * (members // 2))
    return parts[s // 2].at[s % 2 * length : (s % 2 + 1) * length], owner


def top_kernel(*refs, members):
    _, pgroup_ref, *parts, out_ref = refs
    rhs = out_ref.shape[0] - ROWS
    rank2 = out_ref.shape[1]
    m_group = jnp.zeros((rhs, rank2), F32)
    for s in range(members):
        part, _ = part_of(parts, s, members)
        base = part.shape[0] - rhs - ROWS
        m_group = m_group + part[base : base + rhs, :].astype(F32)
    out_ref[:rhs, :] = twice(m_group[:, rank2 // 2 :]).astype(BF16)
    rows = source_rows(*[twice(pgroup_ref[c : c + 1, :].astype(F32)) for c in range(3)])
    out_ref[rhs:, :] = stack_rows(rows).astype(BF16)


def group_kernel(*refs, members):
    far_ref, near_ref, charges_hbm, points_hbm, inner_ref, outer_ref, _ = refs[:7]
    count = members // 2
    parts = refs[7 : 7 + count]
    fb_ref, ld_ref, edge_ref = refs[7 + count : 10 + count]
    (
        moment_ref, source_ref, dev_m_ref, dev_source_ref, ends_ref, end_points_ref, weight_ref, kern_ref, sems,
    ) = refs[10 + count :]
    total, width = charges_hbm.shape[1], ends_ref.shape[2]
    copies = []
    for side in range(2):
        columns = slice(side * (total - width), side * (total - width) + width)
        copies.append(fetch(charges_hbm.at[:, columns], ends_ref.at[side], sems.at[2 * side]))
        copies.append(fetch(points_hbm.at[:, columns], end_points_ref.at[side], sems.at[2 * side + 1]))
    branches, entries = far_ref.shape
    rhs, rank2 = moment_ref.shape[1:]
    rank = rank2 // 2
    me = lax.axis_index("dev")
    low = low_half((rhs, rank2))
    tail = source_tail(rank2)
    first = branches // 2 * rhs
    base = first + branches // 2 * ROWS
    for s in range(members):
        part, owner = part_of(parts, s, members)
        for q in range(branches // 2):
            put_pair(moment_ref, owner * branches + 2 * q, part[q * rhs : (q + 1) * rhs, :])
            put_pair(source_ref, owner * branches + 2 * q, part[first + q * ROWS : first + (q + 1) * ROWS, :])
        mixed = part[base : base + rhs, :].astype(F32)
        keep = (jnp.abs(owner - me) >= 2).astype(F32)
        dev_m_ref[owner] = (pair(low, mixed, pltpu.roll(mixed, rank, 1)) * keep).astype(BF16)
        dev_source_ref[owner] = part[base + rhs :, :]
    for c in range(branches):
        target = target_of(source_ref[me * branches + c][:, :rank])
        fb_ref[c] = interact(target, [far_ref[c, e] for e in range(entries)], source_ref, tail, moment_ref)
    target = target_of(dev_source_ref[me][:, :rank])
    ld_ref[...] = interact(target, list(range(members)), dev_source_ref, tail, dev_m_ref)
    for copy in copies:
        copy.wait()
    edge_pairs(near_ref, ends_ref, end_points_ref, inner_ref, outer_ref, edge_ref, weight_ref, kern_ref)


def downward_kernel(*refs, groups):
    far_ref = refs[0]
    tiles = refs[1 : 1 + groups]
    (
        fb_ref, ld_ref, down_device_ref, down_branch_ref, down_ref, own_ref, own_m_ref, recv_ref, basis_ref, near_ref, edge_ref,
        out_ref, table_ref, grp_m_ref, grp_source_ref, branch_ref, parent_ref, *buffers,
    ) = refs[1 + groups :]
    leaves, entries = far_ref.shape
    rhs, rank2 = parent_ref.shape[1:]
    rank = rank2 // 2
    half = rank // 2
    branches = leaves // FAN
    devices = recv_ref.shape[0]
    slots = (table_ref.shape[0] - leaves) // devices
    me = lax.axis_index("grp")
    low = low_half((rhs, rank2))
    tail = source_tail(rank2)

    for s, tile_ref in enumerate(tiles):
        owner = me ^ s
        keep = (jnp.abs(owner - me) >= 2).astype(F32)
        grp_m_ref[owner] = (tile_ref[:rhs, :].astype(F32) * keep).astype(BF16)
        grp_source_ref[owner] = tile_ref[rhs:, :]
    target = target_of(tiles[0][rhs:, :rank])
    l_group = interact(target, list(range(groups)), grp_source_ref, tail, grp_m_ref).astype(BF16)
    l_device = (ld_ref[...] + dot_t(l_group, down_device_ref[...])).astype(BF16)
    branch_ref[...] = twice(down_branch_ref[...].astype(F32).reshape(rank * branches, rank))
    for c in range(branches):
        matrix = branch_ref[pl.ds(c, rank, stride=branches), :][:, :rank].astype(BF16)
        parent_ref[c] = twice((fb_ref[c] + dot_t(l_device, matrix)).astype(BF16))

    table_ref[:leaves, :rhs, :] = own_m_ref[...]
    table_ref[:leaves, rhs:, :] = own_ref[...]
    base = slots // 2 * rhs

    def unpack(p, carry):
        for q in range(slots // 2):
            slot = leaves + p * slots + 2 * q
            put_pair(table_ref, slot, recv_ref[p, q * rhs : (q + 1) * rhs, :], 0)
            put_pair(table_ref, slot, recv_ref[p, base + q * ROWS : base + (q + 1) * ROWS, :], rhs)
        return carry

    lax.fori_loop(0, devices, unpack, 0, unroll=min(devices, 32))
    low_d = low_half((half, rank2))

    width = buffers[0].shape[0]
    rounds = leaves // width
    low_s = low_half((ROWS, rank2))

    def gather(b, low, rows, ref):
        for e in range(0, entries, 2):
            first, second = far_ref[b, e], far_ref[b, e + 1]
            ref[:, e * rank : (e + 2) * rank] = pair(low, table_ref[first, rows, :], table_ref[second, rows, :])

    def collect_sources(i, targets_ref, sources_ref):
        for h in range(width):
            b = width * i + h
            targets_ref[h] = jnp.transpose(target_of(table_ref[b, rhs:, :rank]))
            gather(b, low_s, slice(rhs, None), sources_ref.at[h])

    def collect_moments(i, moments_ref):
        for h in range(width):
            gather(width * i + h, low, slice(None, rhs), moments_ref.at[h])

    def evaluate(targets_ref, sources_ref, kern_ref):
        for h in range(width):
            sources = jnp.concatenate([sources_ref[h], source_tail(sources_ref.shape[2])], axis=0)
            kern_ref[h] = kern_of(dot(targets_ref[h], sources))

    def apply(i, moments_ref, kern_ref):
        sums = []
        for h in range(width):
            b = width * i + h
            far = dot_t(moments_ref[h], kern_ref[h])
            rows = down_ref[pl.ds(pl.multiple_of(b * half, half), half), :]
            sums.append((far + dot_t(parent_ref[b // FAN], spread_rows(rows, low_d))).astype(BF16))
        return tuple(sums)

    def finish(i, sums):
        for h in range(0, width, 2):
            columns = pl.ds(pl.multiple_of((width * i + h) * rank, rank2), rank2)
            product = dot(jnp.concatenate(sums[h : h + 2], axis=0), basis_ref[:, columns])
            out_ref[:, columns] = near_ref[:, columns] + pair(low, product[:rhs], product[rhs:])

    def stage(i, sums, this, other):
        finish(jnp.maximum(i - 2, 0), sums)
        evaluate(this[0], this[1], this[3])
        sums = apply(jnp.maximum(i - 1, 0), other[2], other[3])
        collect_sources(jnp.minimum(i + 2, rounds - 1), this[0], this[1])
        collect_moments(jnp.minimum(i + 1, rounds - 1), other[2])
        return sums

    even, odd = buffers[:4], buffers[4:]
    collect_sources(0, *even[:2])
    collect_sources(1, *odd[:2])
    collect_moments(0, even[2])
    odd[2][...] = jnp.zeros_like(odd[2])
    odd[3][...] = jnp.zeros_like(odd[3])

    def step(t, sums):
        return stage(2 * t + 1, stage(2 * t, sums, even, odd), odd, even)

    sums = lax.fori_loop(0, rounds // 2, step, (jnp.zeros((rhs, rank), BF16),) * width)
    finish(rounds - 2, sums)
    finish(rounds - 1, apply(rounds - 1, odd[2], odd[3]))
    total, halo = out_ref.shape[1], edge_ref.shape[1] // 2
    out_ref[:, :halo] += edge_ref[:, :halo]
    out_ref[:, total - halo :] += edge_ref[:, halo:]


VMEM = functools.partial(pl.BlockSpec, memory_space=pltpu.VMEM)
SMEM = functools.partial(pl.BlockSpec, memory_space=pltpu.SMEM)
ANY = functools.partial(pl.BlockSpec, memory_space=pl.ANY)
PARAMS = pltpu.CompilerParams()


def hbm(shape, dtype):
    return jax.ShapeDtypeStruct(shape, dtype)


def vmem(*arrays):
    return [pltpu.with_memory_space_constraint(a, pltpu.VMEM) if a.size <= 1 << 19 else a for a in arrays]


def on_device(
    charges, points, basis, up_leaf, up_branch, up_device, down_leaf, down_branch, down_device,
    proxy_leaf, proxy_branch, proxy_device, proxy_group, far_leaf, send_leaf, far_branch, near_leaf,
):
    rhs, total = charges.shape
    rank = basis.shape[0]
    leaves = up_leaf.shape[2]
    size = total // leaves
    branches = leaves // FAN
    slots = send_leaf.shape[0]
    groups = lax.axis_size("grp")
    members = lax.axis_size("dev")
    devices = groups * members
    rank2 = 2 * rank
    half = rank // 2
    halo = REACH * size
    assert rank == size and slots % 2 == 0 and branches % 2 == 0 and members % 2 == 0

    moments, own, listed, inner, outer, shared = pl.pallas_call(
        upward_kernel,
        out_shape=(
            pltpu.VMEM((leaves, rhs, rank2), BF16),
            hbm((leaves, ROWS, rank2), BF16),
            hbm((devices, slots // 2 * (rhs + ROWS), rank2), BF16),
            pltpu.VMEM((halo // rank2 * (rhs + ROWS), rank2), BF16),
            pltpu.VMEM((halo // rank2 * (rhs + ROWS), rank2), BF16),
            hbm(((branches // 2 + 1) * (rhs + ROWS), rank2), BF16),
        ),
        in_specs=[SMEM()] + [VMEM()] * 4 + [ANY()] + [VMEM()] * 4,
        out_specs=(VMEM(),) * 6,
        scratch_shapes=[
            pltpu.VMEM((leaves * ROWS, rank2), F32),
            pltpu.VMEM(up_leaf.shape, BF16),
            pltpu.VMEM((leaves * half, rank2), F32),
            pltpu.VMEM((rank * branches, rank2), F32),
            pltpu.SemaphoreType.DMA(()),
        ],
        compiler_params=PARAMS,
        name="upward",
    )(
        send_leaf,
        charges,
        points,
        basis,
        proxy_leaf,
        up_leaf,
        jnp.transpose(up_branch, (0, 2, 1)),
        up_device[:, :, 0],
        jnp.transpose(proxy_branch, (0, 2, 1)),
        proxy_device[:, :, 0],
    )
    (moments,) = vmem(moments)
    received = lax.all_to_all(listed, ("grp", "dev"), split_axis=0, concat_axis=0, tiled=True)

    partner = lax.ppermute(shared, "dev", [(i, i ^ members // 2) for i in range(members)])
    down, far_turned = pl.pallas_call(
        turn_kernel,
        out_shape=(pltpu.VMEM((leaves * half, rank2), BF16), hbm(far_leaf.shape[::-1], jnp.int32)),
        in_specs=[VMEM(), VMEM(), ANY()],
        out_specs=(VMEM(), VMEM()),
        scratch_shapes=[pltpu.VMEM((leaves * half, rank2), F32)],
        compiler_params=PARAMS,
        name="turn",
    )(down_leaf, far_leaf, shared)
    partner, down = lax.optimization_barrier((partner, down))
    both = jnp.concatenate([shared, partner], axis=0)
    parts = [both]
    for s in range(1, members // 2):
        parts.append(lax.ppermute(both, "dev", [(i, i ^ s) for i in range(members)]))

    reach = (2 * REACH + 2) * size
    near = pl.pallas_call(
        near_kernel,
        out_shape=pltpu.VMEM((rhs, total), F32),
        in_specs=[VMEM()] * 4,
        out_specs=VMEM(),
        scratch_shapes=[
            pltpu.VMEM((2 * ROWS, total), BF16),
            pltpu.VMEM((2 * ROWS, total), BF16),
            pltpu.VMEM((2, leaves, reach), F32),
            pltpu.VMEM((PAIRS, 2 * size, reach), BF16),
            pltpu.VMEM((PAIRS, 2 * size, reach), BF16),
        ],
        compiler_params=PARAMS,
        name="near",
    )(near_leaf, charges, points, *vmem(both))

    swaps = [(i, i + 1 if i % 2 else i - 1) for i in range(1, devices - 1)]
    inner, outer, near = lax.optimization_barrier((inner, outer, near))
    outer = lax.ppermute(outer, ("grp", "dev"), swaps)
    inner = lax.ppermute(inner, "dev", [(i, i ^ 1) for i in range(members)])

    parts = vmem(*parts)
    tile = pl.pallas_call(
        functools.partial(top_kernel, members=members),
        out_shape=hbm((rhs + ROWS, rank2), BF16),
        in_specs=[VMEM()] * (2 + len(parts)),
        out_specs=VMEM(),
        compiler_params=PARAMS,
        name="top",
    )(*vmem(near), proxy_group[:, :, 0], *parts)
    assert groups & (groups - 1) == 0 and members & (members - 1) == 0
    tiles = [tile] + [lax.ppermute(tile, "grp", [(i, i ^ s) for i in range(groups)]) for s in range(1, groups)]
    far_b, part_d, edge = pl.pallas_call(
        functools.partial(group_kernel, members=members),
        out_shape=(hbm((branches, rhs, rank), F32), hbm((rhs, rank), F32), pltpu.VMEM((rhs, 2 * halo), F32)),
        in_specs=[SMEM(), VMEM(), ANY(), ANY(), VMEM(), VMEM(), ANY()] + [VMEM()] * len(parts),
        out_specs=(VMEM(),) * 3,
        scratch_shapes=[
            pltpu.VMEM((members * branches, rhs, rank2), BF16),
            pltpu.VMEM((members * branches, ROWS, rank2), BF16),
            pltpu.VMEM((members, rhs, rank2), BF16),
            pltpu.VMEM((members, ROWS, rank2), BF16),
            pltpu.VMEM((2, rhs, 2 * halo), BF16),
            pltpu.VMEM((2, 3, 2 * halo), BF16),
            pltpu.VMEM((2, leaves, reach), F32),
            pltpu.VMEM((REACH, 2 * size, reach), BF16),
            pltpu.SemaphoreType.DMA((4,)),
        ],
        compiler_params=PARAMS,
        name="group",
    )(jnp.transpose(far_branch), near_leaf, charges, points, *vmem(inner, outer), tile, *parts)

    table = leaves + devices * slots
    return pl.pallas_call(
        functools.partial(downward_kernel, groups=groups),
        out_shape=hbm((rhs, total), F32),
        in_specs=[SMEM()] + [VMEM()] * (groups + 11),
        out_specs=VMEM(),
        scratch_shapes=[
            pltpu.VMEM((table, rhs + ROWS, rank2), BF16),
            pltpu.VMEM((groups, rhs, rank2), BF16),
            pltpu.VMEM((groups, ROWS, rank2), BF16),
            pltpu.VMEM((rank * branches, rank2), F32),
            pltpu.VMEM((branches, rhs, rank2), BF16),
        ]
        + [
            pltpu.VMEM((ROUND, rank, 2 * ROWS), BF16),
            pltpu.VMEM((ROUND, ROWS, far_leaf.shape[0] * rank), BF16),
            pltpu.VMEM((ROUND, rhs, far_leaf.shape[0] * rank), BF16),
            pltpu.VMEM((ROUND, rank, far_leaf.shape[0] * rank), BF16),
        ]
        * 2,
        compiler_params=PARAMS,
        name="downward",
    )(
        far_turned,
        tile,
        *vmem(*tiles[1:]),
        far_b,
        part_d,
        down_device[:, :, 0],
        jnp.transpose(down_branch, (0, 2, 1)),
        *vmem(down),
        own,
        moments,
        *vmem(received),
        basis,
        *vmem(near, edge),
    )


def solution(mesh):
    points = P(None, ("grp", "dev"))
    blocks = P(None, None, ("grp", "dev"))
    placed = (points,) * 3 + (blocks,) * 9 + (P(None, None, "grp"),) + (points,) * 4

    return jax.shard_map(on_device, mesh=mesh, in_specs=placed, out_specs=points, check_vma=False)
```

```python
import functools
import math

import jax
import jax.numpy as jnp
from jax import lax
from jax.experimental import pallas as pl
from jax.experimental.pallas import tpu as pltpu
from jax.sharding import PartitionSpec as P

REACH = 4
FAN = 8
ROUND = 8
PAIRS = 7

INV_FOUR_PI = 1.0 / (4.0 * math.pi)
SOFTEN = 0.25
ROWS = 8

BF16 = jnp.bfloat16
F32 = jnp.float32


def dot(a, b):
    return jnp.dot(a, b, preferred_element_type=F32)


def dot_t(a, b):
    return lax.dot_general(a, b, (((1,), (1,)), ((), ())), preferred_element_type=F32)


def dot_0(a, b):
    return lax.dot_general(a, b, (((0,), (0,)), ((), ())), preferred_element_type=F32)


def fetch(source, target, sem):
    copy = pltpu.make_async_copy(source, target, sem)
    copy.start()
    return copy


def low_half(shape):
    width = shape[-1]
    return lax.broadcasted_iota(jnp.int32, shape, len(shape) - 1) < width // 2


def pair(low, first, second):
    return jnp.where(low, first, second)


def swap(tile):
    half = tile.shape[-1] // 2
    return jnp.concatenate([tile[..., half:], tile[..., :half]], axis=-1)


def twice(tile):
    return jnp.concatenate([tile, tile], axis=-1)


def three(value):
    first = value.astype(BF16).astype(F32)
    rest = value - first
    second = rest.astype(BF16).astype(F32)
    return first, second, rest - second


def source_rows(x, y, z):
    return (-2.0 * x, -2.0 * y, -2.0 * z) + three(x * x + y * y + z * z)


def row_mask(shape, rows):
    row = lax.broadcasted_iota(jnp.int32, shape, 0)
    found = row == rows[0]
    for r in rows[1:]:
        found = found | (row == r)
    return found.astype(F32)


def source_tail(width):
    return row_mask((ROWS, width), (3, 4, 5, 6)).astype(BF16)


def target_of(rows):
    rows = rows.astype(F32)
    shape = rows.shape
    squares = row_mask(shape, (3, 4, 5))
    upper = rows * (-0.5 * row_mask(shape, (0, 1, 2))) + squares
    lower = rows * squares + SOFTEN * row_mask(shape, (6,))
    return jnp.concatenate([upper, lower], axis=0).astype(BF16)


def put_rows(ref, rows, count, first=0):
    for f in range(ROWS):
        value = rows[f - first] if 0 <= f - first < len(rows) else jnp.zeros_like(rows[0])
        ref[pl.ds(f, count, stride=ROWS), :] = value


def stack_rows(rows):
    n = rows[0].shape[1]
    return jnp.concatenate(tuple(rows) + (jnp.zeros((ROWS - len(rows), n), F32),), axis=0)


def couplings(target, slots, source_ref, tail):
    low = low_half(source_ref.shape[1:])
    tiles = [
        jnp.concatenate([pair(low, source_ref[first], source_ref[second]), tail], axis=0)
        for first, second in zip(slots[0::2], slots[1::2])
    ]
    return kern_of(dot_0(target, jnp.concatenate(tiles, axis=1)))


def kern_of(square):
    return (INV_FOUR_PI * lax.rsqrt(square)).astype(BF16)


def gathered(slots, moment_ref):
    low = low_half(moment_ref.shape[1:])
    tiles = [pair(low, moment_ref[first], moment_ref[second]) for first, second in zip(slots[0::2], slots[1::2])]
    return jnp.concatenate(tiles, axis=1)


def interact(target, slots, source_ref, tail, moment_ref):
    return dot_t(gathered(slots, moment_ref), couplings(target, slots, source_ref, tail))


def upward_kernel(
    send_ref, charges_ref, points_ref, basis_ref, proxy_ref, up_leaf_hbm, up_branch_ref, up_device_ref, pbranch_ref,
    pdevice_ref, moment_ref, own_ref, out_ref, inner_ref, outer_ref, shared_ref, tile_ref, late_ref, up_leaf_ref,
    scratch_ref, branch_ref, sem,
):
    slots, devices = send_ref.shape
    leaves, rhs, rank2 = moment_ref.shape
    transfers = fetch(up_leaf_hbm, up_leaf_ref, sem)
    low = low_half((rhs, rank2))
    rows = source_rows(*[twice(jnp.transpose(proxy_ref[c].astype(F32))) for c in range(3)])
    put_rows(tile_ref, rows, leaves)
    own_ref[...] = tile_ref[...].astype(BF16).reshape(own_ref.shape)
    put_rows(tile_ref, rows[:3], leaves)
    put_rows(late_ref, rows[:3], leaves, 3)

    def leaf_pair(i, carry):
        columns = pl.ds(pl.multiple_of(i * rank2, rank2), rank2)
        q = charges_ref[:, columns]
        u = basis_ref[:, columns]
        zero = jnp.zeros_like(q)
        stacked = jnp.concatenate([jnp.where(low, q, zero), jnp.where(low, zero, q)], axis=0)
        product = dot_t(stacked, jnp.concatenate([u, u], axis=0)).astype(BF16)
        moment_ref[2 * i] = product[:rhs]
        moment_ref[2 * i + 1] = product[rhs:]
        return carry

    lax.fori_loop(0, leaves // 2, leaf_pair, 0, unroll=8)
    low8 = low_half((ROWS, rank2))
    base = slots // 2 * rhs

    def pack(p, carry):
        s = [send_ref[t, p] for t in range(slots)]
        tiles = []
        for q in range(slots // 2):
            first, second = s[2 * q], s[2 * q + 1]
            out_ref[p, q * rhs : (q + 1) * rhs, :] = pair(low, moment_ref[first], moment_ref[second])
            ref = (tile_ref, late_ref)[q]
            tiles.append(
                pair(
                    low8,
                    ref[pl.ds(pl.multiple_of(first * ROWS, ROWS), ROWS), :],
                    ref[pl.ds(pl.multiple_of(second * ROWS, ROWS), ROWS), :],
                )
            )
        out_ref[p, base:, :] = (tiles[0] + tiles[1]).astype(BF16)
        return carry

    lax.fori_loop(0, devices, pack, 0, unroll=4)
    total = charges_ref.shape[1]
    halo = inner_ref.shape[0] // (rhs + ROWS) * rank2
    odd = lax.rem(lax.axis_index("dev"), 2) == 1
    for ref, first in ((inner_ref, odd), (outer_ref, jnp.logical_not(odd))):
        start = jnp.where(first, 0, total - halo)
        for n in range(halo // rank2):
            columns = pl.ds(pl.multiple_of(start + n * rank2, rank2), rank2)
            base = n * (rhs + ROWS)
            ref[base : base + rhs, :] = charges_ref[:, columns]
            points = points_ref[:, columns].astype(F32)
            rows = jnp.concatenate([points, jnp.zeros((ROWS - 3, rank2), F32)], axis=0)
            ref[base + rhs : base + rhs + ROWS, :] = rows.astype(BF16)
    transfers.wait()
    raise_moments(
        moment_ref, up_leaf_ref, up_branch_ref, up_device_ref, pbranch_ref, pdevice_ref, shared_ref, scratch_ref, branch_ref
    )


def relayout(x_ref, scratch_ref):
    rank, _, leaves = x_ref.shape
    half = rank // 2
    eye = (
        lax.broadcasted_iota(jnp.int32, (leaves, leaves), 0)
        == lax.broadcasted_iota(jnp.int32, (leaves, leaves), 1)
    ).astype(BF16)
    for k in range(0, half, 2):
        block = jnp.concatenate(
            [x_ref[k], x_ref[k + half], x_ref[k + 1], x_ref[k + 1 + half]], axis=0
        )
        turned = dot_t(eye, block)
        for n in range(2):
            scratch_ref[pl.ds(k + n, leaves, stride=half), :] = turned[:, n * 2 * rank : (n + 1) * 2 * rank]


def spread_rows(block, low):
    zero = jnp.zeros_like(block)
    return jnp.concatenate([jnp.where(low, block, zero), jnp.where(low, zero, block)], axis=0)


def raise_moments(
    moment_ref, up_leaf_ref, up_branch_ref, up_device_ref, pbranch_ref, pdevice_ref, out_ref, scratch_ref, branch_ref
):
    leaves, rhs, rank2 = moment_ref.shape
    rank = rank2 // 2
    half = rank // 2
    branches = leaves // FAN
    relayout(up_leaf_ref, scratch_ref)
    low = low_half((half, rank2))
    low_m = low_half((rhs, rank2))
    low_r = low_half((ROWS, rank2))
    wide = up_branch_ref[...].astype(F32).reshape(rank * branches, rank)
    branch_ref[...] = twice(wide)
    rows = source_rows(*[twice(pbranch_ref[c].astype(F32)) for c in range(3)])
    m_device = jnp.zeros((rhs, rank), F32)
    previous = None
    base = branches // 2 * rhs
    for c in range(branches):
        blocks, moments = [], []
        for b in range(c * FAN, (c + 1) * FAN):
            block = scratch_ref[b * half : (b + 1) * half, :].astype(BF16)
            blocks.append(spread_rows(block, low))
            moments.append(moment_ref[b])
        m_branch = dot_t(jnp.concatenate(moments, axis=1), jnp.concatenate(blocks, axis=1)).astype(BF16)
        matrix = branch_ref[pl.ds(c, rank, stride=branches), :][:, :rank].astype(BF16)
        m_device = m_device + dot_t(m_branch, matrix)
        spread = twice(m_branch)
        source = stack_rows([r[c : c + 1, :] for r in rows]).astype(BF16)
        if c % 2 == 1:
            q = c // 2
            out_ref[q * rhs : (q + 1) * rhs, :] = pair(low_m, previous[0], spread)
            out_ref[base + q * ROWS : base + (q + 1) * ROWS, :] = pair(low_r, previous[1], source)
        previous = spread, source
    base = base + branches // 2 * ROWS
    m_device = m_device.astype(BF16)
    share = dot_t(m_device, up_device_ref[...]).astype(BF16)
    out_ref[base : base + rhs, :] = jnp.concatenate([m_device, share], axis=1)
    rows = source_rows(*[twice(pdevice_ref[c : c + 1, :].astype(F32)) for c in range(3)])
    out_ref[base + rhs :, :] = stack_rows(rows).astype(BF16)


def turn_kernel(down_leaf_ref, far_ref, _, down_ref, turned_ref, scratch_ref):
    turned_ref[...] = jnp.transpose(far_ref[...].astype(F32)).astype(jnp.int32)
    relayout(down_leaf_ref, scratch_ref)
    down_ref[...] = scratch_ref[...].astype(BF16)


def point_rows(points):
    return stack_rows(source_rows(*[points[c : c + 1, :] for c in range(3)]))


def near_weights(near_ref, size, weight_ref):
    near = near_ref[...]
    leaves = near.shape[1]
    reach = weight_ref.shape[2]
    span = 2 * REACH + 1
    counts = [jnp.sum((near == o - REACH).astype(F32), axis=0, keepdims=True) for o in range(span)]
    counts = jnp.concatenate(counts + [jnp.zeros((2 * ROWS - span, leaves), F32)], axis=0).astype(BF16)
    offset = lax.broadcasted_iota(jnp.int32, (2 * ROWS, reach), 0)
    block = lax.broadcasted_iota(jnp.int32, (2 * ROWS, reach), 1) // size
    for h in range(2):
        weight_ref[h] = dot_0(counts, (block == offset + h).astype(BF16))


def near_couplings(target, source, weights, kern_ref):
    kern = kern_of(dot_0(target, source))
    size, reach = kern.shape[0] // 2, kern.shape[1]
    for h in range(2):
        weight = jnp.broadcast_to(weights[h], (2 * ROWS, reach)).astype(BF16)
        for s in range(h * size, (h + 1) * size, 2 * ROWS):
            kern_ref[s : s + 2 * ROWS, :] = kern[s : s + 2 * ROWS, :] * weight


def near_kernel(
    near_ref, charges_ref, points_ref, _, out_ref, source_ref, target_ref, weight_ref, kern_a_ref, kern_b_ref
):
    rhs, total = charges_ref.shape
    size = total // near_ref.shape[1]
    halo = REACH * size
    lanes = 2 * size
    reach = weight_ref.shape[2]
    rows = point_rows(points_ref[...].astype(F32))
    source_ref[...] = jnp.concatenate([rows.astype(BF16), source_tail(total)], axis=0)
    target_ref[...] = target_of(rows)
    near_weights(near_ref, size, weight_ref)
    out_ref[:, :halo] = jnp.zeros((rhs, halo), F32)
    out_ref[:, total - halo :] = jnp.zeros((rhs, halo), F32)
    width = kern_a_ref.shape[0]
    first = halo // lanes
    rounds = (total - 2 * halo) // lanes // width

    def evaluate(i, n, kern_ref):
        j = first + i * width + n
        start = pl.multiple_of(j * lanes, lanes)
        near_couplings(
            target_ref[:, pl.ds(start, lanes)],
            source_ref[:, pl.ds(pl.multiple_of(start - halo, lanes), reach)],
            [weight_ref[h, pl.ds(2 * j + h, 1), :] for h in range(2)],
            kern_ref.at[n],
        )

    def apply(i, n, kern_ref):
        start = pl.multiple_of((first + i * width + n) * lanes, lanes)
        columns = pl.ds(pl.multiple_of(start - halo, lanes), reach)
        out_ref[:, pl.ds(start, lanes)] = dot_t(charges_ref[:, columns], kern_ref[n])

    for n in range(width):
        evaluate(0, n, kern_a_ref)

    def step(t, carry):
        for n in range(width):
            evaluate(2 * t + 1, n, kern_b_ref)
            apply(2 * t, n, kern_a_ref)
        for n in range(width):
            evaluate(jnp.minimum(2 * t + 2, rounds - 1), n, kern_a_ref)
            apply(2 * t + 1, n, kern_b_ref)
        return carry

    lax.fori_loop(0, rounds // 2, step, 0)


def edge_pairs(near_ref, ends_ref, end_points_ref, inner_ref, outer_ref, out_ref, weight_ref, kern_ref):
    rhs = ends_ref.shape[1]
    leaves = near_ref.shape[1]
    halo = out_ref.shape[1] // 2
    lanes = inner_ref.shape[1]
    size = lanes // 2
    count = halo // lanes
    reach = weight_ref.shape[2]
    odd = lax.rem(lax.axis_index("dev"), 2) == 1
    near_weights(near_ref, size, weight_ref)
    inner, outer = inner_ref[...], outer_ref[...]
    height = inner.shape[0] // count
    for side, block in enumerate((jnp.where(odd, inner, outer), jnp.where(odd, outer, inner))):
        beyond = jnp.concatenate([block[n * height : (n + 1) * height, :] for n in range(count)], axis=1)
        parts = [(beyond[:rhs, :], beyond[rhs : rhs + 3, :].astype(F32)), (ends_ref[side], end_points_ref[side].astype(F32))]
        parts = parts if side == 0 else parts[::-1]
        wide = jnp.concatenate([p[0] for p in parts], axis=1)
        rows = point_rows(jnp.concatenate([p[1] for p in parts], axis=1))
        source = jnp.concatenate([rows.astype(BF16), source_tail(rows.shape[1])], axis=0)
        target = target_of(rows[:, halo : 2 * halo])
        for j in range(count):
            leaf = 2 * j + side * (leaves - 2 * count)
            place = side * count + j
            near_couplings(
                target[:, j * lanes : (j + 1) * lanes],
                source[:, j * lanes : j * lanes + reach],
                [weight_ref[h, leaf + h : leaf + h + 1, :] for h in range(2)],
                kern_ref.at[place],
            )
            columns = slice(place * lanes, (place + 1) * lanes)
            out_ref[:, columns] = dot_t(wide[:, j * lanes : j * lanes + reach], kern_ref[place])


def put_pair(ref, slot, tile, row=0):
    low = low_half(tile.shape)
    other = swap(tile)
    ref[slot, row : row + tile.shape[0], :] = pair(low, tile, other)
    ref[slot + 1, row : row + tile.shape[0], :] = pair(low, other, tile)


def part_of(parts, s, members):
    length = parts[0].shape[0] // 2
    owner = lax.axis_index("dev") ^ (s // 2 + s % 2 * (members // 2))
    return parts[s // 2].at[s % 2 * length : (s % 2 + 1) * length], owner


def top_kernel(*refs, members):
    _, pgroup_ref, *parts, out_ref = refs
    rhs = out_ref.shape[0] - ROWS
    rank2 = out_ref.shape[1]
    m_group = jnp.zeros((rhs, rank2), F32)
    for s in range(members):
        part, _ = part_of(parts, s, members)
        base = part.shape[0] - rhs - ROWS
        m_group = m_group + part[base : base + rhs, :].astype(F32)
    out_ref[:rhs, :] = twice(m_group[:, rank2 // 2 :]).astype(BF16)
    rows = source_rows(*[twice(pgroup_ref[c : c + 1, :].astype(F32)) for c in range(3)])
    out_ref[rhs:, :] = stack_rows(rows).astype(BF16)


def group_kernel(*refs, members):
    far_ref, near_ref, charges_hbm, points_hbm, inner_ref, outer_ref, _ = refs[:7]
    count = members // 2
    parts = refs[7 : 7 + count]
    fb_ref, ld_ref, edge_ref = refs[7 + count : 10 + count]
    (
        moment_ref, source_ref, dev_m_ref, dev_source_ref, ends_ref, end_points_ref, weight_ref, kern_ref, sems,
    ) = refs[10 + count :]
    total, width = charges_hbm.shape[1], ends_ref.shape[2]
    copies = []
    for side in range(2):
        columns = slice(side * (total - width), side * (total - width) + width)
        copies.append(fetch(charges_hbm.at[:, columns], ends_ref.at[side], sems.at[2 * side]))
        copies.append(fetch(points_hbm.at[:, columns], end_points_ref.at[side], sems.at[2 * side + 1]))
    branches, entries = far_ref.shape
    rhs, rank2 = moment_ref.shape[1:]
    rank = rank2 // 2
    me = lax.axis_index("dev")
    low = low_half((rhs, rank2))
    tail = source_tail(rank2)
    first = branches // 2 * rhs
    base = first + branches // 2 * ROWS
    for s in range(members):
        part, owner = part_of(parts, s, members)
        for q in range(branches // 2):
            put_pair(moment_ref, owner * branches + 2 * q, part[q * rhs : (q + 1) * rhs, :])
            put_pair(source_ref, owner * branches + 2 * q, part[first + q * ROWS : first + (q + 1) * ROWS, :])
        mixed = part[base : base + rhs, :].astype(F32)
        keep = (jnp.abs(owner - me) >= 2).astype(F32)
        dev_m_ref[owner] = (pair(low, mixed, pltpu.roll(mixed, rank, 1)) * keep).astype(BF16)
        dev_source_ref[owner] = part[base + rhs :, :]
    for c in range(branches):
        target = target_of(source_ref[me * branches + c][:, :rank])
        fb_ref[c] = interact(target, [far_ref[c, e] for e in range(entries)], source_ref, tail, moment_ref)
    target = target_of(dev_source_ref[me][:, :rank])
    ld_ref[...] = interact(target, list(range(members)), dev_source_ref, tail, dev_m_ref)
    for copy in copies:
        copy.wait()
    edge_pairs(near_ref, ends_ref, end_points_ref, inner_ref, outer_ref, edge_ref, weight_ref, kern_ref)


def downward_kernel(*refs, groups):
    far_ref = refs[0]
    tiles = refs[1 : 1 + groups]
    (
        fb_ref, ld_ref, down_device_ref, down_branch_ref, down_ref, own_ref, own_m_ref, recv_ref, basis_ref, near_ref, edge_ref,
        out_ref, table_ref, grp_m_ref, grp_source_ref, branch_ref, parent_ref, *buffers,
    ) = refs[1 + groups :]
    leaves, entries = far_ref.shape
    rhs, rank2 = parent_ref.shape[1:]
    rank = rank2 // 2
    half = rank // 2
    branches = leaves // FAN
    devices = recv_ref.shape[0]
    slots = (table_ref.shape[0] - leaves) // devices
    me = lax.axis_index("grp")
    low = low_half((rhs, rank2))
    tail = source_tail(rank2)

    for s, tile_ref in enumerate(tiles):
        owner = me ^ s
        keep = (jnp.abs(owner - me) >= 2).astype(F32)
        grp_m_ref[owner] = (tile_ref[:rhs, :].astype(F32) * keep).astype(BF16)
        grp_source_ref[owner] = tile_ref[rhs:, :]
    target = target_of(tiles[0][rhs:, :rank])
    l_group = interact(target, list(range(groups)), grp_source_ref, tail, grp_m_ref).astype(BF16)
    l_device = (ld_ref[...] + dot_t(l_group, down_device_ref[...])).astype(BF16)
    branch_ref[...] = twice(down_branch_ref[...].astype(F32).reshape(rank * branches, rank))
    for c in range(branches):
        matrix = branch_ref[pl.ds(c, rank, stride=branches), :][:, :rank].astype(BF16)
        parent_ref[c] = twice((fb_ref[c] + dot_t(l_device, matrix)).astype(BF16))

    table_ref[:leaves, :rhs, :] = own_m_ref[...]
    table_ref[:leaves, rhs:, :] = own_ref[...]
    base = slots // 2 * rhs

    row = lax.broadcasted_iota(jnp.int32, (ROWS, rank2), 0)
    low_r = low_half((ROWS, rank2))
    zero = jnp.zeros((ROWS, rank2), F32)

    def unpack(p, carry):
        tile = recv_ref[p, base:, :].astype(F32)
        squares = 0.25 * tile * tile
        parts = three(squares + pltpu.roll(squares, ROWS - 1, 0) + pltpu.roll(squares, ROWS - 2, 0))
        for q in range(slots // 2):
            slot = leaves + p * slots + 2 * q
            put_pair(table_ref, slot, recv_ref[p, q * rhs : (q + 1) * rhs, :], 0)
            rows = jnp.where(row < 3, pltpu.roll(tile, ROWS - 3, 0) if q else tile, zero)
            for n, part in enumerate(parts):
                shift = 3 + n - 3 * q
                rows = jnp.where(row == 3 + n, pltpu.roll(part, shift, 0) if shift else part, rows)
            other = pltpu.roll(rows, rank, 1)
            table_ref[slot, rhs:, :] = pair(low_r, rows, other).astype(BF16)
            table_ref[slot + 1, rhs:, :] = pair(low_r, other, rows).astype(BF16)
        return carry

    lax.fori_loop(0, devices, unpack, 0, unroll=min(devices, 32))
    low_d = low_half((half, rank2))

    width = buffers[0].shape[0]
    rounds = leaves // width
    low_s = low_half((ROWS, rank2))

    def gather(b, low, rows, ref):
        for e in range(0, entries, 2):
            first, second = far_ref[b, e], far_ref[b, e + 1]
            ref[:, e * rank : (e + 2) * rank] = pair(low, table_ref[first, rows, :], table_ref[second, rows, :])

    def collect_sources(i, h, targets_ref, sources_ref):
        b = width * i + h
        targets_ref[h] = jnp.transpose(target_of(table_ref[b, rhs:, :rank]))
        gather(b, low_s, slice(rhs, None), sources_ref.at[h])

    def collect_moments(i, h, moments_ref):
        gather(width * i + h, low, slice(None, rhs), moments_ref.at[h])

    def evaluate(h, targets_ref, sources_ref, kern_ref):
        sources = jnp.concatenate([sources_ref[h], source_tail(sources_ref.shape[2])], axis=0)
        kern_ref[h] = kern_of(dot(targets_ref[h], sources))

    def apply(i, h, moments_ref, kern_ref):
        b = width * i + h
        far = dot_t(moments_ref[h], kern_ref[h])
        rows = down_ref[pl.ds(pl.multiple_of(b * half, half), half), :]
        return (far + dot_t(parent_ref[b // FAN], spread_rows(rows, low_d))).astype(BF16)

    def finish(i, sums, starts=None):
        for h in starts or range(0, width, 2):
            columns = pl.ds(pl.multiple_of((width * i + h) * rank, rank2), rank2)
            product = dot(jnp.concatenate(sums[h : h + 2], axis=0), basis_ref[:, columns])
            out_ref[:, columns] = near_ref[:, columns] + pair(low, product[:rhs], product[rhs:])

    def stage(i, sums, this, other):
        done, last = jnp.maximum(i - 2, 0), sums
        before, after, later = jnp.maximum(i - 1, 0), jnp.minimum(i + 1, rounds - 1), jnp.minimum(i + 2, rounds - 1)
        sums = []
        for h in range(width):
            evaluate(h, this[0], this[1], this[3])
            sums.append(apply(before, h, other[2], other[3]))
            if h % 2 == 0:
                finish(done, last, (h,))
            collect_sources(later, h, this[0], this[1])
            collect_moments(after, h, other[2])
        return tuple(sums)

    even, odd = buffers[:4], buffers[4:]
    for h in range(width):
        collect_sources(0, h, *even[:2])
        collect_sources(1, h, *odd[:2])
        collect_moments(0, h, even[2])
    odd[2][...] = jnp.zeros_like(odd[2])
    odd[3][...] = jnp.zeros_like(odd[3])

    def step(t, sums):
        return stage(2 * t + 1, stage(2 * t, sums, even, odd), odd, even)

    sums = lax.fori_loop(0, rounds // 2, step, (jnp.zeros((rhs, rank), BF16),) * width)
    finish(rounds - 2, sums)
    finish(rounds - 1, tuple(apply(rounds - 1, h, odd[2], odd[3]) for h in range(width)))
    total, halo = out_ref.shape[1], edge_ref.shape[1] // 2
    out_ref[:, :halo] += edge_ref[:, :halo]
    out_ref[:, total - halo :] += edge_ref[:, halo:]


VMEM = functools.partial(pl.BlockSpec, memory_space=pltpu.VMEM)
SMEM = functools.partial(pl.BlockSpec, memory_space=pltpu.SMEM)
ANY = functools.partial(pl.BlockSpec, memory_space=pl.ANY)
PARAMS = pltpu.CompilerParams()


def hbm(shape, dtype):
    return jax.ShapeDtypeStruct(shape, dtype)


def vmem(*arrays):
    return [pltpu.with_memory_space_constraint(a, pltpu.VMEM) if a.size <= 1 << 19 else a for a in arrays]


def on_device(
    charges, points, basis, up_leaf, up_branch, up_device, down_leaf, down_branch, down_device,
    proxy_leaf, proxy_branch, proxy_device, proxy_group, far_leaf, send_leaf, far_branch, near_leaf,
):
    rhs, total = charges.shape
    rank = basis.shape[0]
    leaves = up_leaf.shape[2]
    size = total // leaves
    branches = leaves // FAN
    slots = send_leaf.shape[0]
    groups = lax.axis_size("grp")
    members = lax.axis_size("dev")
    devices = groups * members
    rank2 = 2 * rank
    half = rank // 2
    halo = REACH * size
    assert rank == size and slots == 4 and branches % 2 == 0 and members % 2 == 0

    moments, own, listed, inner, outer, shared = pl.pallas_call(
        upward_kernel,
        out_shape=(
            pltpu.VMEM((leaves, rhs, rank2), BF16),
            hbm((leaves, ROWS, rank2), BF16),
            hbm((devices, slots // 2 * rhs + ROWS, rank2), BF16),
            pltpu.VMEM((halo // rank2 * (rhs + ROWS), rank2), BF16),
            pltpu.VMEM((halo // rank2 * (rhs + ROWS), rank2), BF16),
            hbm(((branches // 2 + 1) * (rhs + ROWS), rank2), BF16),
        ),
        in_specs=[SMEM()] + [VMEM()] * 4 + [ANY()] + [VMEM()] * 4,
        out_specs=(VMEM(),) * 6,
        scratch_shapes=[
            pltpu.VMEM((leaves * ROWS, rank2), F32),
            pltpu.VMEM((leaves * ROWS, rank2), F32),
            pltpu.VMEM(up_leaf.shape, BF16),
            pltpu.VMEM((leaves * half, rank2), F32),
            pltpu.VMEM((rank * branches, rank2), F32),
            pltpu.SemaphoreType.DMA(()),
        ],
        compiler_params=PARAMS,
        name="upward",
    )(
        send_leaf,
        charges,
        points,
        basis,
        proxy_leaf,
        up_leaf,
        jnp.transpose(up_branch, (0, 2, 1)),
        up_device[:, :, 0],
        jnp.transpose(proxy_branch, (0, 2, 1)),
        proxy_device[:, :, 0],
    )
    (moments,) = vmem(moments)
    received = lax.all_to_all(listed, ("grp", "dev"), split_axis=0, concat_axis=0, tiled=True)

    partner = lax.ppermute(shared, "dev", [(i, i ^ members // 2) for i in range(members)])
    down, far_turned = pl.pallas_call(
        turn_kernel,
        out_shape=(pltpu.VMEM((leaves * half, rank2), BF16), hbm(far_leaf.shape[::-1], jnp.int32)),
        in_specs=[VMEM(), VMEM(), ANY()],
        out_specs=(VMEM(), VMEM()),
        scratch_shapes=[pltpu.VMEM((leaves * half, rank2), F32)],
        compiler_params=PARAMS,
        name="turn",
    )(down_leaf, far_leaf, shared)
    partner, down = lax.optimization_barrier((partner, down))
    both = jnp.concatenate([shared, partner], axis=0)
    parts = [both]
    for s in range(1, members // 2):
        parts.append(lax.ppermute(both, "dev", [(i, i ^ s) for i in range(members)]))

    reach = (2 * REACH + 2) * size
    near = pl.pallas_call(
        near_kernel,
        out_shape=pltpu.VMEM((rhs, total), F32),
        in_specs=[VMEM()] * 4,
        out_specs=VMEM(),
        scratch_shapes=[
            pltpu.VMEM((2 * ROWS, total), BF16),
            pltpu.VMEM((2 * ROWS, total), BF16),
            pltpu.VMEM((2, leaves, reach), F32),
            pltpu.VMEM((PAIRS, 2 * size, reach), BF16),
            pltpu.VMEM((PAIRS, 2 * size, reach), BF16),
        ],
        compiler_params=PARAMS,
        name="near",
    )(near_leaf, charges, points, *vmem(both))

    swaps = [(i, i + 1 if i % 2 else i - 1) for i in range(1, devices - 1)]
    inner, outer, near = lax.optimization_barrier((inner, outer, near))
    outer = lax.ppermute(outer, ("grp", "dev"), swaps)
    inner = lax.ppermute(inner, "dev", [(i, i ^ 1) for i in range(members)])

    parts = vmem(*parts)
    tile = pl.pallas_call(
        functools.partial(top_kernel, members=members),
        out_shape=hbm((rhs + ROWS, rank2), BF16),
        in_specs=[VMEM()] * (2 + len(parts)),
        out_specs=VMEM(),
        compiler_params=PARAMS,
        name="top",
    )(*vmem(near), proxy_group[:, :, 0], *parts)
    assert groups & (groups - 1) == 0 and members & (members - 1) == 0
    tiles = [tile] + [lax.ppermute(tile, "grp", [(i, i ^ s) for i in range(groups)]) for s in range(1, groups)]
    far_b, part_d, edge = pl.pallas_call(
        functools.partial(group_kernel, members=members),
        out_shape=(hbm((branches, rhs, rank), F32), hbm((rhs, rank), F32), pltpu.VMEM((rhs, 2 * halo), F32)),
        in_specs=[SMEM(), VMEM(), ANY(), ANY(), VMEM(), VMEM(), ANY()] + [VMEM()] * len(parts),
        out_specs=(VMEM(),) * 3,
        scratch_shapes=[
            pltpu.VMEM((members * branches, rhs, rank2), BF16),
            pltpu.VMEM((members * branches, ROWS, rank2), BF16),
            pltpu.VMEM((members, rhs, rank2), BF16),
            pltpu.VMEM((members, ROWS, rank2), BF16),
            pltpu.VMEM((2, rhs, 2 * halo), BF16),
            pltpu.VMEM((2, 3, 2 * halo), BF16),
            pltpu.VMEM((2, leaves, reach), F32),
            pltpu.VMEM((REACH, 2 * size, reach), BF16),
            pltpu.SemaphoreType.DMA((4,)),
        ],
        compiler_params=PARAMS,
        name="group",
    )(jnp.transpose(far_branch), near_leaf, charges, points, *vmem(inner, outer), tile, *parts)

    table = leaves + devices * slots
    return pl.pallas_call(
        functools.partial(downward_kernel, groups=groups),
        out_shape=hbm((rhs, total), F32),
        in_specs=[SMEM()] + [VMEM()] * (groups + 11),
        out_specs=VMEM(),
        scratch_shapes=[
            pltpu.VMEM((table, rhs + ROWS, rank2), BF16),
            pltpu.VMEM((groups, rhs, rank2), BF16),
            pltpu.VMEM((groups, ROWS, rank2), BF16),
            pltpu.VMEM((rank * branches, rank2), F32),
            pltpu.VMEM((branches, rhs, rank2), BF16),
        ]
        + [
            pltpu.VMEM((ROUND, rank, 2 * ROWS), BF16),
            pltpu.VMEM((ROUND, ROWS, far_leaf.shape[0] * rank), BF16),
            pltpu.VMEM((ROUND, rhs, far_leaf.shape[0] * rank), BF16),
            pltpu.VMEM((ROUND, rank, far_leaf.shape[0] * rank), BF16),
        ]
        * 2,
        compiler_params=PARAMS,
        name="downward",
    )(
        far_turned,
        tile,
        *vmem(*tiles[1:]),
        far_b,
        part_d,
        down_device[:, :, 0],
        jnp.transpose(down_branch, (0, 2, 1)),
        *vmem(down),
        own,
        moments,
        *vmem(received),
        basis,
        *vmem(near, edge),
    )


def solution(mesh):
    points = P(None, ("grp", "dev"))
    blocks = P(None, None, ("grp", "dev"))
    placed = (points,) * 3 + (blocks,) * 9 + (P(None, None, "grp"),) + (points,) * 4

    return jax.shard_map(on_device, mesh=mesh, in_specs=placed, out_specs=points, check_vma=False)
```

```python
import functools
import math

import jax
import jax.numpy as jnp
from jax import lax
from jax.experimental import pallas as pl
from jax.experimental.pallas import tpu as pltpu
from jax.sharding import PartitionSpec as P

REACH = 4
FAN = 8
ROUND = 8
PAIRS = 7

INV_FOUR_PI = 1.0 / (4.0 * math.pi)
SOFTEN = 0.25
ROWS = 8

BF16 = jnp.bfloat16
F32 = jnp.float32


def dot(a, b):
    return jnp.dot(a, b, preferred_element_type=F32)


def dot_t(a, b):
    return lax.dot_general(a, b, (((1,), (1,)), ((), ())), preferred_element_type=F32)


def dot_0(a, b):
    return lax.dot_general(a, b, (((0,), (0,)), ((), ())), preferred_element_type=F32)


def fetch(source, target, sem):
    copy = pltpu.make_async_copy(source, target, sem)
    copy.start()
    return copy


def low_half(shape):
    width = shape[-1]
    return lax.broadcasted_iota(jnp.int32, shape, len(shape) - 1) < width // 2


def pair(low, first, second):
    return jnp.where(low, first, second)


def swap(tile):
    half = tile.shape[-1] // 2
    return jnp.concatenate([tile[..., half:], tile[..., :half]], axis=-1)


def twice(tile):
    return jnp.concatenate([tile, tile], axis=-1)


def three(value):
    first = value.astype(BF16).astype(F32)
    rest = value - first
    second = rest.astype(BF16).astype(F32)
    return first, second, rest - second


def source_rows(x, y, z):
    return (-2.0 * x, -2.0 * y, -2.0 * z) + three(x * x + y * y + z * z)


def row_mask(shape, rows):
    row = lax.broadcasted_iota(jnp.int32, shape, 0)
    found = row == rows[0]
    for r in rows[1:]:
        found = found | (row == r)
    return found.astype(F32)


def source_tail(width):
    return row_mask((ROWS, width), (3, 4, 5, 6)).astype(BF16)


def target_of(rows):
    rows = rows.astype(F32)
    shape = rows.shape
    squares = row_mask(shape, (3, 4, 5))
    upper = rows * (-0.5 * row_mask(shape, (0, 1, 2))) + squares
    lower = rows * squares + SOFTEN * row_mask(shape, (6,))
    return jnp.concatenate([upper, lower], axis=0).astype(BF16)


def put_rows(ref, rows, count, first=0):
    for f in range(ROWS):
        value = rows[f - first] if 0 <= f - first < len(rows) else jnp.zeros_like(rows[0])
        ref[pl.ds(f, count, stride=ROWS), :] = value


def stack_rows(rows):
    n = rows[0].shape[1]
    return jnp.concatenate(tuple(rows) + (jnp.zeros((ROWS - len(rows), n), F32),), axis=0)


def couplings(target, slots, source_ref, tail):
    low = low_half(source_ref.shape[1:])
    tiles = [
        jnp.concatenate([pair(low, source_ref[first], source_ref[second]), tail], axis=0)
        for first, second in zip(slots[0::2], slots[1::2])
    ]
    return kern_of(dot_0(target, jnp.concatenate(tiles, axis=1)))


def kern_of(square):
    return (INV_FOUR_PI * lax.rsqrt(square)).astype(BF16)


def gathered(slots, moment_ref):
    low = low_half(moment_ref.shape[1:])
    tiles = [pair(low, moment_ref[first], moment_ref[second]) for first, second in zip(slots[0::2], slots[1::2])]
    return jnp.concatenate(tiles, axis=1)


def interact(target, slots, source_ref, tail, moment_ref):
    return dot_t(gathered(slots, moment_ref), couplings(target, slots, source_ref, tail))


def upward_kernel(
    send_ref, charges_ref, points_ref, basis_ref, proxy_ref, up_leaf_hbm, up_branch_ref, up_device_ref, pbranch_ref,
    pdevice_ref, pgroup_ref, moment_ref, own_ref, out_ref, inner_ref, outer_ref, shared_ref, tile_ref, late_ref, up_leaf_ref,
    scratch_ref, branch_ref, sem,
):
    slots, devices = send_ref.shape
    leaves, rhs, rank2 = moment_ref.shape
    transfers = fetch(up_leaf_hbm, up_leaf_ref, sem)
    low = low_half((rhs, rank2))
    rows = source_rows(*[twice(jnp.transpose(proxy_ref[c].astype(F32))) for c in range(3)])
    put_rows(tile_ref, rows, leaves)
    own_ref[...] = tile_ref[...].astype(BF16).reshape(own_ref.shape)
    put_rows(tile_ref, rows[:3], leaves)
    put_rows(late_ref, rows[:3], leaves, 3)

    def leaf_pair(i, carry):
        columns = pl.ds(pl.multiple_of(i * rank2, rank2), rank2)
        q = charges_ref[:, columns]
        u = basis_ref[:, columns]
        zero = jnp.zeros_like(q)
        stacked = jnp.concatenate([jnp.where(low, q, zero), jnp.where(low, zero, q)], axis=0)
        product = dot_t(stacked, jnp.concatenate([u, u], axis=0)).astype(BF16)
        moment_ref[2 * i] = product[:rhs]
        moment_ref[2 * i + 1] = product[rhs:]
        return carry

    lax.fori_loop(0, leaves // 2, leaf_pair, 0, unroll=8)
    transfers.wait()
    share = raise_moments(
        moment_ref, up_leaf_ref, up_branch_ref, up_device_ref, pbranch_ref, pdevice_ref, shared_ref, scratch_ref, branch_ref
    )
    share = jnp.concatenate([share[: rhs // 2], share[rhs // 2 :]], axis=1)
    gx, gy, gz = (-2.0 * pgroup_ref[c : c + 1, :].astype(F32) for c in range(3))
    group_rows = [jnp.concatenate([gx, gy], axis=1), jnp.concatenate([gz, jnp.zeros_like(gz)], axis=1)]
    group_rows = jnp.concatenate([jnp.zeros((ROWS - 2, rank2), F32)] + group_rows, axis=0)
    low8 = low_half((ROWS, rank2))
    base = slots // 2 * rhs

    def pack(p, carry):
        s = [send_ref[t, p] for t in range(slots)]
        tiles = []
        for q in range(slots // 2):
            first, second = s[2 * q], s[2 * q + 1]
            out_ref[p, q * rhs : (q + 1) * rhs, :] = pair(low, moment_ref[first], moment_ref[second])
            ref = (tile_ref, late_ref)[q]
            tiles.append(
                pair(
                    low8,
                    ref[pl.ds(pl.multiple_of(first * ROWS, ROWS), ROWS), :],
                    ref[pl.ds(pl.multiple_of(second * ROWS, ROWS), ROWS), :],
                )
            )
        out_ref[p, base : base + ROWS, :] = (tiles[0] + tiles[1] + group_rows).astype(BF16)
        out_ref[p, base + ROWS :, :] = share
        return carry

    lax.fori_loop(0, devices, pack, 0, unroll=4)
    total = charges_ref.shape[1]
    halo = inner_ref.shape[0] // (rhs + ROWS) * rank2
    odd = lax.rem(lax.axis_index("dev"), 2) == 1
    for ref, first in ((inner_ref, odd), (outer_ref, jnp.logical_not(odd))):
        start = jnp.where(first, 0, total - halo)
        for n in range(halo // rank2):
            columns = pl.ds(pl.multiple_of(start + n * rank2, rank2), rank2)
            base = n * (rhs + ROWS)
            ref[base : base + rhs, :] = charges_ref[:, columns]
            points = points_ref[:, columns].astype(F32)
            rows = jnp.concatenate([points, jnp.zeros((ROWS - 3, rank2), F32)], axis=0)
            ref[base + rhs : base + rhs + ROWS, :] = rows.astype(BF16)


def relayout(x_ref, scratch_ref):
    rank, _, leaves = x_ref.shape
    half = rank // 2
    eye = (
        lax.broadcasted_iota(jnp.int32, (leaves, leaves), 0)
        == lax.broadcasted_iota(jnp.int32, (leaves, leaves), 1)
    ).astype(BF16)
    for k in range(0, half, 2):
        block = jnp.concatenate(
            [x_ref[k], x_ref[k + half], x_ref[k + 1], x_ref[k + 1 + half]], axis=0
        )
        turned = dot_t(eye, block)
        for n in range(2):
            scratch_ref[pl.ds(k + n, leaves, stride=half), :] = turned[:, n * 2 * rank : (n + 1) * 2 * rank]


def spread_rows(block, low):
    zero = jnp.zeros_like(block)
    return jnp.concatenate([jnp.where(low, block, zero), jnp.where(low, zero, block)], axis=0)


def raise_moments(
    moment_ref, up_leaf_ref, up_branch_ref, up_device_ref, pbranch_ref, pdevice_ref, out_ref, scratch_ref, branch_ref
):
    leaves, rhs, rank2 = moment_ref.shape
    rank = rank2 // 2
    half = rank // 2
    branches = leaves // FAN
    relayout(up_leaf_ref, scratch_ref)
    low = low_half((half, rank2))
    low_m = low_half((rhs, rank2))
    low_r = low_half((ROWS, rank2))
    wide = up_branch_ref[...].astype(F32).reshape(rank * branches, rank)
    branch_ref[...] = twice(wide)
    rows = source_rows(*[twice(pbranch_ref[c].astype(F32)) for c in range(3)])
    m_device = jnp.zeros((rhs, rank), F32)
    previous = None
    base = branches // 2 * rhs
    for c in range(branches):
        blocks, moments = [], []
        for b in range(c * FAN, (c + 1) * FAN):
            block = scratch_ref[b * half : (b + 1) * half, :].astype(BF16)
            blocks.append(spread_rows(block, low))
            moments.append(moment_ref[b])
        m_branch = dot_t(jnp.concatenate(moments, axis=1), jnp.concatenate(blocks, axis=1)).astype(BF16)
        matrix = branch_ref[pl.ds(c, rank, stride=branches), :][:, :rank].astype(BF16)
        m_device = m_device + dot_t(m_branch, matrix)
        spread = twice(m_branch)
        source = stack_rows([r[c : c + 1, :] for r in rows]).astype(BF16)
        if c % 2 == 1:
            q = c // 2
            out_ref[q * rhs : (q + 1) * rhs, :] = pair(low_m, previous[0], spread)
            out_ref[base + q * ROWS : base + (q + 1) * ROWS, :] = pair(low_r, previous[1], source)
        previous = spread, source
    base = base + branches // 2 * ROWS
    m_device = m_device.astype(BF16)
    share = dot_t(m_device, up_device_ref[...]).astype(BF16)
    out_ref[base : base + rhs, :] = jnp.concatenate([m_device, share], axis=1)
    rows = source_rows(*[twice(pdevice_ref[c : c + 1, :].astype(F32)) for c in range(3)])
    out_ref[base + rhs :, :] = stack_rows(rows).astype(BF16)
    return share


def turn_kernel(down_leaf_ref, far_ref, _, down_ref, turned_ref, scratch_ref):
    turned_ref[...] = jnp.transpose(far_ref[...].astype(F32)).astype(jnp.int32)
    relayout(down_leaf_ref, scratch_ref)
    down_ref[...] = scratch_ref[...].astype(BF16)


def point_rows(points):
    return stack_rows(source_rows(*[points[c : c + 1, :] for c in range(3)]))


def near_weights(near_ref, size, weight_ref):
    near = near_ref[...]
    leaves = near.shape[1]
    reach = weight_ref.shape[2]
    span = 2 * REACH + 1
    counts = [jnp.sum((near == o - REACH).astype(F32), axis=0, keepdims=True) for o in range(span)]
    counts = jnp.concatenate(counts + [jnp.zeros((2 * ROWS - span, leaves), F32)], axis=0).astype(BF16)
    offset = lax.broadcasted_iota(jnp.int32, (2 * ROWS, reach), 0)
    block = lax.broadcasted_iota(jnp.int32, (2 * ROWS, reach), 1) // size
    for h in range(2):
        weight_ref[h] = dot_0(counts, (block == offset + h).astype(BF16))


def near_couplings(target, source, weights, kern_ref):
    kern = kern_of(dot_0(target, source))
    size, reach = kern.shape[0] // 2, kern.shape[1]
    for h in range(2):
        weight = jnp.broadcast_to(weights[h], (2 * ROWS, reach)).astype(BF16)
        for s in range(h * size, (h + 1) * size, 2 * ROWS):
            kern_ref[s : s + 2 * ROWS, :] = kern[s : s + 2 * ROWS, :] * weight


def near_kernel(
    near_ref, charges_ref, points_ref, _, out_ref, source_ref, target_ref, weight_ref, kern_a_ref, kern_b_ref
):
    rhs, total = charges_ref.shape
    size = total // near_ref.shape[1]
    halo = REACH * size
    lanes = 2 * size
    reach = weight_ref.shape[2]
    rows = point_rows(points_ref[...].astype(F32))
    source_ref[...] = jnp.concatenate([rows.astype(BF16), source_tail(total)], axis=0)
    target_ref[...] = target_of(rows)
    near_weights(near_ref, size, weight_ref)
    out_ref[:, :halo] = jnp.zeros((rhs, halo), F32)
    out_ref[:, total - halo :] = jnp.zeros((rhs, halo), F32)
    width = kern_a_ref.shape[0]
    first = halo // lanes
    rounds = (total - 2 * halo) // lanes // width

    def evaluate(i, n, kern_ref):
        j = first + i * width + n
        start = pl.multiple_of(j * lanes, lanes)
        near_couplings(
            target_ref[:, pl.ds(start, lanes)],
            source_ref[:, pl.ds(pl.multiple_of(start - halo, lanes), reach)],
            [weight_ref[h, pl.ds(2 * j + h, 1), :] for h in range(2)],
            kern_ref.at[n],
        )

    def apply(i, n, kern_ref):
        start = pl.multiple_of((first + i * width + n) * lanes, lanes)
        columns = pl.ds(pl.multiple_of(start - halo, lanes), reach)
        out_ref[:, pl.ds(start, lanes)] = dot_t(charges_ref[:, columns], kern_ref[n])

    for n in range(width):
        evaluate(0, n, kern_a_ref)

    def step(t, carry):
        for n in range(width):
            evaluate(2 * t + 1, n, kern_b_ref)
            apply(2 * t, n, kern_a_ref)
        for n in range(width):
            evaluate(jnp.minimum(2 * t + 2, rounds - 1), n, kern_a_ref)
            apply(2 * t + 1, n, kern_b_ref)
        return carry

    lax.fori_loop(0, rounds // 2, step, 0)


def edge_pairs(near_ref, ends_ref, end_points_ref, inner_ref, outer_ref, out_ref, weight_ref, kern_ref):
    rhs = ends_ref.shape[1]
    leaves = near_ref.shape[1]
    halo = out_ref.shape[1] // 2
    lanes = inner_ref.shape[1]
    size = lanes // 2
    count = halo // lanes
    reach = weight_ref.shape[2]
    odd = lax.rem(lax.axis_index("dev"), 2) == 1
    near_weights(near_ref, size, weight_ref)
    inner, outer = inner_ref[...], outer_ref[...]
    height = inner.shape[0] // count
    for side, block in enumerate((jnp.where(odd, inner, outer), jnp.where(odd, outer, inner))):
        beyond = jnp.concatenate([block[n * height : (n + 1) * height, :] for n in range(count)], axis=1)
        parts = [(beyond[:rhs, :], beyond[rhs : rhs + 3, :].astype(F32)), (ends_ref[side], end_points_ref[side].astype(F32))]
        parts = parts if side == 0 else parts[::-1]
        wide = jnp.concatenate([p[0] for p in parts], axis=1)
        rows = point_rows(jnp.concatenate([p[1] for p in parts], axis=1))
        source = jnp.concatenate([rows.astype(BF16), source_tail(rows.shape[1])], axis=0)
        target = target_of(rows[:, halo : 2 * halo])
        for j in range(count):
            leaf = 2 * j + side * (leaves - 2 * count)
            place = side * count + j
            near_couplings(
                target[:, j * lanes : (j + 1) * lanes],
                source[:, j * lanes : j * lanes + reach],
                [weight_ref[h, leaf + h : leaf + h + 1, :] for h in range(2)],
                kern_ref.at[place],
            )
            columns = slice(place * lanes, (place + 1) * lanes)
            out_ref[:, columns] = dot_t(wide[:, j * lanes : j * lanes + reach], kern_ref[place])


def put_pair(ref, slot, tile, row=0):
    low = low_half(tile.shape)
    other = swap(tile)
    ref[slot, row : row + tile.shape[0], :] = pair(low, tile, other)
    ref[slot + 1, row : row + tile.shape[0], :] = pair(low, other, tile)


def part_of(parts, s, members):
    length = parts[0].shape[0] // 2
    owner = lax.axis_index("dev") ^ (s // 2 + s % 2 * (members // 2))
    return parts[s // 2].at[s % 2 * length : (s % 2 + 1) * length], owner


def group_kernel(*refs, members):
    far_ref = refs[0]
    count = members // 2
    parts = refs[1 : 1 + count]
    fb_ref, ld_ref = refs[1 + count : 3 + count]
    moment_ref, source_ref, dev_m_ref, dev_source_ref = refs[3 + count :]
    branches, entries = far_ref.shape
    rhs, rank2 = moment_ref.shape[1:]
    rank = rank2 // 2
    me = lax.axis_index("dev")
    low = low_half((rhs, rank2))
    tail = source_tail(rank2)
    first = branches // 2 * rhs
    base = first + branches // 2 * ROWS
    for s in range(members):
        part, owner = part_of(parts, s, members)
        for q in range(branches // 2):
            put_pair(moment_ref, owner * branches + 2 * q, part[q * rhs : (q + 1) * rhs, :])
            put_pair(source_ref, owner * branches + 2 * q, part[first + q * ROWS : first + (q + 1) * ROWS, :])
        mixed = part[base : base + rhs, :].astype(F32)
        keep = (jnp.abs(owner - me) >= 2).astype(F32)
        dev_m_ref[owner] = (pair(low, mixed, pltpu.roll(mixed, rank, 1)) * keep).astype(BF16)
        dev_source_ref[owner] = part[base + rhs :, :]
    for c in range(branches):
        target = target_of(source_ref[me * branches + c][:, :rank])
        fb_ref[c] = interact(target, [far_ref[c, e] for e in range(entries)], source_ref, tail, moment_ref)
    target = target_of(dev_source_ref[me][:, :rank])
    ld_ref[...] = interact(target, list(range(members)), dev_source_ref, tail, dev_m_ref)


def downward_kernel(*refs, groups):
    far_ref = refs[0]
    (
        fb_ref, ld_ref, down_device_ref, down_branch_ref, down_ref, own_ref, own_m_ref, recv_ref, basis_ref, near_ref,
        list_ref, charges_hbm, points_hbm, inner_ref, outer_ref, out_ref, edge_ref, ends_ref, end_points_ref, weight_ref,
        edge_kern_ref, sems, table_ref, grp_m_ref, grp_source_ref, branch_ref, parent_ref, *buffers,
    ) = refs[1:]
    leaves, entries = far_ref.shape
    rhs, rank2 = parent_ref.shape[1:]
    rank = rank2 // 2
    half = rank // 2
    branches = leaves // FAN
    devices = recv_ref.shape[0]
    slots = (table_ref.shape[0] - leaves) // devices
    columns_all, width = charges_hbm.shape[1], ends_ref.shape[2]
    copies = []
    for side in range(2):
        columns = slice(side * (columns_all - width), side * (columns_all - width) + width)
        copies.append(fetch(charges_hbm.at[:, columns], ends_ref.at[side], sems.at[2 * side]))
        copies.append(fetch(points_hbm.at[:, columns], end_points_ref.at[side], sems.at[2 * side + 1]))
    me = lax.axis_index("grp")
    low = low_half((rhs, rank2))
    tail = source_tail(rank2)

    base = slots // 2 * rhs
    members = devices // groups
    low_g = low_half((ROWS, rank2))
    for g in range(groups):
        total = jnp.zeros((rhs // 2, rank2), F32)
        for p in range(g * members, (g + 1) * members):
            total = total + recv_ref[p, base + ROWS :, :].astype(F32)
        total = jnp.concatenate([total[:, :rank], total[:, rank:]], axis=0).astype(BF16).astype(F32)
        keep = (jnp.abs(g - me) >= 2).astype(F32)
        grp_m_ref[g] = twice(total * keep).astype(BF16)
        tile = recv_ref[g * members, base : base + ROWS, :].astype(F32)
        other = pltpu.roll(tile, rank, 1)
        left, right = pair(low_g, tile, other), pair(low_g, other, tile)
        x, y, z = left[ROWS - 2 : ROWS - 1, :], right[ROWS - 2 : ROWS - 1, :], left[ROWS - 1 :, :]
        rows = (x, y, z) + three(0.25 * (x * x + y * y + z * z))
        grp_source_ref[g] = stack_rows(rows).astype(BF16)
    target = target_of(grp_source_ref[me][:, :rank])
    l_group = interact(target, list(range(groups)), grp_source_ref, tail, grp_m_ref).astype(BF16)
    l_device = (ld_ref[...] + dot_t(l_group, down_device_ref[...])).astype(BF16)
    branch_ref[...] = twice(down_branch_ref[...].astype(F32).reshape(rank * branches, rank))
    for c in range(branches):
        matrix = branch_ref[pl.ds(c, rank, stride=branches), :][:, :rank].astype(BF16)
        parent_ref[c] = twice((fb_ref[c] + dot_t(l_device, matrix)).astype(BF16))

    for copy in copies:
        copy.wait()
    edge_pairs(list_ref, ends_ref, end_points_ref, inner_ref, outer_ref, edge_ref, weight_ref, edge_kern_ref)

    table_ref[:leaves, :rhs, :] = own_m_ref[...]
    table_ref[:leaves, rhs:, :] = own_ref[...]
    base = slots // 2 * rhs

    row = lax.broadcasted_iota(jnp.int32, (ROWS, rank2), 0)
    low_r = low_half((ROWS, rank2))
    zero = jnp.zeros((ROWS, rank2), F32)

    def unpack(p, carry):
        tile = recv_ref[p, base : base + ROWS, :].astype(F32)
        squares = 0.25 * tile * tile
        parts = three(squares + pltpu.roll(squares, ROWS - 1, 0) + pltpu.roll(squares, ROWS - 2, 0))
        for q in range(slots // 2):
            slot = leaves + p * slots + 2 * q
            put_pair(table_ref, slot, recv_ref[p, q * rhs : (q + 1) * rhs, :], 0)
            rows = jnp.where(row < 3, pltpu.roll(tile, ROWS - 3, 0) if q else tile, zero)
            for n, part in enumerate(parts):
                shift = 3 + n - 3 * q
                rows = jnp.where(row == 3 + n, pltpu.roll(part, shift, 0) if shift else part, rows)
            other = pltpu.roll(rows, rank, 1)
            table_ref[slot, rhs:, :] = pair(low_r, rows, other).astype(BF16)
            table_ref[slot + 1, rhs:, :] = pair(low_r, other, rows).astype(BF16)
        return carry

    lax.fori_loop(0, devices, unpack, 0, unroll=min(devices, 32))
    low_d = low_half((half, rank2))

    width = buffers[0].shape[0]
    rounds = leaves // width
    low_s = low_half((ROWS, rank2))

    def gather(b, low, rows, ref):
        for e in range(0, entries, 2):
            first, second = far_ref[b, e], far_ref[b, e + 1]
            ref[:, e * rank : (e + 2) * rank] = pair(low, table_ref[first, rows, :], table_ref[second, rows, :])

    def collect_sources(i, h, targets_ref, sources_ref):
        b = width * i + h
        targets_ref[h] = jnp.transpose(target_of(table_ref[b, rhs:, :rank]))
        gather(b, low_s, slice(rhs, None), sources_ref.at[h])

    def collect_moments(i, h, moments_ref):
        gather(width * i + h, low, slice(None, rhs), moments_ref.at[h])

    def evaluate(h, targets_ref, sources_ref, kern_ref):
        sources = jnp.concatenate([sources_ref[h], source_tail(sources_ref.shape[2])], axis=0)
        kern_ref[h] = kern_of(dot(targets_ref[h], sources))

    def apply(i, h, moments_ref, kern_ref):
        b = width * i + h
        far = dot_t(moments_ref[h], kern_ref[h])
        rows = down_ref[pl.ds(pl.multiple_of(b * half, half), half), :]
        return (far + dot_t(parent_ref[b // FAN], spread_rows(rows, low_d))).astype(BF16)

    def finish(i, sums, starts=None):
        for h in starts or range(0, width, 2):
            columns = pl.ds(pl.multiple_of((width * i + h) * rank, rank2), rank2)
            product = dot(jnp.concatenate(sums[h : h + 2], axis=0), basis_ref[:, columns])
            out_ref[:, columns] = near_ref[:, columns] + pair(low, product[:rhs], product[rhs:])

    def stage(i, sums, this, other):
        done, last = jnp.maximum(i - 2, 0), sums
        before, after, later = jnp.maximum(i - 1, 0), jnp.minimum(i + 1, rounds - 1), jnp.minimum(i + 2, rounds - 1)
        sums = []
        for h in range(width):
            evaluate(h, this[0], this[1], this[3])
            sums.append(apply(before, h, other[2], other[3]))
            if h % 2 == 0:
                finish(done, last, (h,))
            collect_sources(later, h, this[0], this[1])
            collect_moments(after, h, other[2])
        return tuple(sums)

    even, odd = buffers[:4], buffers[4:]
    for h in range(width):
        collect_sources(0, h, *even[:2])
        collect_sources(1, h, *odd[:2])
        collect_moments(0, h, even[2])
    odd[2][...] = jnp.zeros_like(odd[2])
    odd[3][...] = jnp.zeros_like(odd[3])

    def step(t, sums):
        return stage(2 * t + 1, stage(2 * t, sums, even, odd), odd, even)

    sums = lax.fori_loop(0, rounds // 2, step, (jnp.zeros((rhs, rank), BF16),) * width)
    finish(rounds - 2, sums)
    finish(rounds - 1, tuple(apply(rounds - 1, h, odd[2], odd[3]) for h in range(width)))
    total, halo = out_ref.shape[1], edge_ref.shape[1] // 2
    out_ref[:, :halo] += edge_ref[:, :halo]
    out_ref[:, total - halo :] += edge_ref[:, halo:]


VMEM = functools.partial(pl.BlockSpec, memory_space=pltpu.VMEM)
SMEM = functools.partial(pl.BlockSpec, memory_space=pltpu.SMEM)
ANY = functools.partial(pl.BlockSpec, memory_space=pl.ANY)
PARAMS = pltpu.CompilerParams()


def hbm(shape, dtype):
    return jax.ShapeDtypeStruct(shape, dtype)


def vmem(*arrays):
    return [pltpu.with_memory_space_constraint(a, pltpu.VMEM) if a.size <= 1 << 19 else a for a in arrays]


def on_device(
    charges, points, basis, up_leaf, up_branch, up_device, down_leaf, down_branch, down_device,
    proxy_leaf, proxy_branch, proxy_device, proxy_group, far_leaf, send_leaf, far_branch, near_leaf,
):
    rhs, total = charges.shape
    rank = basis.shape[0]
    leaves = up_leaf.shape[2]
    size = total // leaves
    branches = leaves // FAN
    slots = send_leaf.shape[0]
    groups = lax.axis_size("grp")
    members = lax.axis_size("dev")
    devices = groups * members
    rank2 = 2 * rank
    half = rank // 2
    halo = REACH * size
    assert rank == size and slots == 4 and branches % 2 == 0 and members % 2 == 0

    moments, own, listed, inner, outer, shared = pl.pallas_call(
        upward_kernel,
        out_shape=(
            pltpu.VMEM((leaves, rhs, rank2), BF16),
            hbm((leaves, ROWS, rank2), BF16),
            hbm((devices, slots // 2 * rhs + ROWS + rhs // 2, rank2), BF16),
            pltpu.VMEM((halo // rank2 * (rhs + ROWS), rank2), BF16),
            pltpu.VMEM((halo // rank2 * (rhs + ROWS), rank2), BF16),
            hbm(((branches // 2 + 1) * (rhs + ROWS), rank2), BF16),
        ),
        in_specs=[SMEM()] + [VMEM()] * 4 + [ANY()] + [VMEM()] * 5,
        out_specs=(VMEM(),) * 6,
        scratch_shapes=[
            pltpu.VMEM((leaves * ROWS, rank2), F32),
            pltpu.VMEM((leaves * ROWS, rank2), F32),
            pltpu.VMEM(up_leaf.shape, BF16),
            pltpu.VMEM((leaves * half, rank2), F32),
            pltpu.VMEM((rank * branches, rank2), F32),
            pltpu.SemaphoreType.DMA(()),
        ],
        compiler_params=PARAMS,
        name="upward",
    )(
        send_leaf,
        charges,
        points,
        basis,
        proxy_leaf,
        up_leaf,
        jnp.transpose(up_branch, (0, 2, 1)),
        up_device[:, :, 0],
        jnp.transpose(proxy_branch, (0, 2, 1)),
        proxy_device[:, :, 0],
        proxy_group[:, :, 0],
    )
    (moments,) = vmem(moments)
    received = lax.all_to_all(listed, ("grp", "dev"), split_axis=0, concat_axis=0, tiled=True)

    partner = lax.ppermute(shared, "dev", [(i, i ^ members // 2) for i in range(members)])
    down, far_turned = pl.pallas_call(
        turn_kernel,
        out_shape=(hbm((leaves * half, rank2), BF16), hbm(far_leaf.shape[::-1], jnp.int32)),
        in_specs=[VMEM(), VMEM(), ANY()],
        out_specs=(VMEM(), VMEM()),
        scratch_shapes=[pltpu.VMEM((leaves * half, rank2), F32)],
        compiler_params=PARAMS,
        name="turn",
    )(down_leaf, far_leaf, shared)
    partner, down = lax.optimization_barrier((partner, down))
    both = jnp.concatenate([shared, partner], axis=0)
    parts = [both]
    for s in range(1, members // 2):
        parts.append(lax.ppermute(both, "dev", [(i, i ^ s) for i in range(members)]))

    reach = (2 * REACH + 2) * size
    near = pl.pallas_call(
        near_kernel,
        out_shape=pltpu.VMEM((rhs, total), F32),
        in_specs=[VMEM()] * 4,
        out_specs=VMEM(),
        scratch_shapes=[
            pltpu.VMEM((2 * ROWS, total), BF16),
            pltpu.VMEM((2 * ROWS, total), BF16),
            pltpu.VMEM((2, leaves, reach), F32),
            pltpu.VMEM((PAIRS, 2 * size, reach), BF16),
            pltpu.VMEM((PAIRS, 2 * size, reach), BF16),
        ],
        compiler_params=PARAMS,
        name="near",
    )(near_leaf, charges, points, *vmem(both))

    swaps = [(i, i + 1 if i % 2 else i - 1) for i in range(1, devices - 1)]
    inner, outer, near = lax.optimization_barrier((inner, outer, near))
    outer = lax.ppermute(outer, ("grp", "dev"), swaps)
    inner = lax.ppermute(inner, "dev", [(i, i ^ 1) for i in range(members)])

    parts = vmem(*parts)
    assert members & (members - 1) == 0
    far_b, part_d = pl.pallas_call(
        functools.partial(group_kernel, members=members),
        out_shape=(hbm((branches, rhs, rank), F32), hbm((rhs, rank), F32)),
        in_specs=[SMEM()] + [VMEM()] * len(parts),
        out_specs=(VMEM(),) * 2,
        scratch_shapes=[
            pltpu.VMEM((members * branches, rhs, rank2), BF16),
            pltpu.VMEM((members * branches, ROWS, rank2), BF16),
            pltpu.VMEM((members, rhs, rank2), BF16),
            pltpu.VMEM((members, ROWS, rank2), BF16),
        ],
        compiler_params=PARAMS,
        name="group",
    )(jnp.transpose(far_branch), *parts)

    table = leaves + devices * slots
    return pl.pallas_call(
        functools.partial(downward_kernel, groups=groups),
        out_shape=hbm((rhs, total), F32),
        in_specs=[SMEM()] + [VMEM()] * 11 + [ANY(), ANY(), VMEM(), VMEM()],
        out_specs=VMEM(),
        scratch_shapes=[
            pltpu.VMEM((rhs, 2 * halo), F32),
            pltpu.VMEM((2, rhs, 2 * halo), BF16),
            pltpu.VMEM((2, 3, 2 * halo), BF16),
            pltpu.VMEM((2, leaves, reach), F32),
            pltpu.VMEM((REACH, 2 * size, reach), BF16),
            pltpu.SemaphoreType.DMA((4,)),
            pltpu.VMEM((table, rhs + ROWS, rank2), BF16),
            pltpu.VMEM((groups, rhs, rank2), BF16),
            pltpu.VMEM((groups, ROWS, rank2), BF16),
            pltpu.VMEM((rank * branches, rank2), F32),
            pltpu.VMEM((branches, rhs, rank2), BF16),
        ]
        + [
            pltpu.VMEM((ROUND, rank, 2 * ROWS), BF16),
            pltpu.VMEM((ROUND, ROWS, far_leaf.shape[0] * rank), BF16),
            pltpu.VMEM((ROUND, rhs, far_leaf.shape[0] * rank), BF16),
            pltpu.VMEM((ROUND, rank, far_leaf.shape[0] * rank), BF16),
        ]
        * 2,
        compiler_params=PARAMS,
        name="downward",
    )(
        far_turned,
        far_b,
        part_d,
        down_device[:, :, 0],
        jnp.transpose(down_branch, (0, 2, 1)),
        down,
        own,
        moments,
        *vmem(received),
        basis,
        *vmem(near),
        near_leaf,
        charges,
        points,
        *vmem(inner, outer),
    )


def solution(mesh):
    points = P(None, ("grp", "dev"))
    blocks = P(None, None, ("grp", "dev"))
    placed = (points,) * 3 + (blocks,) * 9 + (P(None, None, "grp"),) + (points,) * 4

    return jax.shard_map(on_device, mesh=mesh, in_specs=placed, out_specs=points, check_vma=False)
```

```python
import functools
import math

import jax
import jax.numpy as jnp
from jax import lax
from jax.experimental import pallas as pl
from jax.experimental.pallas import tpu as pltpu
from jax.sharding import PartitionSpec as P

REACH = 4
FAN = 8
ROUND = 8
PAIRS = 7

INV_FOUR_PI = 1.0 / (4.0 * math.pi)
SOFTEN = 0.25
ROWS = 8

BF16 = jnp.bfloat16
F32 = jnp.float32


def dot(a, b):
    return jnp.dot(a, b, preferred_element_type=F32)


def dot_t(a, b):
    return lax.dot_general(a, b, (((1,), (1,)), ((), ())), preferred_element_type=F32)


def dot_0(a, b):
    return lax.dot_general(a, b, (((0,), (0,)), ((), ())), preferred_element_type=F32)


def fetch(source, target, sem):
    copy = pltpu.make_async_copy(source, target, sem)
    copy.start()
    return copy


def low_half(shape):
    width = shape[-1]
    return lax.broadcasted_iota(jnp.int32, shape, len(shape) - 1) < width // 2


def pair(low, first, second):
    return jnp.where(low, first, second)


def swap(tile):
    half = tile.shape[-1] // 2
    return jnp.concatenate([tile[..., half:], tile[..., :half]], axis=-1)


def twice(tile):
    return jnp.concatenate([tile, tile], axis=-1)


def three(value):
    first = value.astype(BF16).astype(F32)
    rest = value - first
    second = rest.astype(BF16).astype(F32)
    return first, second, rest - second


def source_rows(x, y, z):
    return (-2.0 * x, -2.0 * y, -2.0 * z) + three(x * x + y * y + z * z)


def row_mask(shape, rows):
    row = lax.broadcasted_iota(jnp.int32, shape, 0)
    found = row == rows[0]
    for r in rows[1:]:
        found = found | (row == r)
    return found.astype(F32)


def source_tail(width):
    return row_mask((ROWS, width), (3, 4, 5, 6)).astype(BF16)


def target_of(rows):
    rows = rows.astype(F32)
    shape = rows.shape
    squares = row_mask(shape, (3, 4, 5))
    upper = rows * (-0.5 * row_mask(shape, (0, 1, 2))) + squares
    lower = rows * squares + SOFTEN * row_mask(shape, (6,))
    return jnp.concatenate([upper, lower], axis=0).astype(BF16)


def put_rows(ref, rows, count, first=0):
    for f in range(ROWS):
        value = rows[f - first] if 0 <= f - first < len(rows) else jnp.zeros_like(rows[0])
        ref[pl.ds(f, count, stride=ROWS), :] = value


def stack_rows(rows):
    n = rows[0].shape[1]
    return jnp.concatenate(tuple(rows) + (jnp.zeros((ROWS - len(rows), n), F32),), axis=0)


def couplings(target, slots, source_ref, tail):
    low = low_half(source_ref.shape[1:])
    tiles = [
        jnp.concatenate([pair(low, source_ref[first], source_ref[second]), tail], axis=0)
        for first, second in zip(slots[0::2], slots[1::2])
    ]
    return kern_of(dot_0(target, jnp.concatenate(tiles, axis=1)))


def kern_of(square):
    return (INV_FOUR_PI * lax.rsqrt(square)).astype(BF16)


def gathered(slots, moment_ref):
    low = low_half(moment_ref.shape[1:])
    tiles = [pair(low, moment_ref[first], moment_ref[second]) for first, second in zip(slots[0::2], slots[1::2])]
    return jnp.concatenate(tiles, axis=1)


def interact(target, slots, source_ref, tail, moment_ref):
    return dot_t(gathered(slots, moment_ref), couplings(target, slots, source_ref, tail))


def upward_kernel(
    send_ref, charges_ref, points_ref, basis_ref, proxy_ref, up_leaf_hbm, up_branch_ref, up_device_ref, pbranch_ref,
    pdevice_ref, pgroup_ref, moment_ref, own_ref, out_ref, inner_ref, outer_ref, shared_ref, tile_ref, late_ref, up_leaf_ref,
    scratch_ref, branch_ref, sem,
):
    slots, devices = send_ref.shape
    leaves, rhs, rank2 = moment_ref.shape
    transfers = fetch(up_leaf_hbm, up_leaf_ref, sem)
    low = low_half((rhs, rank2))
    rows = source_rows(*[twice(jnp.transpose(proxy_ref[c].astype(F32))) for c in range(3)])
    put_rows(tile_ref, rows, leaves)
    own_ref[...] = tile_ref[...].astype(BF16).reshape(own_ref.shape)
    put_rows(tile_ref, rows[:3], leaves)
    put_rows(late_ref, rows[:3], leaves, 3)

    def leaf_pair(i, carry):
        columns = pl.ds(pl.multiple_of(i * rank2, rank2), rank2)
        q = charges_ref[:, columns]
        u = basis_ref[:, columns]
        zero = jnp.zeros_like(q)
        stacked = jnp.concatenate([jnp.where(low, q, zero), jnp.where(low, zero, q)], axis=0)
        product = dot_t(stacked, jnp.concatenate([u, u], axis=0)).astype(BF16)
        moment_ref[2 * i] = product[:rhs]
        moment_ref[2 * i + 1] = product[rhs:]
        return carry

    lax.fori_loop(0, leaves // 2, leaf_pair, 0, unroll=8)
    transfers.wait()
    share = raise_moments(
        moment_ref, up_leaf_ref, up_branch_ref, up_device_ref, pbranch_ref, pdevice_ref, shared_ref, scratch_ref, branch_ref
    )
    share = jnp.concatenate([share[: rhs // 2], share[rhs // 2 :]], axis=1)
    gx, gy, gz = (-2.0 * pgroup_ref[c : c + 1, :].astype(F32) for c in range(3))
    group_rows = [jnp.concatenate([gx, gy], axis=1), jnp.concatenate([gz, jnp.zeros_like(gz)], axis=1)]
    group_rows = jnp.concatenate([jnp.zeros((ROWS - 2, rank2), F32)] + group_rows, axis=0)
    low8 = low_half((ROWS, rank2))
    base = slots // 2 * rhs

    def pack(p, carry):
        s = [send_ref[t, p] for t in range(slots)]
        tiles = []
        for q in range(slots // 2):
            first, second = s[2 * q], s[2 * q + 1]
            out_ref[p, q * rhs : (q + 1) * rhs, :] = pair(low, moment_ref[first], moment_ref[second])
            ref = (tile_ref, late_ref)[q]
            tiles.append(
                pair(
                    low8,
                    ref[pl.ds(pl.multiple_of(first * ROWS, ROWS), ROWS), :],
                    ref[pl.ds(pl.multiple_of(second * ROWS, ROWS), ROWS), :],
                )
            )
        out_ref[p, base : base + ROWS, :] = (tiles[0] + tiles[1] + group_rows).astype(BF16)
        out_ref[p, base + ROWS :, :] = share
        return carry

    lax.fori_loop(0, devices, pack, 0, unroll=4)
    total = charges_ref.shape[1]
    halo = inner_ref.shape[0] // (rhs + ROWS) * rank2
    odd = lax.rem(lax.axis_index("dev"), 2) == 1
    for ref, first in ((inner_ref, odd), (outer_ref, jnp.logical_not(odd))):
        start = jnp.where(first, 0, total - halo)
        for n in range(halo // rank2):
            columns = pl.ds(pl.multiple_of(start + n * rank2, rank2), rank2)
            base = n * (rhs + ROWS)
            ref[base : base + rhs, :] = charges_ref[:, columns]
            points = points_ref[:, columns].astype(F32)
            rows = jnp.concatenate([points, jnp.zeros((ROWS - 3, rank2), F32)], axis=0)
            ref[base + rhs : base + rhs + ROWS, :] = rows.astype(BF16)


def relayout(x_ref, scratch_ref):
    rank, _, leaves = x_ref.shape
    half = rank // 2
    eye = (
        lax.broadcasted_iota(jnp.int32, (leaves, leaves), 0)
        == lax.broadcasted_iota(jnp.int32, (leaves, leaves), 1)
    ).astype(BF16)
    for k in range(0, half, 2):
        block = jnp.concatenate(
            [x_ref[k], x_ref[k + half], x_ref[k + 1], x_ref[k + 1 + half]], axis=0
        )
        turned = dot_t(eye, block)
        for n in range(2):
            scratch_ref[pl.ds(k + n, leaves, stride=half), :] = turned[:, n * 2 * rank : (n + 1) * 2 * rank]


def spread_rows(block, low):
    zero = jnp.zeros_like(block)
    return jnp.concatenate([jnp.where(low, block, zero), jnp.where(low, zero, block)], axis=0)


def raise_moments(
    moment_ref, up_leaf_ref, up_branch_ref, up_device_ref, pbranch_ref, pdevice_ref, out_ref, scratch_ref, branch_ref
):
    leaves, rhs, rank2 = moment_ref.shape
    rank = rank2 // 2
    half = rank // 2
    branches = leaves // FAN
    relayout(up_leaf_ref, scratch_ref)
    low = low_half((half, rank2))
    low_m = low_half((rhs, rank2))
    low_r = low_half((ROWS, rank2))
    wide = up_branch_ref[...].astype(F32).reshape(rank * branches, rank)
    branch_ref[...] = twice(wide)
    rows = source_rows(*[twice(pbranch_ref[c].astype(F32)) for c in range(3)])
    m_device = jnp.zeros((rhs, rank), F32)
    previous = None
    base = branches // 2 * rhs
    for c in range(branches):
        blocks, moments = [], []
        for b in range(c * FAN, (c + 1) * FAN):
            block = scratch_ref[b * half : (b + 1) * half, :].astype(BF16)
            blocks.append(spread_rows(block, low))
            moments.append(moment_ref[b])
        m_branch = dot_t(jnp.concatenate(moments, axis=1), jnp.concatenate(blocks, axis=1)).astype(BF16)
        matrix = branch_ref[pl.ds(c, rank, stride=branches), :][:, :rank].astype(BF16)
        m_device = m_device + dot_t(m_branch, matrix)
        spread = twice(m_branch)
        source = stack_rows([r[c : c + 1, :] for r in rows]).astype(BF16)
        if c % 2 == 1:
            q = c // 2
            out_ref[q * rhs : (q + 1) * rhs, :] = pair(low_m, previous[0], spread)
            out_ref[base + q * ROWS : base + (q + 1) * ROWS, :] = pair(low_r, previous[1], source)
        previous = spread, source
    base = base + branches // 2 * ROWS
    m_device = m_device.astype(BF16)
    share = dot_t(m_device, up_device_ref[...]).astype(BF16)
    out_ref[base : base + rhs, :] = jnp.concatenate([m_device, share], axis=1)
    rows = source_rows(*[twice(pdevice_ref[c : c + 1, :].astype(F32)) for c in range(3)])
    out_ref[base + rhs :, :] = stack_rows(rows).astype(BF16)
    return share


def turn_kernel(down_leaf_ref, far_ref, _, down_ref, turned_ref, scratch_ref):
    turned_ref[...] = jnp.transpose(far_ref[...].astype(F32)).astype(jnp.int32)
    relayout(down_leaf_ref, scratch_ref)
    down_ref[...] = scratch_ref[...].astype(BF16)


def point_rows(points):
    return stack_rows(source_rows(*[points[c : c + 1, :] for c in range(3)]))


def near_weights(near_ref, size, weight_ref):
    near = near_ref[...]
    leaves = near.shape[1]
    reach = weight_ref.shape[2]
    span = 2 * REACH + 1
    counts = [jnp.sum((near == o - REACH).astype(F32), axis=0, keepdims=True) for o in range(span)]
    counts = jnp.concatenate(counts + [jnp.zeros((2 * ROWS - span, leaves), F32)], axis=0).astype(BF16)
    offset = lax.broadcasted_iota(jnp.int32, (2 * ROWS, reach), 0)
    block = lax.broadcasted_iota(jnp.int32, (2 * ROWS, reach), 1) // size
    for h in range(2):
        weight_ref[h] = dot_0(counts, (block == offset + h).astype(BF16))


def near_couplings(target, source, weights, kern_ref):
    kern = kern_of(dot_0(target, source))
    size, reach = kern.shape[0] // 2, kern.shape[1]
    for h in range(2):
        weight = jnp.broadcast_to(weights[h], (2 * ROWS, reach)).astype(BF16)
        for s in range(h * size, (h + 1) * size, 2 * ROWS):
            kern_ref[s : s + 2 * ROWS, :] = kern[s : s + 2 * ROWS, :] * weight


def near_kernel(
    near_ref, charges_ref, points_ref, _, out_ref, edge_ref, source_ref, target_ref, weight_ref, kern_a_ref, kern_b_ref
):
    rhs, total = charges_ref.shape
    size = total // near_ref.shape[1]
    halo = REACH * size
    lanes = 2 * size
    reach = weight_ref.shape[2]
    rows = point_rows(points_ref[...].astype(F32))
    source_ref[...] = jnp.concatenate([rows.astype(BF16), source_tail(total)], axis=0)
    target_ref[...] = target_of(rows)
    near_weights(near_ref, size, weight_ref)
    edge_ref[:, :REACH, :] = weight_ref[:, :REACH, :]
    edge_ref[:, REACH:, :] = weight_ref[:, weight_ref.shape[1] - REACH :, :]
    out_ref[:, :halo] = jnp.zeros((rhs, halo), F32)
    out_ref[:, total - halo :] = jnp.zeros((rhs, halo), F32)
    width = kern_a_ref.shape[0]
    first = halo // lanes
    rounds = (total - 2 * halo) // lanes // width

    def evaluate(i, n, kern_ref):
        j = first + i * width + n
        start = pl.multiple_of(j * lanes, lanes)
        near_couplings(
            target_ref[:, pl.ds(start, lanes)],
            source_ref[:, pl.ds(pl.multiple_of(start - halo, lanes), reach)],
            [weight_ref[h, pl.ds(2 * j + h, 1), :] for h in range(2)],
            kern_ref.at[n],
        )

    def apply(i, n, kern_ref):
        start = pl.multiple_of((first + i * width + n) * lanes, lanes)
        columns = pl.ds(pl.multiple_of(start - halo, lanes), reach)
        out_ref[:, pl.ds(start, lanes)] = dot_t(charges_ref[:, columns], kern_ref[n])

    for n in range(width):
        evaluate(0, n, kern_a_ref)

    def step(t, carry):
        for n in range(width):
            evaluate(2 * t + 1, n, kern_b_ref)
            apply(2 * t, n, kern_a_ref)
        for n in range(width):
            evaluate(jnp.minimum(2 * t + 2, rounds - 1), n, kern_a_ref)
            apply(2 * t + 1, n, kern_b_ref)
        return carry

    lax.fori_loop(0, rounds // 2, step, 0)


def edge_pairs(ends_ref, end_points_ref, inner_ref, outer_ref, out_ref, weight_ref, kern_ref):
    rhs = ends_ref.shape[1]
    halo = out_ref.shape[1] // 2
    lanes = inner_ref.shape[1]
    count = halo // lanes
    reach = weight_ref.shape[2]
    odd = lax.rem(lax.axis_index("dev"), 2) == 1
    inner, outer = inner_ref[...], outer_ref[...]
    height = inner.shape[0] // count
    for side, block in enumerate((jnp.where(odd, inner, outer), jnp.where(odd, outer, inner))):
        beyond = jnp.concatenate([block[n * height : (n + 1) * height, :] for n in range(count)], axis=1)
        parts = [(beyond[:rhs, :], beyond[rhs : rhs + 3, :].astype(F32)), (ends_ref[side], end_points_ref[side].astype(F32))]
        parts = parts if side == 0 else parts[::-1]
        wide = jnp.concatenate([p[0] for p in parts], axis=1)
        rows = point_rows(jnp.concatenate([p[1] for p in parts], axis=1))
        source = jnp.concatenate([rows.astype(BF16), source_tail(rows.shape[1])], axis=0)
        target = target_of(rows[:, halo : 2 * halo])
        for j in range(count):
            leaf = 2 * j + side * 2 * count
            place = side * count + j
            near_couplings(
                target[:, j * lanes : (j + 1) * lanes],
                source[:, j * lanes : j * lanes + reach],
                [weight_ref[h, leaf + h : leaf + h + 1, :] for h in range(2)],
                kern_ref.at[place],
            )
            columns = slice(place * lanes, (place + 1) * lanes)
            out_ref[:, columns] = dot_t(wide[:, j * lanes : j * lanes + reach], kern_ref[place])


def put_pair(ref, slot, tile, row=0):
    low = low_half(tile.shape)
    other = swap(tile)
    ref[slot, row : row + tile.shape[0], :] = pair(low, tile, other)
    ref[slot + 1, row : row + tile.shape[0], :] = pair(low, other, tile)


def part_of(parts, s, members):
    length = parts[0].shape[0] // 2
    owner = lax.axis_index("dev") ^ (s // 2 + s % 2 * (members // 2))
    return parts[s // 2].at[s % 2 * length : (s % 2 + 1) * length], owner


def group_kernel(*refs, members):
    far_ref = refs[0]
    count = members // 2
    parts = refs[1 : 1 + count]
    fb_ref, ld_ref = refs[1 + count : 3 + count]
    moment_ref, source_ref, dev_m_ref, dev_source_ref = refs[3 + count :]
    branches, entries = far_ref.shape
    rhs, rank2 = moment_ref.shape[1:]
    rank = rank2 // 2
    me = lax.axis_index("dev")
    low = low_half((rhs, rank2))
    tail = source_tail(rank2)
    first = branches // 2 * rhs
    base = first + branches // 2 * ROWS
    for s in range(members):
        part, owner = part_of(parts, s, members)
        for q in range(branches // 2):
            put_pair(moment_ref, owner * branches + 2 * q, part[q * rhs : (q + 1) * rhs, :])
            put_pair(source_ref, owner * branches + 2 * q, part[first + q * ROWS : first + (q + 1) * ROWS, :])
        mixed = part[base : base + rhs, :].astype(F32)
        keep = (jnp.abs(owner - me) >= 2).astype(F32)
        dev_m_ref[owner] = (pair(low, mixed, pltpu.roll(mixed, rank, 1)) * keep).astype(BF16)
        dev_source_ref[owner] = part[base + rhs :, :]
    for c in range(branches):
        target = target_of(source_ref[me * branches + c][:, :rank])
        fb_ref[c] = interact(target, [far_ref[c, e] for e in range(entries)], source_ref, tail, moment_ref)
    target = target_of(dev_source_ref[me][:, :rank])
    ld_ref[...] = interact(target, list(range(members)), dev_source_ref, tail, dev_m_ref)


def downward_kernel(*refs, groups):
    far_ref = refs[0]
    (
        fb_ref, ld_ref, down_device_ref, down_branch_ref, down_ref, own_ref, own_m_ref, recv_ref, basis_ref, near_ref,
        weight_ref, charges_hbm, points_hbm, inner_ref, outer_ref, out_ref, edge_ref, ends_ref, end_points_ref,
        edge_kern_ref, sems, table_ref, grp_m_ref, grp_source_ref, branch_ref, parent_ref, *buffers,
    ) = refs[1:]
    leaves, entries = far_ref.shape
    rhs, rank2 = parent_ref.shape[1:]
    rank = rank2 // 2
    half = rank // 2
    branches = leaves // FAN
    devices = recv_ref.shape[0]
    slots = (table_ref.shape[0] - leaves) // devices
    columns_all, width = charges_hbm.shape[1], ends_ref.shape[2]
    copies = []
    for side in range(2):
        columns = slice(side * (columns_all - width), side * (columns_all - width) + width)
        copies.append(fetch(charges_hbm.at[:, columns], ends_ref.at[side], sems.at[2 * side]))
        copies.append(fetch(points_hbm.at[:, columns], end_points_ref.at[side], sems.at[2 * side + 1]))
    me = lax.axis_index("grp")
    low = low_half((rhs, rank2))
    tail = source_tail(rank2)

    own_copies = [
        fetch(own_m_ref, table_ref.at[:leaves, :rhs, :], sems.at[4]),
        fetch(own_ref, table_ref.at[:leaves, rhs:, :], sems.at[5]),
    ]

    base = slots // 2 * rhs
    members = devices // groups
    low_g = low_half((ROWS, rank2))
    for g in range(groups):
        total = jnp.zeros((rhs // 2, rank2), F32)
        for p in range(g * members, (g + 1) * members):
            total = total + recv_ref[p, base + ROWS :, :].astype(F32)
        total = jnp.concatenate([total[:, :rank], total[:, rank:]], axis=0).astype(BF16).astype(F32)
        keep = (jnp.abs(g - me) >= 2).astype(F32)
        grp_m_ref[g] = twice(total * keep).astype(BF16)
        tile = recv_ref[g * members, base : base + ROWS, :].astype(F32)
        other = pltpu.roll(tile, rank, 1)
        left, right = pair(low_g, tile, other), pair(low_g, other, tile)
        x, y, z = left[ROWS - 2 : ROWS - 1, :], right[ROWS - 2 : ROWS - 1, :], left[ROWS - 1 :, :]
        rows = (x, y, z) + three(0.25 * (x * x + y * y + z * z))
        grp_source_ref[g] = stack_rows(rows).astype(BF16)
    target = target_of(grp_source_ref[me][:, :rank])
    l_group = interact(target, list(range(groups)), grp_source_ref, tail, grp_m_ref).astype(BF16)
    l_device = (ld_ref[...] + dot_t(l_group, down_device_ref[...])).astype(BF16)
    branch_ref[...] = twice(down_branch_ref[...].astype(F32).reshape(rank * branches, rank))
    for c in range(branches):
        matrix = branch_ref[pl.ds(c, rank, stride=branches), :][:, :rank].astype(BF16)
        parent_ref[c] = twice((fb_ref[c] + dot_t(l_device, matrix)).astype(BF16))

    for copy in copies:
        copy.wait()
    edge_pairs(ends_ref, end_points_ref, inner_ref, outer_ref, edge_ref, weight_ref, edge_kern_ref)

    base = slots // 2 * rhs

    row = lax.broadcasted_iota(jnp.int32, (ROWS, rank2), 0)
    low_r = low_half((ROWS, rank2))
    zero = jnp.zeros((ROWS, rank2), F32)

    def unpack(p, carry):
        tile = recv_ref[p, base : base + ROWS, :].astype(F32)
        squares = 0.25 * tile * tile
        parts = three(squares + pltpu.roll(squares, ROWS - 1, 0) + pltpu.roll(squares, ROWS - 2, 0))
        for q in range(slots // 2):
            slot = leaves + p * slots + 2 * q
            put_pair(table_ref, slot, recv_ref[p, q * rhs : (q + 1) * rhs, :], 0)
            rows = jnp.where(row < 3, pltpu.roll(tile, ROWS - 3, 0) if q else tile, zero)
            for n, part in enumerate(parts):
                shift = 3 + n - 3 * q
                rows = jnp.where(row == 3 + n, pltpu.roll(part, shift, 0) if shift else part, rows)
            other = pltpu.roll(rows, rank, 1)
            table_ref[slot, rhs:, :] = pair(low_r, rows, other).astype(BF16)
            table_ref[slot + 1, rhs:, :] = pair(low_r, other, rows).astype(BF16)
        return carry

    lax.fori_loop(0, devices, unpack, 0, unroll=min(devices, 32))
    for copy in own_copies:
        copy.wait()
    low_d = low_half((half, rank2))

    width = buffers[0].shape[0]
    rounds = leaves // width
    low_s = low_half((ROWS, rank2))

    def gather(b, low, rows, ref):
        for e in range(0, entries, 2):
            first, second = far_ref[b, e], far_ref[b, e + 1]
            ref[:, e * rank : (e + 2) * rank] = pair(low, table_ref[first, rows, :], table_ref[second, rows, :])

    def collect_sources(i, h, targets_ref, sources_ref):
        b = width * i + h
        targets_ref[h] = jnp.transpose(target_of(table_ref[b, rhs:, :rank]))
        gather(b, low_s, slice(rhs, None), sources_ref.at[h])

    def collect_moments(i, h, moments_ref):
        gather(width * i + h, low, slice(None, rhs), moments_ref.at[h])

    def evaluate(h, targets_ref, sources_ref, kern_ref):
        sources = jnp.concatenate([sources_ref[h], source_tail(sources_ref.shape[2])], axis=0)
        kern_ref[h] = kern_of(dot(targets_ref[h], sources))

    def apply(i, h, moments_ref, kern_ref):
        b = width * i + h
        far = dot_t(moments_ref[h], kern_ref[h])
        rows = down_ref[pl.ds(pl.multiple_of(b * half, half), half), :]
        return (far + dot_t(parent_ref[b // FAN], spread_rows(rows, low_d))).astype(BF16)

    def finish(i, sums, starts=None):
        for h in starts or range(0, width, 2):
            columns = pl.ds(pl.multiple_of((width * i + h) * rank, rank2), rank2)
            product = dot(jnp.concatenate(sums[h : h + 2], axis=0), basis_ref[:, columns])
            out_ref[:, columns] = near_ref[:, columns] + pair(low, product[:rhs], product[rhs:])

    def stage(i, sums, this, other):
        done, last = jnp.maximum(i - 2, 0), sums
        before, after, later = jnp.maximum(i - 1, 0), jnp.minimum(i + 1, rounds - 1), jnp.minimum(i + 2, rounds - 1)
        sums = []
        for h in range(width):
            evaluate(h, this[0], this[1], this[3])
            sums.append(apply(before, h, other[2], other[3]))
            if h % 2 == 0:
                finish(done, last, (h,))
            collect_sources(later, h, this[0], this[1])
            collect_moments(after, h, other[2])
        return tuple(sums)

    even, odd = buffers[:4], buffers[4:]
    for h in range(width):
        collect_sources(0, h, *even[:2])
        collect_sources(1, h, *odd[:2])
        collect_moments(0, h, even[2])
    odd[2][...] = jnp.zeros_like(odd[2])
    odd[3][...] = jnp.zeros_like(odd[3])

    def step(t, sums):
        return stage(2 * t + 1, stage(2 * t, sums, even, odd), odd, even)

    sums = lax.fori_loop(0, rounds // 2, step, (jnp.zeros((rhs, rank), BF16),) * width)
    finish(rounds - 2, sums)
    finish(rounds - 1, tuple(apply(rounds - 1, h, odd[2], odd[3]) for h in range(width)))
    total, halo = out_ref.shape[1], edge_ref.shape[1] // 2
    out_ref[:, :halo] += edge_ref[:, :halo]
    out_ref[:, total - halo :] += edge_ref[:, halo:]


VMEM = functools.partial(pl.BlockSpec, memory_space=pltpu.VMEM)
SMEM = functools.partial(pl.BlockSpec, memory_space=pltpu.SMEM)
ANY = functools.partial(pl.BlockSpec, memory_space=pl.ANY)
PARAMS = pltpu.CompilerParams()


def hbm(shape, dtype):
    return jax.ShapeDtypeStruct(shape, dtype)


def vmem(*arrays):
    return [pltpu.with_memory_space_constraint(a, pltpu.VMEM) if a.size <= 1 << 19 else a for a in arrays]


def on_device(
    charges, points, basis, up_leaf, up_branch, up_device, down_leaf, down_branch, down_device,
    proxy_leaf, proxy_branch, proxy_device, proxy_group, far_leaf, send_leaf, far_branch, near_leaf,
):
    rhs, total = charges.shape
    rank = basis.shape[0]
    leaves = up_leaf.shape[2]
    size = total // leaves
    branches = leaves // FAN
    slots = send_leaf.shape[0]
    groups = lax.axis_size("grp")
    members = lax.axis_size("dev")
    devices = groups * members
    rank2 = 2 * rank
    half = rank // 2
    halo = REACH * size
    assert rank == size and slots == 4 and branches % 2 == 0 and members % 2 == 0

    moments, own, listed, inner, outer, shared = pl.pallas_call(
        upward_kernel,
        out_shape=(
            pltpu.VMEM((leaves, rhs, rank2), BF16),
            hbm((leaves, ROWS, rank2), BF16),
            hbm((devices, slots // 2 * rhs + ROWS + rhs // 2, rank2), BF16),
            pltpu.VMEM((halo // rank2 * (rhs + ROWS), rank2), BF16),
            pltpu.VMEM((halo // rank2 * (rhs + ROWS), rank2), BF16),
            hbm(((branches // 2 + 1) * (rhs + ROWS), rank2), BF16),
        ),
        in_specs=[SMEM()] + [VMEM()] * 4 + [ANY()] + [VMEM()] * 5,
        out_specs=(VMEM(),) * 6,
        scratch_shapes=[
            pltpu.VMEM((leaves * ROWS, rank2), F32),
            pltpu.VMEM((leaves * ROWS, rank2), F32),
            pltpu.VMEM(up_leaf.shape, BF16),
            pltpu.VMEM((leaves * half, rank2), F32),
            pltpu.VMEM((rank * branches, rank2), F32),
            pltpu.SemaphoreType.DMA(()),
        ],
        compiler_params=PARAMS,
        name="upward",
    )(
        send_leaf,
        charges,
        points,
        basis,
        proxy_leaf,
        up_leaf,
        jnp.transpose(up_branch, (0, 2, 1)),
        up_device[:, :, 0],
        jnp.transpose(proxy_branch, (0, 2, 1)),
        proxy_device[:, :, 0],
        proxy_group[:, :, 0],
    )
    (moments,) = vmem(moments)
    received = lax.all_to_all(listed, ("grp", "dev"), split_axis=0, concat_axis=0, tiled=True)

    partner = lax.ppermute(shared, "dev", [(i, i ^ members // 2) for i in range(members)])
    down, far_turned = pl.pallas_call(
        turn_kernel,
        out_shape=(hbm((leaves * half, rank2), BF16), hbm(far_leaf.shape[::-1], jnp.int32)),
        in_specs=[VMEM(), VMEM(), ANY()],
        out_specs=(VMEM(), VMEM()),
        scratch_shapes=[pltpu.VMEM((leaves * half, rank2), F32)],
        compiler_params=PARAMS,
        name="turn",
    )(down_leaf, far_leaf, shared)
    partner, down = lax.optimization_barrier((partner, down))
    both = jnp.concatenate([shared, partner], axis=0)
    parts = [both]
    for s in range(1, members // 2):
        parts.append(lax.ppermute(both, "dev", [(i, i ^ s) for i in range(members)]))

    reach = (2 * REACH + 2) * size
    near, edge_weights = pl.pallas_call(
        near_kernel,
        out_shape=(pltpu.VMEM((rhs, total), F32), hbm((2, 2 * REACH, reach), F32)),
        in_specs=[VMEM()] * 4,
        out_specs=(VMEM(), VMEM()),
        scratch_shapes=[
            pltpu.VMEM((2 * ROWS, total), BF16),
            pltpu.VMEM((2 * ROWS, total), BF16),
            pltpu.VMEM((2, leaves, reach), F32),
            pltpu.VMEM((PAIRS, 2 * size, reach), BF16),
            pltpu.VMEM((PAIRS, 2 * size, reach), BF16),
        ],
        compiler_params=PARAMS,
        name="near",
    )(near_leaf, charges, points, *vmem(both))

    swaps = [(i, i + 1 if i % 2 else i - 1) for i in range(1, devices - 1)]
    inner, outer, near = lax.optimization_barrier((inner, outer, near))
    outer = lax.ppermute(outer, ("grp", "dev"), swaps)
    inner = lax.ppermute(inner, "dev", [(i, i ^ 1) for i in range(members)])

    parts = vmem(*parts)
    assert members & (members - 1) == 0
    far_b, part_d = pl.pallas_call(
        functools.partial(group_kernel, members=members),
        out_shape=(hbm((branches, rhs, rank), F32), hbm((rhs, rank), F32)),
        in_specs=[SMEM()] + [VMEM()] * len(parts),
        out_specs=(VMEM(),) * 2,
        scratch_shapes=[
            pltpu.VMEM((members * branches, rhs, rank2), BF16),
            pltpu.VMEM((members * branches, ROWS, rank2), BF16),
            pltpu.VMEM((members, rhs, rank2), BF16),
            pltpu.VMEM((members, ROWS, rank2), BF16),
        ],
        compiler_params=PARAMS,
        name="group",
    )(jnp.transpose(far_branch), *parts)

    table = leaves + devices * slots
    return pl.pallas_call(
        functools.partial(downward_kernel, groups=groups),
        out_shape=hbm((rhs, total), F32),
        in_specs=[SMEM()] + [VMEM()] * 11 + [ANY(), ANY(), VMEM(), VMEM()],
        out_specs=VMEM(),
        scratch_shapes=[
            pltpu.VMEM((rhs, 2 * halo), F32),
            pltpu.VMEM((2, rhs, 2 * halo), BF16),
            pltpu.VMEM((2, 3, 2 * halo), BF16),
            pltpu.VMEM((REACH, 2 * size, reach), BF16),
            pltpu.SemaphoreType.DMA((6,)),
            pltpu.VMEM((table, rhs + ROWS, rank2), BF16),
            pltpu.VMEM((groups, rhs, rank2), BF16),
            pltpu.VMEM((groups, ROWS, rank2), BF16),
            pltpu.VMEM((rank * branches, rank2), F32),
            pltpu.VMEM((branches, rhs, rank2), BF16),
        ]
        + [
            pltpu.VMEM((ROUND, rank, 2 * ROWS), BF16),
            pltpu.VMEM((ROUND, ROWS, far_leaf.shape[0] * rank), BF16),
            pltpu.VMEM((ROUND, rhs, far_leaf.shape[0] * rank), BF16),
            pltpu.VMEM((ROUND, rank, far_leaf.shape[0] * rank), BF16),
        ]
        * 2,
        compiler_params=PARAMS,
        name="downward",
    )(
        far_turned,
        far_b,
        part_d,
        down_device[:, :, 0],
        jnp.transpose(down_branch, (0, 2, 1)),
        down,
        own,
        moments,
        *vmem(received),
        basis,
        *vmem(near),
        edge_weights,
        charges,
        points,
        *vmem(inner, outer),
    )


def solution(mesh):
    points = P(None, ("grp", "dev"))
    blocks = P(None, None, ("grp", "dev"))
    placed = (points,) * 3 + (blocks,) * 9 + (P(None, None, "grp"),) + (points,) * 4

    return jax.shard_map(on_device, mesh=mesh, in_specs=placed, out_specs=points, check_vma=False)
```
